32 devices in a mesh: sec: 4 (over y, core), dev: 8 (over z, x).
Axes of the slice: x: 2, y: 2, z: 4, core: 2. Of those that a mesh axis runs over, the one named last changes fastest.
Arguments:
- potential: float32 [64, 32, 512], P('dev', None, 'sec'), may hold values from -6 to 6
- previous: float32 [64, 32, 512], P('dev', None, 'sec'), may hold values from -6 to 6
- wave_coeff: float32 [64, 32, 512], P('dev', None, 'sec'), may hold values from 0.03 to 0.16
- sketch_in: bfloat16 [16384, 512], P('dev'), may hold values from -6 to 6
- omega: float32 [64, 512], replicated, may hold values from -6 to 6
- blocks: int32 [8, 9], P('dev'), may hold values from 0 to 255, as said below
- owners: int32 [8, 9], P('dev'), may hold values from 0 to 7, as said below
Outputs:
- basis: bfloat16 [4, 16384, 512], P('sec', 'dev')
- gram_factor: float32 [4, 512, 512], P('sec')
The draws below stay inside these ranges and needn't reach their ends.
Inputs may be any that keep to these rules, and one draw needn't show every extreme that they name: `blocks`: within one section's 3 entries of a row the block numbers are distinct. Within a row of owners no owner appears more than 2 times, and one owner, the same for all rows, appears exactly 2 times in every row.
All inputs are finite; a program needn't handle non-finite values.
Results may differ from the reference program's by a relative error of at most 0.003.
Values sent between devices are 32-bit elements; how exact they have to be, the bound alone decides.
No kernel may reach another device: no remote copies, remote signals or barrier semaphores. Data moves between devices by JAX's collectives and lax.ppermute only.
A program may use at most 256 MiB of HBM per device.

```python
import math
import jax
import jax.numpy as jnp
from jax import lax

CX = 8
CY = 32
CZ = 128
CAP = 2
SEL = 3
STEPS = 16
MB = 4
RANK = 512
NX = 64
NZ = 512
SNAPS = 64
SKETCH_ROWS = 16384
N_SEC = 4
N_DEV = 8


def draw_owners(key, part):
    list_width = (N_SEC - 1) * SEL
    tickets = N_DEV * CAP
    key_rank, key_jitter, key_order = jax.random.split(jax.random.fold_in(key, 11), 3)
    ranking = jax.random.permutation(key_rank, N_DEV)
    owner_of = jnp.arange(tickets, dtype=jnp.int32) // CAP
    standing = ranking[owner_of]
    priority = jnp.where(standing == 0, 1048576, (N_DEV - standing) * 8192 // N_DEV)
    jitter = jax.random.randint(key_jitter, (N_DEV, tickets), 0, 4096)
    scores = (priority[None, :] + jitter) * tickets + jnp.arange(tickets, dtype=jnp.int32)[None, :]
    picked = lax.top_k(scores, list_width)[1]
    chosen = picked // CAP
    mixing = jax.random.randint(key_order, (N_DEV, list_width), 0, 65536) * list_width + jnp.arange(list_width, dtype=jnp.int32)[None, :]
    ordering = jnp.argsort(mixing, axis=1)
    return jnp.take_along_axis(chosen, ordering, axis=1).astype(jnp.int32)


def draw_blocks(key, part):
    cell_count = CX * CY
    groups = N_DEV * (N_SEC - 1)
    group_keys = jax.random.split(jax.random.fold_in(key, 23), groups)
    selected = jax.vmap(lambda group_key: jax.random.permutation(group_key, cell_count)[:SEL])(group_keys)
    leading = (selected[0] - selected[0, 0] + cell_count - 1) % cell_count
    second = (selected[1] - selected[1, 0]) % cell_count
    selected = selected.at[0].set(leading).at[1].set(second)
    return selected.reshape(N_DEV, (N_SEC - 1) * SEL).astype(jnp.int32)


def level_of(stream_key, dims, cuts, smallest, top_value):
    level = 1.0
    for axis_at, blocks in cuts:
        steps = jax.random.uniform(jax.random.fold_in(jax.random.fold_in(stream_key, 6), axis_at), (blocks,), jnp.float32, smallest / len(cuts), top_value / len(cuts))
        level = level * jnp.repeat(jnp.exp(steps), dims[axis_at] // blocks).reshape((-1,) + (1,) * (len(dims) - 1 - axis_at))
    return level


def scatter_about(key, dims, deviation, limit, cuts=(), held_as=jnp.bfloat16):
    result = jax.random.normal(key, dims, jnp.float32) * deviation
    if len(cuts) > 0:
        result = level_of(key, dims, cuts, -0.22, 0.18) * result
    return jnp.clip(result, min=-limit, max=limit).astype(held_as)


def setup_inputs(seed: int = 0) -> dict:
    arg_keys = jax.random.split(jax.random.key(seed), 8)
    return {
        "potential": scatter_about(arg_keys[0], (NX, CY, NZ), 1.0, 6.0, ((0, 8), (2, 4)), jnp.float32),
        "previous": scatter_about(arg_keys[1], (NX, CY, NZ), 1.0, 6.0, ((0, 8), (2, 4)), jnp.float32),
        "wave_coeff": jnp.clip(jnp.exp(math.log(0.16) - 1.6739764 * jax.random.uniform(arg_keys[2], (NX, CY, NZ), jnp.float32) ** level_of(arg_keys[2], (NX, CY, NZ), ((0, 8), (2, 4)), -0.2, 0.2)), 0.03, 0.16),
        "sketch_in": scatter_about(arg_keys[3], (SKETCH_ROWS, RANK), 1.0, 6.0, ((0, 8),)),
        "omega": scatter_about(arg_keys[4], (SNAPS, RANK), 1.0, 6.0, (), jnp.float32),
        "blocks": draw_blocks(jax.random.fold_in(arg_keys[7], 71), 0),
        "owners": draw_owners(jax.random.fold_in(arg_keys[7], 71), 0),
    }


damping = 0.05

def step_field(current, earlier, stiffness):
    padded = jnp.pad(current, 1)
    neighbours = padded[2:, 1:-1, 1:-1] + padded[:-2, 1:-1, 1:-1]
    neighbours = neighbours + padded[1:-1, 2:, 1:-1] + padded[1:-1, :-2, 1:-1]
    neighbours = neighbours + padded[1:-1, 1:-1, 2:] + padded[1:-1, 1:-1, :-2]
    neighbours = neighbours - 6.0 * current
    return 2.0 * current - earlier + stiffness * neighbours - damping * (current - earlier)

def reference(potential, previous, wave_coeff, sketch_in, omega, blocks, owners):
    sim_sections = N_SEC - 1
    sim_depth = sim_sections * CZ
    current = potential[:, :, :sim_depth]
    earlier = previous[:, :, :sim_depth]
    stiffness = wave_coeff[:, :, :sim_depth]
    list_width = sim_sections * SEL
    column = jnp.arange(N_DEV, dtype=jnp.int32)[:, None]
    section = (jnp.arange(list_width, dtype=jnp.int32) // SEL)[None, :]
    first_index = (column * CX + blocks // CY).reshape(-1).astype(jnp.int32)
    second_index = (blocks % CY).reshape(-1).astype(jnp.int32)
    depth_start = jnp.broadcast_to(section * CZ, blocks.shape).reshape(-1).astype(jnp.int32)
    position = jnp.arange(list_width, dtype=jnp.int32)
    matches = owners[:, :, None] == owners[:, None, :]
    before = position[:, None] < position[None, :]
    counts = lax.optimization_barrier(jnp.sum((matches & before[None]).astype(jnp.int32), axis=1))
    slot_index = (owners * (N_DEV * CAP) + column * CAP + counts).reshape(-1).astype(jnp.int32)
    cell_offsets = jnp.arange(CZ, dtype=jnp.int32)
    sketch = sketch_in.astype(jnp.float32).reshape(N_DEV * N_DEV * CAP, CZ, RANK)

    def advance(state_pair, unused):
        current, earlier = state_pair
        newest = step_field(current, earlier, stiffness)
        snapshot = newest[first_index[:, None], second_index[:, None], depth_start[:, None] + cell_offsets[None, :]]
        return ((newest, current), snapshot)
    for batch_index in range(MB):
        (current, earlier), snapshots = lax.scan(advance, (current, earlier), None, length=STEPS)
        weights = omega[batch_index * STEPS:(batch_index + 1) * STEPS]
        contribution = jnp.einsum('tbz,tk->bzk', snapshots, weights, precision=lax.Precision.HIGHEST)
        sketch = sketch.at[slot_index].add(contribution)
    sketch_rows = sketch.reshape(-1, RANK)
    gram_matrix = jnp.dot(sketch_rows.T, sketch_rows, precision=lax.Precision.HIGHEST)
    lower_factor = jnp.linalg.cholesky(gram_matrix)
    row_scale = math.sqrt(sketch_rows.shape[0])
    basis_rows = jax.scipy.linalg.solve_triangular(lower_factor, sketch_rows.T, lower=True).T * row_scale
    basis_out = jnp.concatenate([jnp.zeros((N_SEC - 1, sketch_rows.shape[0], RANK), jnp.bfloat16), basis_rows.astype(jnp.bfloat16)[None]], axis=0)
    factor = jnp.concatenate([jnp.zeros((N_SEC - 1, RANK, RANK), jnp.float32), (lower_factor.T / row_scale)[None]], axis=0)
    return (basis_out, factor)
```

```python
import functools
import math

import jax
import jax.numpy as jnp
import numpy as np
from jax import lax
from jax.experimental import pallas as pl
from jax.experimental.pallas import tpu as pltpu
from jax.sharding import PartitionSpec as P

CAP = 2
damping = 0.05
LANES = 128
highest = lax.Precision.HIGHEST
decay = math.sqrt(1.0 - damping)
BOTH = ("sec", "dev")


def neighbour_path(columns):
    order = []
    for i in range(0, columns, 2):
        pair = [i, i + 1]
        order += pair if (i // 2) % 2 == 0 else pair[::-1]
    return order


def vmem(*arrays):
    return [pl.BlockSpec(memory_space=pltpu.VMEM)] * len(arrays)


def big(limit=48):
    return pltpu.CompilerParams(vmem_limit_bytes=limit << 20)


def slab_of(order, column, section, per_slab):
    place = order.index(column)
    forward, backward = place // per_slab, (len(order) - 1 - place) // per_slab
    return jnp.where(section % 2 == 0, forward, backward)


def split_kernel(order, slab, per_slab, u_ref, e_ref, k_ref, table_ref, out_ref, turned):
    section = lax.axis_index("sec")
    extent_x, extent_y, depth = u_ref.shape
    for a, ref in enumerate((u_ref, e_ref, k_ref)):
        for p in range(2):
            rows = jnp.concatenate([ref[x] for x in range(p, extent_x, 2)], axis=0)
            if a == 1:
                rows = rows * decay
            turned[2 * a + p] = rows.T
    for column in range(len(order)):
        at = slab_of(order, column, section, per_slab)
        start = pl.multiple_of(at * slab, 8)
        for q in range(6):
            out_ref[column, q * slab : (q + 1) * slab, :] = turned[q, pl.ds(start, slab), :]
        out_ref[column, 6 * slab :, :] = jnp.broadcast_to(table_ref[...], (8, LANES))


def steps_kernel(
    first_step, slab, per_device, last, snaps, sections,
    table, kl, kc, kr, sl, sc, sr, w_in, *rest,
):
    if last:
        send_ref, w_ref, field_a, field_b, gain, own = rest
    else:
        state_ref, w_ref, field_a, field_b, gain, own = rest
    section = jnp.minimum(lax.axis_index("sec"), sections - 2)
    list_start = section * per_device
    columns = kc.shape[0]
    rows = 3 * slab
    lane = lax.broadcasted_iota(jnp.int32, (8, LANES), 1)
    y_first, y_last = lane % 32 == 0, lane % 32 == 31
    zero = jnp.zeros((8, LANES), jnp.float32)

    for o in range(2 * columns):
        d, p = o // 2, o % 2
        for field, at in ((field_a, p), (field_b, 2 + p)):
            field[o, 0:8, :] = zero
            field[o, 8 + rows : 16 + rows, :] = zero
            for h, ref in enumerate((sl, sc, sr)):
                field[o, 8 + h * slab : 8 + (h + 1) * slab, :] = ref[
                    d, at * slab : (at + 1) * slab, :
                ]
        for h, ref in enumerate((kl, kc, kr)):
            k = ref[d, (4 + p) * slab : (5 + p) * slab, :]
            gain[o, h * slab : (h + 1) * slab, :] = k * (1.0 / decay)
            own[o, h * slab : (h + 1) * slab, :] = ((2.0 - damping) - 6.0 * k) * (1.0 / decay)
    w_ref[...] = w_in[...]

    def step(src, dst, tiles, number):
        for z in tiles:
            at = slice(8 + 8 * z, 16 + 8 * z)
            low = slice(7 + 8 * z, 15 + 8 * z)
            high = slice(9 + 8 * z, 17 + 8 * z)
            here = slice(8 * z, 8 * z + 8)
            values = [src[o, at, :] for o in range(2 * columns)]
            up = [pltpu.roll(values[2 * d + 1], 32, 1) for d in range(columns)]
            down = [pltpu.roll(values[2 * d], LANES - 32, 1) for d in range(columns)]
            for o in range(2 * columns):
                d, p = o // 2, o % 2
                v = values[o]
                if p == 0:
                    side = jnp.where(lane < 32, up[d - 1] if d > 0 else zero, up[d])
                    total = values[o + 1] + side
                else:
                    side = jnp.where(
                        lane >= LANES - 32, down[d + 1] if d + 1 < columns else zero, down[d]
                    )
                    total = values[o - 1] + side
                total = total + (src[o, low, :] + src[o, high, :])
                total = total + jnp.where(y_first, 0.0, pltpu.roll(v, 1, 1))
                total = total + jnp.where(y_last, 0.0, pltpu.roll(v, LANES - 1, 1))
                dst[o, at, :] = own[o, here, :] * v + gain[o, here, :] * total - dst[o, at, :]

        def column_blocks(d, carry):
            for i in range(per_device):
                block = table[d, list_start + i]
                x, y = block >> 5, block & 31
                at_lane = ((x >> 1) << 5) + y
                o = 2 * d + (x & 1)
                j = d * per_device + i
                held = w_ref[j]
                for h in range(slab // 8):
                    target = h * snaps + number
                    value = dst[o, 8 + slab + 8 * h : 16 + slab + 8 * h, :]
                    moved = pltpu.roll(value, (target - at_lane) & (LANES - 1), 1)
                    held = jnp.where(lane == target, moved, held)
                w_ref[j] = held
            return carry

        lax.fori_loop(0, columns, column_blocks, 0, unroll=min(columns, 8))

    for phase in range(slab // 8):
        tiles = range(phase, 3 * slab // 8 - phase)

        def pair(m, carry):
            number = first_step + 8 * phase + 2 * m
            step(field_a, field_b, tiles, number)
            step(field_b, field_a, tiles, number + 1)
            return carry

        lax.fori_loop(0, 4, pair, 0)

    if last:
        send_ref[...] = jnp.zeros(send_ref.shape, jnp.float32)
        width = per_device * (sections - 1)

        def place(d, carry):
            for i in range(per_device):
                mine = table[d, width + list_start + i]

                def earlier(n, c):
                    return c + jnp.where(table[d, width + n] == mine, 1, 0)

                count = lax.fori_loop(0, list_start + i, earlier, 0)
                send_ref[mine, d * CAP + count] = w_ref[d * per_device + i]
            return carry

        lax.fori_loop(0, columns, place, 0)
    else:
        for o in range(2 * columns):
            d, p = o // 2, o % 2
            state_ref[d, p * slab : (p + 1) * slab, :] = field_a[o, 8 + slab : 8 + 2 * slab, :]
            state_ref[d, (2 + p) * slab : (3 + p) * slab, :] = field_b[
                o, 8 + slab : 8 + 2 * slab, :
            ]


def unpack(tile, h, snaps, lane):
    if h:
        tile = pltpu.roll(tile, LANES - h * snaps, 1)
    return jnp.where(lane < snaps, tile, 0.0)


def product_kernel(
    order, slab, per_slab, snaps, sections, w_ref, s_ref, out_ref, sorted_ref, wide, low
):
    section = lax.axis_index("sec")
    slots = w_ref.shape[1]
    halves = slab // 8
    lane = lax.broadcasted_iota(jnp.int32, (8, LANES), 1)
    for column in range(0, len(order)):
        if order.index(column) % per_slab:
            continue
        at = slab_of(order, column, section, per_slab)
        for q in range(slots):
            tile = w_ref[column, q]
            sorted_ref[at, q] = tile
            for h in range(halves):
                w = unpack(tile, h, snaps, lane)
                w1 = w.astype(jnp.bfloat16).astype(jnp.float32)
                w2 = (w - w1).astype(jnp.bfloat16).astype(jnp.float32)
                w3 = w - w1 - w2
                start = pl.multiple_of(q * LANES + at * slab + 8 * h, 8)
                wide[pl.ds(start, 8), :] = w1 + pltpu.roll(w2, snaps, 1)
                low[pl.ds(start, 8), :] = w3
    both = wide[...].astype(jnp.bfloat16)
    tail = low[...].astype(jnp.bfloat16)
    rows = (((0,), (0,)), ((), ()))
    dot = functools.partial(
        lax.dot_general, dimension_numbers=rows, preferred_element_type=jnp.float32
    )
    sketch = s_ref[...]
    a_first = dot(both, sketch)
    a_tail = dot(tail, sketch)
    cross = a_first[:snaps] + (a_first[snaps:] + a_tail[:snaps])
    c_first = dot(both, both)
    c_tail = dot(tail, both)[:snaps, :]
    c_tail = jnp.where(lax.broadcasted_iota(jnp.int32, c_tail.shape, 1) < snaps, c_tail, 0.0)
    half = c_first[:snaps, :] + c_first[snaps:, :]
    own = half + pltpu.roll(half, snaps, 1)
    square = jnp.concatenate([c_tail, jnp.zeros_like(c_tail)], axis=0).T[:snaps, :]
    inner = jnp.where(
        lax.broadcasted_iota(jnp.int32, own.shape, 1) < snaps, own, 0.0
    ) + (c_tail + square)
    keep = jnp.where(section == sections - 1, 0.0, 1.0)
    out_ref[...] = jnp.zeros(out_ref.shape, jnp.float32)
    strips = cross.shape[1] // LANES
    for r in range(snaps // 8):
        for c in range(strips):
            out_ref[r * strips + c, 0] = (
                cross[8 * r : 8 * r + 8, c * LANES : (c + 1) * LANES] * keep
            )
        out_ref[r * strips, 1] = inner[8 * r : 8 * r + 8, :] * keep


def gather_kernel(parts_ref, out_ref):
    total = jnp.sum(parts_ref[...], axis=0)
    for i in range(out_ref.shape[0]):
        out_ref[i] = total


def factor_kernel(scale, sections, parts_ref, omega_ref, s_ref, factor_ref, inverse_ref, g):
    rank = s_ref.shape[0]
    snaps = omega_ref.shape[0]
    strips = rank // LANES
    analysis = lax.axis_index("sec") == sections - 1
    rows_first = (((0,), (0,)), ((), ()))
    cross = jnp.concatenate(
        [
            jnp.concatenate([parts_ref[r * strips + c, 0] for c in range(strips)], axis=1)
            for r in range(snaps // 8)
        ],
        axis=0,
    )
    inner = jnp.concatenate([parts_ref[r * strips, 1] for r in range(snaps // 8)], axis=0)
    omega = omega_ref[...]
    half = cross + 0.5 * jnp.dot(
        inner[:, :snaps], omega, precision=highest, preferred_element_type=jnp.float32
    )
    left = jnp.concatenate([half, omega], axis=0)
    right = jnp.concatenate([omega, half], axis=0)
    g[...] = s_ref[...] + lax.dot_general(
        left, right, rows_first, precision=highest, preferred_element_type=jnp.float32
    )
    row_number = lax.broadcasted_iota(jnp.int32, (rank, rank), 0)
    lane_number = lax.broadcasted_iota(jnp.int32, (rank, rank), 1)
    inverse_ref[...] = jnp.where(row_number == lane_number, 1.0, 0.0)
    sub = lax.broadcasted_iota(jnp.int32, (8, LANES), 0)
    lane = lax.broadcasted_iota(jnp.int32, (8, LANES), 1)
    tiles = LANES // 8

    def block(k, carry):
        start = pl.multiple_of(k * LANES, LANES)
        d = [g[pl.ds(start + 8 * i, 8), pl.ds(start, LANES)] for i in range(tiles)]
        e = [jnp.where(lane == sub + 8 * i, 1.0, 0.0) for i in range(tiles)]
        for j in range(LANES):
            p, r = j // 8, j % 8
            row_d = jnp.broadcast_to(d[p][r : r + 1, :], (8, LANES))
            row_e = jnp.broadcast_to(e[p][r : r + 1, :], (8, LANES))
            inv = 1.0 / jnp.broadcast_to(row_d[:, j : j + 1], (8, LANES))
            row_d = row_d * inv
            row_e = row_e * inv
            for i in range(p, tiles):
                if i == p and r == 7:
                    continue
                col = jnp.broadcast_to(d[i][:, j : j + 1], (8, LANES))
                if i == p:
                    col = jnp.where(sub > r, col, 0.0)
                d[i] = d[i] - col * row_d
                e[i] = e[i] - col * row_e
        own_rows, own_inverse = [], []
        for i in range(tiles):
            diag = lane == sub + 8 * i
            root = lax.rsqrt(jnp.sum(jnp.where(diag, d[i], 0.0), axis=1, keepdims=True))
            own_rows.append(jnp.where(lane >= sub + 8 * i, d[i] * root, 0.0))
            own_inverse.append(e[i] * root)
        upper = jnp.concatenate(own_rows, axis=0)
        small = jnp.concatenate(own_inverse, axis=0)
        panel = jnp.dot(
            small,
            jnp.concatenate([g[pl.ds(start, LANES), :], inverse_ref[pl.ds(start, LANES), :]], 1),
            precision=highest,
            preferred_element_type=jnp.float32,
        )
        lanes_all = lax.broadcasted_iota(jnp.int32, (LANES, rank), 1)
        after = lanes_all >= start + LANES
        fresh = jnp.where(after, panel[:, :rank], 0.0)
        below = panel[:, rank:]
        inverse_ref[pl.ds(start, LANES), :] = below
        change = lax.dot_general(
            fresh,
            jnp.concatenate([fresh, below], axis=1),
            rows_first,
            precision=highest,
            preferred_element_type=jnp.float32,
        )
        factor_ref[pl.ds(start, LANES), :] = fresh
        factor_ref[pl.ds(start, LANES), pl.ds(start, LANES)] = upper
        g[...] = g[...] - change[:, :rank]
        inverse_ref[...] = inverse_ref[...] - change[:, rank:]
        return carry

    lax.fori_loop(0, strips, block, 0)
    factor_ref[...] = jnp.where(analysis, factor_ref[...] * (1.0 / scale), 0.0)
    inverse_ref[...] = inverse_ref[...] * scale


def basis_kernel(
    slab, snaps, sections, inverse_ref, omega_ref, s_ref, w0, w1, w2, out_ref, wide
):
    analysis = lax.axis_index("sec") == sections - 1

    @pl.when(analysis)
    def _():
        lane = lax.broadcasted_iota(jnp.int32, (8, LANES), 1)
        slabs, slots = w0.shape[:2]

        def fill(q, carry):
            for a in range(slabs):
                tile = w0[a, q] + w1[a, q] + w2[a, q]
                for h in range(slab // 8):
                    start = pl.multiple_of(q * LANES + a * slab + 8 * h, 8)
                    wide[pl.ds(start, 8), :] = unpack(tile, h, snaps, lane)
            return carry

        lax.fori_loop(0, slots, fill, 0)
        inverse = inverse_ref[...]
        columns = (((1,), (1,)), ((), ()))
        mixed = lax.dot_general(
            omega_ref[...], inverse, columns, precision=highest, preferred_element_type=jnp.float32
        )
        mixed = jnp.concatenate([mixed, jnp.zeros_like(mixed)], axis=0)
        x1 = inverse.astype(jnp.bfloat16)
        rest = inverse - x1.astype(jnp.float32)
        x2 = rest.astype(jnp.bfloat16)
        rows = 256

        def strip(i, carry):
            at = pl.ds(pl.multiple_of(i * rows, rows), rows)
            s = s_ref[at, :]
            dot = functools.partial(
                lax.dot_general, dimension_numbers=columns, preferred_element_type=jnp.float32
            )
            q = dot(s, x1) + dot(s, x2)
            q = q + jnp.dot(
                wide[at, :], mixed, precision=highest, preferred_element_type=jnp.float32
            )
            out_ref[at, :] = q.astype(jnp.bfloat16)
            return carry

        lax.fori_loop(0, s_ref.shape[0] // rows, strip, 0)

    @pl.when(jnp.logical_not(analysis))
    def _():
        out_ref[...] = jnp.zeros(out_ref.shape, jnp.bfloat16)


def shards(potential, previous, wave_coeff, sketch_in, omega, blocks, owners):
    sections = lax.axis_size("sec")
    columns = lax.axis_size("dev")
    devices = sections * columns
    extent_x, extent_y, depth = potential.shape
    list_width = owners.shape[1]
    per_device = list_width // (sections - 1)
    snaps, rank = omega.shape
    slab = max(8, depth // columns)
    per_slab = slab * columns // depth
    slabs = depth // slab
    slots = columns * CAP
    order = neighbour_path(columns)
    path = []
    for section in range(sections - 1):
        path += [section * columns + d for d in (order if section % 2 == 0 else order[::-1])]
    up = [(path[i], path[i + per_slab]) for i in range(len(path) - per_slab)]
    down = [(b, a) for a, b in up]
    f32 = jnp.float32

    gram = lax.psum(
        lax.dot_general(
            sketch_in, sketch_in, (((0,), (0,)), ((), ())), preferred_element_type=f32
        ),
        "dev",
    )
    scaled = omega * jnp.asarray(
        decay ** np.arange(1, snaps + 1, dtype=np.float64), f32
    )[:, None]

    lists = jnp.pad(
        jnp.concatenate([blocks, owners], axis=1).astype(f32), ((0, 0), (0, LANES - 2 * list_width))
    )
    chunk = 6 * slab + 8
    operands = (potential, previous, wave_coeff, lists)
    outgoing = pl.pallas_call(
        functools.partial(split_kernel, order, slab, per_slab),
        out_shape=jax.ShapeDtypeStruct((columns, chunk, LANES), f32),
        in_specs=vmem(*operands),
        out_specs=pl.BlockSpec(memory_space=pltpu.VMEM),
        scratch_shapes=[pltpu.VMEM((6, depth, LANES), f32)],
        compiler_params=big(),
    )(*operands)
    raw = lax.all_to_all(outgoing, "dev", split_axis=0, concat_axis=0, tiled=True)
    table = raw[:, 6 * slab, : 2 * list_width].astype(jnp.int32)

    def sides(x):
        return lax.ppermute(x, BOTH, up), x, lax.ppermute(x, BOTH, down)

    fields = sides(raw)
    state = fields
    held = jnp.zeros((columns * per_device, 8, LANES), f32)
    rounds = snaps // slab
    for number in range(rounds):
        last = number == rounds - 1
        operands = (table, *fields, *state, held)
        result = (columns, slots, 8, LANES) if last else (columns, 4 * slab, LANES)
        moved, held = pl.pallas_call(
            functools.partial(
                steps_kernel, number * slab, slab, per_device, last, snaps, sections
            ),
            out_shape=(
                jax.ShapeDtypeStruct(result, f32),
                jax.ShapeDtypeStruct(held.shape, f32),
            ),
            in_specs=[pl.BlockSpec(memory_space=pltpu.SMEM)] + vmem(*operands[1:]),
            out_specs=tuple(vmem(0, 0)),
            scratch_shapes=[pltpu.VMEM((2 * columns, 3 * slab + 16, LANES), f32)] * 2
            + [pltpu.VMEM((2 * columns, 3 * slab, LANES), f32)] * 2,
            compiler_params=big(),
        )(*operands)
        if not last:
            state = sides(moved)
    arrived = lax.all_to_all(moved, "dev", split_axis=0, concat_axis=0, tiled=True)

    operands = (arrived, sketch_in)
    parts, ordered = pl.pallas_call(
        functools.partial(product_kernel, order, slab, per_slab, snaps, sections),
        out_shape=(
            jax.ShapeDtypeStruct((devices, 2, 8, LANES), f32),
            jax.ShapeDtypeStruct((slabs, slots, 8, LANES), f32),
        ),
        in_specs=vmem(*operands),
        out_specs=tuple(vmem(0, 0)),
        scratch_shapes=[pltpu.VMEM((slots * depth, LANES), f32)] * 2,
        compiler_params=big(60),
    )(*operands)
    terms = lax.all_to_all(parts, BOTH, split_axis=0, concat_axis=0, tiled=True)
    copies = pl.pallas_call(
        gather_kernel,
        out_shape=jax.ShapeDtypeStruct(terms.shape, f32),
        in_specs=vmem(0),
        out_specs=pl.BlockSpec(memory_space=pltpu.VMEM),
    )(terms)
    sums = lax.all_to_all(copies, BOTH, split_axis=0, concat_axis=0, tiled=True)
    sums, ordered = lax.optimization_barrier((sums, ordered))
    pieces = [lax.ppermute(ordered, "sec", [(i, sections - 1)]) for i in range(sections - 1)]

    scale = math.sqrt(columns * columns * CAP * depth)
    operands = (sums, scaled, gram)
    factor, inverse = pl.pallas_call(
        functools.partial(factor_kernel, scale, sections),
        out_shape=(jax.ShapeDtypeStruct((rank, rank), f32),) * 2,
        in_specs=vmem(*operands),
        out_specs=tuple(vmem(0, 0)),
        scratch_shapes=[pltpu.VMEM((rank, rank), f32)],
        compiler_params=big(),
    )(*operands)
    operands = (inverse, scaled, sketch_in, *pieces)
    basis = pl.pallas_call(
        functools.partial(basis_kernel, slab, snaps, sections),
        out_shape=jax.ShapeDtypeStruct(sketch_in.shape, jnp.bfloat16),
        in_specs=vmem(*operands),
        out_specs=pl.BlockSpec(memory_space=pltpu.VMEM),
        scratch_shapes=[pltpu.VMEM((slots * depth, LANES), f32)],
        compiler_params=big(60),
    )(*operands)
    return (basis[None], factor[None])


def solution(mesh):
    placed = (
        P("dev", None, "sec"),
        P("dev", None, "sec"),
        P("dev", None, "sec"),
        P("dev", None),
        P(),
        P("dev", None),
        P("dev", None),
    )
    return jax.shard_map(
        shards,
        mesh=mesh,
        in_specs=placed,
        out_specs=(P("sec", "dev", None), P("sec", None, None)),
        check_vma=False,
    )
```

```python
import functools
import math

import jax
import jax.numpy as jnp
import numpy as np
from jax import lax
from jax.experimental import pallas as pl
from jax.experimental.pallas import tpu as pltpu
from jax.sharding import PartitionSpec as P

CAP = 2
damping = 0.05
LANES = 128
highest = lax.Precision.HIGHEST
decay = math.sqrt(1.0 - damping)
BOTH = ("sec", "dev")


def neighbour_path(columns):
    order = []
    for i in range(0, columns, 2):
        pair = [i, i + 1]
        order += pair if (i // 2) % 2 == 0 else pair[::-1]
    return order


def vmem(*arrays):
    return [pl.BlockSpec(memory_space=pltpu.VMEM)] * len(arrays)


def big(limit=48):
    return pltpu.CompilerParams(vmem_limit_bytes=limit << 20)


def slab_of(order, column, section, per_slab):
    place = order.index(column)
    forward, backward = place // per_slab, (len(order) - 1 - place) // per_slab
    return jnp.where(section % 2 == 0, forward, backward)


def split_kernel(order, slab, per_slab, u_ref, e_ref, k_ref, table_ref, out_ref, turned):
    section = lax.axis_index("sec")
    extent_x, extent_y, depth = u_ref.shape
    for a, ref in enumerate((u_ref, e_ref, k_ref)):
        for p in range(2):
            rows = jnp.concatenate([ref[x] for x in range(p, extent_x, 2)], axis=0)
            if a == 1:
                rows = rows * decay
            turned[2 * a + p] = rows.T
    for column in range(len(order)):
        at = slab_of(order, column, section, per_slab)
        start = pl.multiple_of(at * slab, 8)
        for q in range(6):
            out_ref[column, q * slab : (q + 1) * slab, :] = turned[q, pl.ds(start, slab), :]
        out_ref[column, 6 * slab :, :] = jnp.broadcast_to(table_ref[...], (8, LANES))


def steps_kernel(
    first_step, slab, per_device, last, snaps, sections,
    table, kl, kc, kr, sl, sc, sr, w_in, *rest,
):
    if last:
        send_ref, w_ref, field_a, field_b, gain, own = rest
    else:
        state_ref, w_ref, field_a, field_b, gain, own = rest
    section = jnp.minimum(lax.axis_index("sec"), sections - 2)
    list_start = section * per_device
    columns = kc.shape[0]
    rows = 3 * slab
    lane = lax.broadcasted_iota(jnp.int32, (8, LANES), 1)
    y_first, y_last = lane % 32 == 0, lane % 32 == 31
    zero = jnp.zeros((8, LANES), jnp.float32)

    for o in range(2 * columns):
        d, p = o // 2, o % 2
        for field, at in ((field_a, p), (field_b, 2 + p)):
            field[o, 0:8, :] = zero
            field[o, 8 + rows : 16 + rows, :] = zero
            for h, ref in enumerate((sl, sc, sr)):
                field[o, 8 + h * slab : 8 + (h + 1) * slab, :] = ref[
                    d, at * slab : (at + 1) * slab, :
                ]
        for h, ref in enumerate((kl, kc, kr)):
            k = ref[d, (4 + p) * slab : (5 + p) * slab, :]
            gain[o, h * slab : (h + 1) * slab, :] = k * (1.0 / decay)
            own[o, h * slab : (h + 1) * slab, :] = ((2.0 - damping) - 6.0 * k) * (1.0 / decay)
    w_ref[...] = w_in[...]

    def step(src, dst, tiles, number):
        for z in tiles:
            at = slice(8 + 8 * z, 16 + 8 * z)
            low = slice(7 + 8 * z, 15 + 8 * z)
            high = slice(9 + 8 * z, 17 + 8 * z)
            here = slice(8 * z, 8 * z + 8)
            values = [src[o, at, :] for o in range(2 * columns)]
            up = [pltpu.roll(values[2 * d + 1], 32, 1) for d in range(columns)]
            down = [pltpu.roll(values[2 * d], LANES - 32, 1) for d in range(columns)]
            for o in range(2 * columns):
                d, p = o // 2, o % 2
                v = values[o]
                if p == 0:
                    side = jnp.where(lane < 32, up[d - 1] if d > 0 else zero, up[d])
                    total = values[o + 1] + side
                else:
                    side = jnp.where(
                        lane >= LANES - 32, down[d + 1] if d + 1 < columns else zero, down[d]
                    )
                    total = values[o - 1] + side
                total = total + (src[o, low, :] + src[o, high, :])
                total = total + jnp.where(y_first, 0.0, pltpu.roll(v, 1, 1))
                total = total + jnp.where(y_last, 0.0, pltpu.roll(v, LANES - 1, 1))
                dst[o, at, :] = own[o, here, :] * v + gain[o, here, :] * total - dst[o, at, :]

        def column_blocks(d, carry):
            for i in range(per_device):
                block = table[d, list_start + i]
                x, y = block >> 5, block & 31
                at_lane = ((x >> 1) << 5) + y
                o = 2 * d + (x & 1)
                j = d * per_device + i
                held = w_ref[j]
                for h in range(slab // 8):
                    target = h * snaps + number
                    value = dst[o, 8 + slab + 8 * h : 16 + slab + 8 * h, :]
                    moved = pltpu.roll(value, (target - at_lane) & (LANES - 1), 1)
                    held = jnp.where(lane == target, moved, held)
                w_ref[j] = held
            return carry

        lax.fori_loop(0, columns, column_blocks, 0, unroll=min(columns, 8))

    for phase in range(slab // 8):
        tiles = range(phase, 3 * slab // 8 - phase)

        def pair(m, carry):
            number = first_step + 8 * phase + 2 * m
            step(field_a, field_b, tiles, number)
            step(field_b, field_a, tiles, number + 1)
            return carry

        lax.fori_loop(0, 4, pair, 0)

    if last:
        send_ref[...] = jnp.zeros(send_ref.shape, jnp.float32)
        width = per_device * (sections - 1)

        def place(d, carry):
            for i in range(per_device):
                mine = table[d, width + list_start + i]

                def earlier(n, c):
                    return c + jnp.where(table[d, width + n] == mine, 1, 0)

                count = lax.fori_loop(0, list_start + i, earlier, 0)
                send_ref[mine, d * CAP + count] = w_ref[d * per_device + i]
            return carry

        lax.fori_loop(0, columns, place, 0)
    else:
        for o in range(2 * columns):
            d, p = o // 2, o % 2
            state_ref[d, p * slab : (p + 1) * slab, :] = field_a[o, 8 + slab : 8 + 2 * slab, :]
            state_ref[d, (2 + p) * slab : (3 + p) * slab, :] = field_b[
                o, 8 + slab : 8 + 2 * slab, :
            ]


def unpack(tile, h, snaps, lane):
    if h:
        tile = pltpu.roll(tile, LANES - h * snaps, 1)
    return jnp.where(lane < snaps, tile, 0.0)


def product_kernel(
    order, slab, per_slab, snaps, sections, w_ref, s_ref, out_ref, sorted_ref, wide, low
):
    section = lax.axis_index("sec")
    slots = w_ref.shape[1]
    halves = slab // 8
    lane = lax.broadcasted_iota(jnp.int32, (8, LANES), 1)
    for column in range(0, len(order)):
        if order.index(column) % per_slab:
            continue
        at = slab_of(order, column, section, per_slab)
        for q in range(slots):
            tile = w_ref[column, q]
            sorted_ref[at, q] = tile
            for h in range(halves):
                w = unpack(tile, h, snaps, lane)
                w1 = w.astype(jnp.bfloat16).astype(jnp.float32)
                w2 = (w - w1).astype(jnp.bfloat16).astype(jnp.float32)
                w3 = w - w1 - w2
                start = pl.multiple_of(q * LANES + at * slab + 8 * h, 8)
                wide[pl.ds(start, 8), :] = w1 + pltpu.roll(w2, snaps, 1)
                low[pl.ds(start, 8), :] = w3
    both = wide[...].astype(jnp.bfloat16)
    tail = low[...].astype(jnp.bfloat16)
    rows = (((0,), (0,)), ((), ()))
    dot = functools.partial(
        lax.dot_general, dimension_numbers=rows, preferred_element_type=jnp.float32
    )
    sketch = s_ref[...]
    a_first = dot(both, sketch)
    a_tail = dot(tail, sketch)
    cross = a_first[:snaps] + (a_first[snaps:] + a_tail[:snaps])
    c_first = dot(both, both)
    c_tail = dot(tail, both)[:snaps, :]
    c_tail = jnp.where(lax.broadcasted_iota(jnp.int32, c_tail.shape, 1) < snaps, c_tail, 0.0)
    half = c_first[:snaps, :] + c_first[snaps:, :]
    own = half + pltpu.roll(half, snaps, 1)
    square = jnp.concatenate([c_tail, jnp.zeros_like(c_tail)], axis=0).T[:snaps, :]
    inner = jnp.where(
        lax.broadcasted_iota(jnp.int32, own.shape, 1) < snaps, own, 0.0
    ) + (c_tail + square)
    keep = jnp.where(section == sections - 1, 0.0, 1.0)
    out_ref[...] = jnp.zeros(out_ref.shape, jnp.float32)
    strips = cross.shape[1] // LANES
    for r in range(snaps // 8):
        for c in range(strips):
            out_ref[r * strips + c, 0] = (
                cross[8 * r : 8 * r + 8, c * LANES : (c + 1) * LANES] * keep
            )
        out_ref[r * strips, 1] = inner[8 * r : 8 * r + 8, :] * keep


def gather_kernel(parts_ref, out_ref):
    total = jnp.sum(parts_ref[...], axis=0)
    for i in range(out_ref.shape[0]):
        out_ref[i] = total


def factor_block(d, e, sub, lane):
    tiles = len(d)
    wide = lambda x: jnp.broadcast_to(x, (8, LANES))
    for p in range(tiles):
        first = 8 * p
        cols = [wide(d[p][:, first + j : first + j + 1]) for j in range(8)]
        s = [[wide(cols[k][j : j + 1, :]) if k >= j else None for k in range(8)] for j in range(8)]
        t = [wide(d[p][j : j + 1, :]) for j in range(8)]
        te = [wide(e[p][j : j + 1, :]) for j in range(8)]
        inv, m = [], [[None] * 8 for _ in range(8)]
        for j in range(8):
            inv.append(1.0 / s[j][j])
            for k in range(j + 1, 8):
                m[j][k] = s[j][k] * inv[j]
            for k in range(j + 1, 8):
                for n in range(k, 8):
                    s[k][n] = s[k][n] - m[j][k] * s[j][n]
                t[k] = t[k] - m[j][k] * t[j]
                te[k] = te[k] - m[j][k] * te[j]
        if p + 1 < tiles:
            z, ze = [None] * 8, [None] * 8
            for j in reversed(range(8)):
                z[j], ze[j] = t[j] * inv[j], te[j] * inv[j]
                for k in range(j + 1, 8):
                    z[j] = z[j] - m[j][k] * z[k]
                    ze[j] = ze[j] - m[j][k] * ze[k]
            for i in range(p + 1, tiles):
                di, ei = d[i], e[i]
                for j in range(8):
                    col = wide(d[i][:, first + j : first + j + 1])
                    di = di - col * z[j]
                    ei = ei - col * ze[j]
                d[i], e[i] = di, ei
        rows, rows_e = t[0] * lax.rsqrt(s[0][0]), te[0] * lax.rsqrt(s[0][0])
        for j in range(1, 8):
            root = lax.rsqrt(s[j][j])
            rows = jnp.where(sub == j, t[j] * root, rows)
            rows_e = jnp.where(sub == j, te[j] * root, rows_e)
        d[p] = jnp.where(lane >= sub + first, rows, 0.0)
        e[p] = rows_e
    return jnp.concatenate(d, axis=0), jnp.concatenate(e, axis=0)


def factor_kernel(scale, sections, parts_ref, omega_ref, s_ref, factor_ref, inverse_ref, g):
    rank = s_ref.shape[0]
    snaps = omega_ref.shape[0]
    strips = rank // LANES
    analysis = lax.axis_index("sec") == sections - 1
    rows_first = (((0,), (0,)), ((), ()))
    cross = jnp.concatenate(
        [
            jnp.concatenate([parts_ref[r * strips + c, 0] for c in range(strips)], axis=1)
            for r in range(snaps // 8)
        ],
        axis=0,
    )
    inner = jnp.concatenate([parts_ref[r * strips, 1] for r in range(snaps // 8)], axis=0)
    omega = omega_ref[...]
    half = cross + 0.5 * jnp.dot(
        inner[:, :snaps], omega, precision=highest, preferred_element_type=jnp.float32
    )
    left = jnp.concatenate([half, omega], axis=0)
    right = jnp.concatenate([omega, half], axis=0)
    g[...] = s_ref[...] + lax.dot_general(
        left, right, rows_first, precision=highest, preferred_element_type=jnp.float32
    )
    row_number = lax.broadcasted_iota(jnp.int32, (rank, rank), 0)
    lane_number = lax.broadcasted_iota(jnp.int32, (rank, rank), 1)
    inverse_ref[...] = jnp.where(row_number == lane_number, 1.0, 0.0)
    sub = lax.broadcasted_iota(jnp.int32, (8, LANES), 0)
    lane = lax.broadcasted_iota(jnp.int32, (8, LANES), 1)
    tiles = LANES // 8

    def block(k, carry):
        start = pl.multiple_of(k * LANES, LANES)
        d = [g[pl.ds(start + 8 * i, 8), pl.ds(start, LANES)] for i in range(tiles)]
        e = [jnp.where(lane == sub + 8 * i, 1.0, 0.0) for i in range(tiles)]
        upper, small = factor_block(d, e, sub, lane)
        panel = jnp.dot(
            small,
            jnp.concatenate([g[pl.ds(start, LANES), :], inverse_ref[pl.ds(start, LANES), :]], 1),
            precision=highest,
            preferred_element_type=jnp.float32,
        )
        lanes_all = lax.broadcasted_iota(jnp.int32, (LANES, rank), 1)
        after = lanes_all >= start + LANES
        fresh = jnp.where(after, panel[:, :rank], 0.0)
        below = panel[:, rank:]
        inverse_ref[pl.ds(start, LANES), :] = below
        change = lax.dot_general(
            fresh,
            jnp.concatenate([fresh, below], axis=1),
            rows_first,
            precision=highest,
            preferred_element_type=jnp.float32,
        )
        factor_ref[pl.ds(start, LANES), :] = fresh
        factor_ref[pl.ds(start, LANES), pl.ds(start, LANES)] = upper
        g[...] = g[...] - change[:, :rank]
        inverse_ref[...] = inverse_ref[...] - change[:, rank:]
        return carry

    lax.fori_loop(0, strips, block, 0)
    factor_ref[...] = jnp.where(analysis, factor_ref[...] * (1.0 / scale), 0.0)
    inverse_ref[...] = inverse_ref[...] * scale


def basis_kernel(
    slab, snaps, sections, inverse_ref, omega_ref, s_ref, w0, w1, w2, out_ref, wide
):
    analysis = lax.axis_index("sec") == sections - 1

    @pl.when(analysis)
    def _():
        lane = lax.broadcasted_iota(jnp.int32, (8, LANES), 1)
        slabs, slots = w0.shape[:2]

        def fill(q, carry):
            for a in range(slabs):
                tile = w0[a, q] + w1[a, q] + w2[a, q]
                for h in range(slab // 8):
                    start = pl.multiple_of(q * LANES + a * slab + 8 * h, 8)
                    wide[pl.ds(start, 8), :] = unpack(tile, h, snaps, lane)
            return carry

        lax.fori_loop(0, slots, fill, 0)
        inverse = inverse_ref[...]
        columns = (((1,), (1,)), ((), ()))
        mixed = lax.dot_general(
            omega_ref[...], inverse, columns, precision=highest, preferred_element_type=jnp.float32
        )
        mixed = jnp.concatenate([mixed, jnp.zeros_like(mixed)], axis=0)
        x1 = inverse.astype(jnp.bfloat16)
        rest = inverse - x1.astype(jnp.float32)
        x2 = rest.astype(jnp.bfloat16)
        rows = 256

        def strip(i, carry):
            at = pl.ds(pl.multiple_of(i * rows, rows), rows)
            s = s_ref[at, :]
            dot = functools.partial(
                lax.dot_general, dimension_numbers=columns, preferred_element_type=jnp.float32
            )
            q = dot(s, x1) + dot(s, x2)
            q = q + jnp.dot(
                wide[at, :], mixed, precision=highest, preferred_element_type=jnp.float32
            )
            out_ref[at, :] = q.astype(jnp.bfloat16)
            return carry

        lax.fori_loop(0, s_ref.shape[0] // rows, strip, 0)

    @pl.when(jnp.logical_not(analysis))
    def _():
        out_ref[...] = jnp.zeros(out_ref.shape, jnp.bfloat16)


def shards(potential, previous, wave_coeff, sketch_in, omega, blocks, owners):
    sections = lax.axis_size("sec")
    columns = lax.axis_size("dev")
    devices = sections * columns
    extent_x, extent_y, depth = potential.shape
    list_width = owners.shape[1]
    per_device = list_width // (sections - 1)
    snaps, rank = omega.shape
    slab = max(8, depth // columns)
    per_slab = slab * columns // depth
    slabs = depth // slab
    slots = columns * CAP
    order = neighbour_path(columns)
    path = []
    for section in range(sections - 1):
        path += [section * columns + d for d in (order if section % 2 == 0 else order[::-1])]
    up = [(path[i], path[i + per_slab]) for i in range(len(path) - per_slab)]
    down = [(b, a) for a, b in up]
    f32 = jnp.float32

    own_gram = lax.dot_general(
        sketch_in, sketch_in, (((0,), (0,)), ((), ())), preferred_element_type=f32
    )
    scaled = omega * jnp.asarray(
        decay ** np.arange(1, snaps + 1, dtype=np.float64), f32
    )[:, None]

    lists = jnp.pad(
        jnp.concatenate([blocks, owners], axis=1).astype(f32), ((0, 0), (0, LANES - 2 * list_width))
    )
    chunk = 6 * slab + 8
    operands = (potential, previous, wave_coeff, lists)
    outgoing = pl.pallas_call(
        functools.partial(split_kernel, order, slab, per_slab),
        out_shape=jax.ShapeDtypeStruct((columns, chunk, LANES), f32),
        in_specs=vmem(*operands),
        out_specs=pl.BlockSpec(memory_space=pltpu.VMEM),
        scratch_shapes=[pltpu.VMEM((6, depth, LANES), f32)],
        compiler_params=big(),
    )(*operands)
    outgoing, own_gram = lax.optimization_barrier((outgoing, own_gram))
    gram = lax.psum(own_gram, "dev")
    raw = lax.all_to_all(outgoing, "dev", split_axis=0, concat_axis=0, tiled=True)
    table = raw[:, 6 * slab, : 2 * list_width].astype(jnp.int32)

    def sides(x):
        return lax.ppermute(x, BOTH, up), x, lax.ppermute(x, BOTH, down)

    fields = sides(raw)
    state = fields
    held = jnp.zeros((columns * per_device, 8, LANES), f32)
    rounds = snaps // slab
    for number in range(rounds):
        last = number == rounds - 1
        operands = (table, *fields, *state, held)
        result = (columns, slots, 8, LANES) if last else (columns, 4 * slab, LANES)
        moved, held = pl.pallas_call(
            functools.partial(
                steps_kernel, number * slab, slab, per_device, last, snaps, sections
            ),
            out_shape=(
                jax.ShapeDtypeStruct(result, f32),
                jax.ShapeDtypeStruct(held.shape, f32),
            ),
            in_specs=[pl.BlockSpec(memory_space=pltpu.SMEM)] + vmem(*operands[1:]),
            out_specs=tuple(vmem(0, 0)),
            scratch_shapes=[pltpu.VMEM((2 * columns, 3 * slab + 16, LANES), f32)] * 2
            + [pltpu.VMEM((2 * columns, 3 * slab, LANES), f32)] * 2,
            compiler_params=big(),
        )(*operands)
        if not last:
            state = sides(moved)
    arrived = lax.all_to_all(moved, "dev", split_axis=0, concat_axis=0, tiled=True)

    operands = (arrived, sketch_in)
    parts, ordered = pl.pallas_call(
        functools.partial(product_kernel, order, slab, per_slab, snaps, sections),
        out_shape=(
            jax.ShapeDtypeStruct((devices, 2, 8, LANES), f32),
            jax.ShapeDtypeStruct((slabs, slots, 8, LANES), f32),
        ),
        in_specs=vmem(*operands),
        out_specs=tuple(vmem(0, 0)),
        scratch_shapes=[pltpu.VMEM((slots * depth, LANES), f32)] * 2,
        compiler_params=big(60),
    )(*operands)
    terms = lax.all_to_all(parts, BOTH, split_axis=0, concat_axis=0, tiled=True)
    copies = pl.pallas_call(
        gather_kernel,
        out_shape=jax.ShapeDtypeStruct(terms.shape, f32),
        in_specs=vmem(0),
        out_specs=pl.BlockSpec(memory_space=pltpu.VMEM),
    )(terms)
    sums = lax.all_to_all(copies, BOTH, split_axis=0, concat_axis=0, tiled=True)
    sums, ordered = lax.optimization_barrier((sums, ordered))
    pieces = [lax.ppermute(ordered, "sec", [(i, sections - 1)]) for i in range(sections - 1)]

    scale = math.sqrt(columns * columns * CAP * depth)
    operands = (sums, scaled, gram)
    factor, inverse = pl.pallas_call(
        functools.partial(factor_kernel, scale, sections),
        out_shape=(jax.ShapeDtypeStruct((rank, rank), f32),) * 2,
        in_specs=vmem(*operands),
        out_specs=tuple(vmem(0, 0)),
        scratch_shapes=[pltpu.VMEM((rank, rank), f32)],
        compiler_params=big(),
    )(*operands)
    operands = (inverse, scaled, sketch_in, *pieces)
    basis = pl.pallas_call(
        functools.partial(basis_kernel, slab, snaps, sections),
        out_shape=jax.ShapeDtypeStruct(sketch_in.shape, jnp.bfloat16),
        in_specs=vmem(*operands),
        out_specs=pl.BlockSpec(memory_space=pltpu.VMEM),
        scratch_shapes=[pltpu.VMEM((slots * depth, LANES), f32)],
        compiler_params=big(60),
    )(*operands)
    return (basis[None], factor[None])


def solution(mesh):
    placed = (
        P("dev", None, "sec"),
        P("dev", None, "sec"),
        P("dev", None, "sec"),
        P("dev", None),
        P(),
        P("dev", None),
        P("dev", None),
    )
    return jax.shard_map(
        shards,
        mesh=mesh,
        in_specs=placed,
        out_specs=(P("sec", "dev", None), P("sec", None, None)),
        check_vma=False,
    )
```

```python
import functools
import math

import jax
import jax.numpy as jnp
import numpy as np
from jax import lax
from jax.experimental import pallas as pl
from jax.experimental.pallas import tpu as pltpu
from jax.sharding import PartitionSpec as P

CAP = 2
damping = 0.05
LANES = 128
highest = lax.Precision.HIGHEST
decay = math.sqrt(1.0 - damping)
BOTH = ("sec", "dev")


def neighbour_path(columns):
    order = []
    for i in range(0, columns, 2):
        pair = [i, i + 1]
        order += pair if (i // 2) % 2 == 0 else pair[::-1]
    return order


def vmem(*arrays):
    return [pl.BlockSpec(memory_space=pltpu.VMEM)] * len(arrays)


def big(limit=48):
    return pltpu.CompilerParams(vmem_limit_bytes=limit << 20)


def slab_of(order, column, section, per_slab):
    place = order.index(column)
    forward, backward = place // per_slab, (len(order) - 1 - place) // per_slab
    return jnp.where(section % 2 == 0, forward, backward)


def split_kernel(order, slab, per_slab, u_ref, e_ref, k_ref, table_ref, out_ref, turned):
    section = lax.axis_index("sec")
    extent_x, extent_y, depth = u_ref.shape
    for a, ref in enumerate((u_ref, e_ref, k_ref)):
        for p in range(2):
            rows = jnp.concatenate([ref[x] for x in range(p, extent_x, 2)], axis=0)
            if a == 1:
                rows = rows * decay
            turned[2 * a + p] = rows.T
    for column in range(len(order)):
        at = slab_of(order, column, section, per_slab)
        start = pl.multiple_of(at * slab, 8)
        for q in range(6):
            out_ref[column, q * slab : (q + 1) * slab, :] = turned[q, pl.ds(start, slab), :]
        out_ref[column, 6 * slab :, :] = jnp.broadcast_to(table_ref[...], (8, LANES))


def steps_kernel(*args):
    sections = args[5]

    @pl.when(lax.axis_index("sec") < sections - 1)
    def _():
        evolve(*args)


def evolve(
    first_step, slab, per_device, last, snaps, sections,
    table, kl, kc, kr, sl, sc, sr, w_in, *rest,
):
    if last:
        send_ref, w_ref, field_a, field_b, gain, own = rest
    else:
        state_ref, w_ref, field_a, field_b, gain, own = rest
    list_start = lax.axis_index("sec") * per_device
    columns = kc.shape[0]
    rows = 3 * slab
    lane = lax.broadcasted_iota(jnp.int32, (8, LANES), 1)
    y_first, y_last = lane % 32 == 0, lane % 32 == 31
    zero = jnp.zeros((8, LANES), jnp.float32)

    for o in range(2 * columns):
        d, p = o // 2, o % 2
        for field, at in ((field_a, p), (field_b, 2 + p)):
            field[o, 0:8, :] = zero
            field[o, 8 + rows : 16 + rows, :] = zero
            for h, ref in enumerate((sl, sc, sr)):
                field[o, 8 + h * slab : 8 + (h + 1) * slab, :] = ref[
                    d, at * slab : (at + 1) * slab, :
                ]
        for h, ref in enumerate((kl, kc, kr)):
            k = ref[d, (4 + p) * slab : (5 + p) * slab, :]
            gain[o, h * slab : (h + 1) * slab, :] = k * (1.0 / decay)
            own[o, h * slab : (h + 1) * slab, :] = ((2.0 - damping) - 6.0 * k) * (1.0 / decay)
    w_ref[...] = w_in[...]

    def step(src, dst, tiles, number):
        for z in tiles:
            at = slice(8 + 8 * z, 16 + 8 * z)
            low = slice(7 + 8 * z, 15 + 8 * z)
            high = slice(9 + 8 * z, 17 + 8 * z)
            here = slice(8 * z, 8 * z + 8)
            values = [src[o, at, :] for o in range(2 * columns)]
            up = [pltpu.roll(values[2 * d + 1], 32, 1) for d in range(columns)]
            down = [pltpu.roll(values[2 * d], LANES - 32, 1) for d in range(columns)]
            for o in range(2 * columns):
                d, p = o // 2, o % 2
                v = values[o]
                if p == 0:
                    side = jnp.where(lane < 32, up[d - 1] if d > 0 else zero, up[d])
                    total = values[o + 1] + side
                else:
                    side = jnp.where(
                        lane >= LANES - 32, down[d + 1] if d + 1 < columns else zero, down[d]
                    )
                    total = values[o - 1] + side
                total = total + (src[o, low, :] + src[o, high, :])
                total = total + jnp.where(y_first, 0.0, pltpu.roll(v, 1, 1))
                total = total + jnp.where(y_last, 0.0, pltpu.roll(v, LANES - 1, 1))
                dst[o, at, :] = own[o, here, :] * v + gain[o, here, :] * total - dst[o, at, :]

        def column_blocks(d, carry):
            for i in range(per_device):
                block = table[d, list_start + i]
                x, y = block >> 5, block & 31
                at_lane = ((x >> 1) << 5) + y
                o = 2 * d + (x & 1)
                j = d * per_device + i
                held = w_ref[j]
                for h in range(slab // 8):
                    target = h * snaps + number
                    value = dst[o, 8 + slab + 8 * h : 16 + slab + 8 * h, :]
                    moved = pltpu.roll(value, (target - at_lane) & (LANES - 1), 1)
                    held = jnp.where(lane == target, moved, held)
                w_ref[j] = held
            return carry

        lax.fori_loop(0, columns, column_blocks, 0, unroll=min(columns, 8))

    for phase in range(slab // 8):
        tiles = range(phase, 3 * slab // 8 - phase)

        def pair(m, carry):
            number = first_step + 8 * phase + 2 * m
            step(field_a, field_b, tiles, number)
            step(field_b, field_a, tiles, number + 1)
            return carry

        lax.fori_loop(0, 4, pair, 0)

    if last:
        send_ref[...] = jnp.zeros(send_ref.shape, jnp.float32)
        width = per_device * (sections - 1)

        def place(d, carry):
            for i in range(per_device):
                mine = table[d, width + list_start + i]

                def earlier(n, c):
                    return c + jnp.where(table[d, width + n] == mine, 1, 0)

                count = lax.fori_loop(0, list_start + i, earlier, 0)
                send_ref[mine, d * CAP + count] = w_ref[d * per_device + i]
            return carry

        lax.fori_loop(0, columns, place, 0)
    else:
        for o in range(2 * columns):
            d, p = o // 2, o % 2
            state_ref[d, p * slab : (p + 1) * slab, :] = field_a[o, 8 + slab : 8 + 2 * slab, :]
            state_ref[d, (2 + p) * slab : (3 + p) * slab, :] = field_b[
                o, 8 + slab : 8 + 2 * slab, :
            ]


def unpack(tile, h, snaps, lane):
    if h:
        tile = pltpu.roll(tile, LANES - h * snaps, 1)
    return jnp.where(lane < snaps, tile, 0.0)


def product_kernel(*args):
    sections = args[4]

    @pl.when(lax.axis_index("sec") < sections - 1)
    def _():
        products(*args)


def products(order, slab, per_slab, snaps, sections, w_ref, s_ref, out_ref, sorted_ref, wide, low):
    section = lax.axis_index("sec")
    slots = w_ref.shape[1]
    halves = slab // 8
    lane = lax.broadcasted_iota(jnp.int32, (8, LANES), 1)
    for column in range(0, len(order)):
        if order.index(column) % per_slab:
            continue
        at = slab_of(order, column, section, per_slab)
        for q in range(slots):
            tile = w_ref[column, q]
            sorted_ref[at, q] = tile
            for h in range(halves):
                w = unpack(tile, h, snaps, lane)
                w1 = w.astype(jnp.bfloat16).astype(jnp.float32)
                w2 = (w - w1).astype(jnp.bfloat16).astype(jnp.float32)
                w3 = w - w1 - w2
                start = pl.multiple_of(q * LANES + at * slab + 8 * h, 8)
                wide[pl.ds(start, 8), :] = w1 + pltpu.roll(w2, snaps, 1)
                low[pl.ds(start, 8), :] = w3
    both = wide[...].astype(jnp.bfloat16)
    tail = low[...].astype(jnp.bfloat16)
    rows = (((0,), (0,)), ((), ()))
    dot = functools.partial(
        lax.dot_general, dimension_numbers=rows, preferred_element_type=jnp.float32
    )
    sketch = s_ref[...]
    a_first = dot(both, sketch)
    a_tail = dot(tail, sketch)
    cross = a_first[:snaps] + (a_first[snaps:] + a_tail[:snaps])
    c_first = dot(both, both)
    c_tail = dot(tail, both)[:snaps, :]
    c_tail = jnp.where(lax.broadcasted_iota(jnp.int32, c_tail.shape, 1) < snaps, c_tail, 0.0)
    half = c_first[:snaps, :] + c_first[snaps:, :]
    own = half + pltpu.roll(half, snaps, 1)
    square = jnp.concatenate([c_tail, jnp.zeros_like(c_tail)], axis=0).T[:snaps, :]
    inner = jnp.where(
        lax.broadcasted_iota(jnp.int32, own.shape, 1) < snaps, own, 0.0
    ) + (c_tail + square)
    strips = cross.shape[1] // LANES
    share = out_ref.shape[1]
    for r in range(snaps // 8):
        here = slice(8 * r, 8 * r + 8)
        for c in range(strips):
            at = r * (strips + 1) + c
            out_ref[at // share, at % share] = cross[here, c * LANES : (c + 1) * LANES]
        at = r * (strips + 1) + strips
        out_ref[at // share, at % share] = inner[here, :]


def factor_block(d, e, sub, lane):
    tiles = len(d)
    wide = lambda x: jnp.broadcast_to(x, (8, LANES))
    for p in range(tiles):
        first = 8 * p
        cols = [wide(d[p][:, first + j : first + j + 1]) for j in range(8)]
        s = [[wide(cols[k][j : j + 1, :]) if k >= j else None for k in range(8)] for j in range(8)]
        t = [wide(d[p][j : j + 1, :]) for j in range(8)]
        te = [wide(e[p][j : j + 1, :]) for j in range(8)]
        inv, m = [], [[None] * 8 for _ in range(8)]
        for j in range(8):
            inv.append(1.0 / s[j][j])
            for k in range(j + 1, 8):
                m[j][k] = s[j][k] * inv[j]
            for k in range(j + 1, 8):
                for n in range(k, 8):
                    s[k][n] = s[k][n] - m[j][k] * s[j][n]
                t[k] = t[k] - m[j][k] * t[j]
                te[k] = te[k] - m[j][k] * te[j]
        if p + 1 < tiles:
            z, ze = [None] * 8, [None] * 8
            for j in reversed(range(8)):
                z[j], ze[j] = t[j] * inv[j], te[j] * inv[j]
                for k in range(j + 1, 8):
                    z[j] = z[j] - m[j][k] * z[k]
                    ze[j] = ze[j] - m[j][k] * ze[k]
            for i in range(p + 1, tiles):
                di, ei = d[i], e[i]
                for j in range(8):
                    col = wide(d[i][:, first + j : first + j + 1])
                    di = di - col * z[j]
                    ei = ei - col * ze[j]
                d[i], e[i] = di, ei
        rows, rows_e = t[0] * lax.rsqrt(s[0][0]), te[0] * lax.rsqrt(s[0][0])
        for j in range(1, 8):
            root = lax.rsqrt(s[j][j])
            rows = jnp.where(sub == j, t[j] * root, rows)
            rows_e = jnp.where(sub == j, te[j] * root, rows_e)
        d[p] = jnp.where(lane >= sub + first, rows, 0.0)
        e[p] = rows_e
    return jnp.concatenate(d, axis=0), jnp.concatenate(e, axis=0)


def factor_kernel(scale, sections, parts_ref, omega_ref, s_ref, factor_ref, inverse_ref, g):
    analysis = lax.axis_index("sec") == sections - 1

    @pl.when(analysis)
    def _():
        factorize(scale, parts_ref, omega_ref, s_ref, factor_ref, inverse_ref, g)

    @pl.when(jnp.logical_not(analysis))
    def _():
        factor_ref[...] = jnp.zeros(factor_ref.shape, jnp.float32)


def factorize(scale, parts_ref, omega_ref, s_ref, factor_ref, inverse_ref, g):
    rank = s_ref.shape[0]
    snaps = omega_ref.shape[0]
    strips = rank // LANES
    rows_first = (((0,), (0,)), ((), ()))

    def band(r, c):
        return parts_ref[r * (strips + 1) + c]

    cross = jnp.concatenate(
        [
            jnp.concatenate([band(r, c) for c in range(strips)], axis=1)
            for r in range(snaps // 8)
        ],
        axis=0,
    )
    inner = jnp.concatenate([band(r, strips) for r in range(snaps // 8)], axis=0)
    omega = omega_ref[...]
    half = cross + 0.5 * jnp.dot(
        inner[:, :snaps], omega, precision=highest, preferred_element_type=jnp.float32
    )
    left = jnp.concatenate([half, omega], axis=0)
    right = jnp.concatenate([omega, half], axis=0)
    g[...] = s_ref[...] + lax.dot_general(
        left, right, rows_first, precision=highest, preferred_element_type=jnp.float32
    )
    row_number = lax.broadcasted_iota(jnp.int32, (rank, rank), 0)
    lane_number = lax.broadcasted_iota(jnp.int32, (rank, rank), 1)
    inverse_ref[...] = jnp.where(row_number == lane_number, 1.0, 0.0)
    sub = lax.broadcasted_iota(jnp.int32, (8, LANES), 0)
    lane = lax.broadcasted_iota(jnp.int32, (8, LANES), 1)
    tiles = LANES // 8

    def block(k, carry):
        start = pl.multiple_of(k * LANES, LANES)
        d = [g[pl.ds(start + 8 * i, 8), pl.ds(start, LANES)] for i in range(tiles)]
        e = [jnp.where(lane == sub + 8 * i, 1.0, 0.0) for i in range(tiles)]
        upper, small = factor_block(d, e, sub, lane)
        panel = jnp.dot(
            small,
            jnp.concatenate([g[pl.ds(start, LANES), :], inverse_ref[pl.ds(start, LANES), :]], 1),
            precision=highest,
            preferred_element_type=jnp.float32,
        )
        lanes_all = lax.broadcasted_iota(jnp.int32, (LANES, rank), 1)
        after = lanes_all >= start + LANES
        fresh = jnp.where(after, panel[:, :rank], 0.0)
        below = panel[:, rank:]
        inverse_ref[pl.ds(start, LANES), :] = below
        change = lax.dot_general(
            fresh,
            jnp.concatenate([fresh, below], axis=1),
            rows_first,
            precision=highest,
            preferred_element_type=jnp.float32,
        )
        factor_ref[pl.ds(start, LANES), :] = fresh
        factor_ref[pl.ds(start, LANES), pl.ds(start, LANES)] = upper
        g[...] = g[...] - change[:, :rank]
        inverse_ref[...] = inverse_ref[...] - change[:, rank:]
        return carry

    lax.fori_loop(0, strips, block, 0)
    factor_ref[...] = factor_ref[...] * (1.0 / scale)
    inverse_ref[...] = (inverse_ref[...] * scale).T


def basis_kernel(
    slab, snaps, sections, inverse_ref, omega_ref, s_ref, w0, w1, w2, out_ref, wide
):
    analysis = lax.axis_index("sec") == sections - 1

    @pl.when(analysis)
    def _():
        lane = lax.broadcasted_iota(jnp.int32, (8, LANES), 1)
        slabs, slots = w0.shape[:2]

        def fill(q, carry):
            for a in range(slabs):
                tile = w0[a, q] + w1[a, q] + w2[a, q]
                for h in range(slab // 8):
                    w = unpack(tile, h, snaps, lane)
                    high = w.astype(jnp.bfloat16).astype(jnp.float32)
                    start = pl.multiple_of(q * LANES + a * slab + 8 * h, 8)
                    wide[pl.ds(start, 8), :] = high + pltpu.roll(w - high, snaps, 1)
            return carry

        lax.fori_loop(0, slots, fill, 0)

        def split(x):
            high = x.astype(jnp.bfloat16)
            return high, (x - high.astype(jnp.float32)).astype(jnp.bfloat16)

        dot = functools.partial(jnp.dot, preferred_element_type=jnp.float32)
        inverse = inverse_ref[...]
        mixed = jnp.dot(
            omega_ref[...], inverse, precision=highest, preferred_element_type=jnp.float32
        )
        x1, x2 = split(inverse)
        m1, m2 = split(jnp.concatenate([mixed, mixed], axis=0))
        rows = 256

        def strip(i, carry):
            at = pl.ds(pl.multiple_of(i * rows, rows), rows)
            s = s_ref[at, :]
            w = wide[at, :].astype(jnp.bfloat16)
            q = (dot(s, x1) + dot(s, x2)) + (dot(w, m1) + dot(w, m2))
            out_ref[at, :] = q.astype(jnp.bfloat16)
            return carry

        lax.fori_loop(0, s_ref.shape[0] // rows, strip, 0)

    @pl.when(jnp.logical_not(analysis))
    def _():
        out_ref[...] = jnp.zeros(out_ref.shape, jnp.bfloat16)


def shards(potential, previous, wave_coeff, sketch_in, omega, blocks, owners):
    sections = lax.axis_size("sec")
    columns = lax.axis_size("dev")
    devices = sections * columns
    extent_x, extent_y, depth = potential.shape
    list_width = owners.shape[1]
    per_device = list_width // (sections - 1)
    snaps, rank = omega.shape
    slab = max(8, depth // columns)
    per_slab = slab * columns // depth
    slabs = depth // slab
    slots = columns * CAP
    order = neighbour_path(columns)
    path = []
    for section in range(sections - 1):
        path += [section * columns + d for d in (order if section % 2 == 0 else order[::-1])]
    up = [(path[i], path[i + per_slab]) for i in range(len(path) - per_slab)]
    down = [(b, a) for a, b in up]
    f32 = jnp.float32

    analysis = lax.axis_index("sec") == sections - 1

    def whole_gram():
        own = lax.dot_general(
            sketch_in, sketch_in, (((0,), (0,)), ((), ())), preferred_element_type=f32
        )
        own = own.reshape(columns, rank // columns, rank)
        own = lax.all_to_all(own, "dev", split_axis=0, concat_axis=0, tiled=True)
        own = jnp.broadcast_to(jnp.sum(own, axis=0)[None], own.shape)
        own = lax.all_to_all(own, "dev", split_axis=0, concat_axis=0, tiled=True)
        return own.reshape(rank, rank)

    scaled = omega * jnp.asarray(
        decay ** np.arange(1, snaps + 1, dtype=np.float64), f32
    )[:, None]

    lists = jnp.pad(
        jnp.concatenate([blocks, owners], axis=1).astype(f32), ((0, 0), (0, LANES - 2 * list_width))
    )
    chunk = 6 * slab + 8
    operands = (potential, previous, wave_coeff, lists)
    outgoing = pl.pallas_call(
        functools.partial(split_kernel, order, slab, per_slab),
        out_shape=jax.ShapeDtypeStruct((columns, chunk, LANES), f32),
        in_specs=vmem(*operands),
        out_specs=pl.BlockSpec(memory_space=pltpu.VMEM),
        scratch_shapes=[pltpu.VMEM((6, depth, LANES), f32)],
        compiler_params=big(),
    )(*operands)
    raw = lax.all_to_all(outgoing, "dev", split_axis=0, concat_axis=0, tiled=True)
    gram, raw = lax.optimization_barrier(
        (lax.cond(analysis, whole_gram, lambda: jnp.zeros((rank, rank), f32)), raw)
    )
    table = raw[:, 6 * slab, : 2 * list_width].astype(jnp.int32)

    def sides(x):
        return lax.ppermute(x, BOTH, up), x, lax.ppermute(x, BOTH, down)

    fields = sides(raw)
    state = fields
    held = jnp.zeros((columns * per_device, 8, LANES), f32)
    rounds = snaps // slab
    for number in range(rounds):
        last = number == rounds - 1
        operands = (table, *fields, *state, held)
        result = (columns, slots, 8, LANES) if last else (columns, 4 * slab, LANES)
        moved, held = pl.pallas_call(
            functools.partial(
                steps_kernel, number * slab, slab, per_device, last, snaps, sections
            ),
            out_shape=(
                jax.ShapeDtypeStruct(result, f32),
                jax.ShapeDtypeStruct(held.shape, f32),
            ),
            in_specs=[pl.BlockSpec(memory_space=pltpu.SMEM)] + vmem(*operands[1:]),
            out_specs=tuple(vmem(0, 0)),
            scratch_shapes=[pltpu.VMEM((2 * columns, 3 * slab + 16, LANES), f32)] * 2
            + [pltpu.VMEM((2 * columns, 3 * slab, LANES), f32)] * 2,
            compiler_params=big(),
        )(*operands)
        if not last:
            state = sides(moved)
    arrived = lax.all_to_all(moved, "dev", split_axis=0, concat_axis=0, tiled=True)

    operands = (arrived, sketch_in)
    bands = (snaps // 8) * (rank // LANES + 1)
    share = -(-bands // columns)
    parts, ordered = pl.pallas_call(
        functools.partial(product_kernel, order, slab, per_slab, snaps, sections),
        out_shape=(
            jax.ShapeDtypeStruct((columns, share, 8, LANES), f32),
            jax.ShapeDtypeStruct((slabs, slots, 8, LANES), f32),
        ),
        in_specs=vmem(*operands),
        out_specs=tuple(vmem(0, 0)),
        scratch_shapes=[pltpu.VMEM((slots * depth, LANES), f32)] * 2,
        compiler_params=big(60),
    )(*operands)

    def to_analysis(x):
        return [lax.ppermute(x, "sec", [(i, sections - 1)]) for i in range(sections - 1)]

    terms = lax.all_to_all(parts, "dev", split_axis=0, concat_axis=0, tiled=True)
    terms = to_analysis(jnp.sum(terms, axis=0))
    pieces = to_analysis(ordered)

    def exchange(terms):
        total = jnp.broadcast_to(sum(terms[1:], terms[0])[None], parts.shape)
        return lax.all_to_all(total, "dev", split_axis=0, concat_axis=0, tiled=True)

    sums = lax.cond(analysis, exchange, lambda terms: jnp.zeros(parts.shape, f32), terms)
    sums = sums.reshape(columns * share, 8, LANES)

    scale = math.sqrt(columns * columns * CAP * depth)
    operands = (sums, scaled, gram)
    factor, inverse = pl.pallas_call(
        functools.partial(factor_kernel, scale, sections),
        out_shape=(jax.ShapeDtypeStruct((rank, rank), f32),) * 2,
        in_specs=vmem(*operands),
        out_specs=tuple(vmem(0, 0)),
        scratch_shapes=[pltpu.VMEM((rank, rank), f32)],
        compiler_params=big(),
    )(*operands)
    operands = (inverse, scaled, sketch_in, *pieces)
    basis = pl.pallas_call(
        functools.partial(basis_kernel, slab, snaps, sections),
        out_shape=jax.ShapeDtypeStruct(sketch_in.shape, jnp.bfloat16),
        in_specs=vmem(*operands),
        out_specs=pl.BlockSpec(memory_space=pltpu.VMEM),
        scratch_shapes=[pltpu.VMEM((slots * depth, LANES), f32)],
        compiler_params=big(60),
    )(*operands)
    return (basis[None], factor[None])


def solution(mesh):
    placed = (
        P("dev", None, "sec"),
        P("dev", None, "sec"),
        P("dev", None, "sec"),
        P("dev", None),
        P(),
        P("dev", None),
        P("dev", None),
    )
    return jax.shard_map(
        shards,
        mesh=mesh,
        in_specs=placed,
        out_specs=(P("sec", "dev", None), P("sec", None, None)),
        check_vma=False,
    )
```

```python
import functools
import math

import jax
import jax.numpy as jnp
import numpy as np
from jax import lax
from jax.experimental import pallas as pl
from jax.experimental.pallas import tpu as pltpu
from jax.sharding import PartitionSpec as P

CAP = 2
damping = 0.05
LANES = 128
highest = lax.Precision.HIGHEST
decay = math.sqrt(1.0 - damping)
BOTH = ("sec", "dev")


def neighbour_path(columns):
    order = []
    for i in range(0, columns, 2):
        pair = [i, i + 1]
        order += pair if (i // 2) % 2 == 0 else pair[::-1]
    return order


def vmem(*arrays):
    return [pl.BlockSpec(memory_space=pltpu.VMEM)] * len(arrays)


def big(limit=48):
    return pltpu.CompilerParams(vmem_limit_bytes=limit << 20)


def slab_of(order, column, section, per_slab):
    place = order.index(column)
    forward, backward = place // per_slab, (len(order) - 1 - place) // per_slab
    return jnp.where(section % 2 == 0, forward, backward)


def split_kernel(order, slab, per_slab, u_ref, e_ref, k_ref, table_ref, out_ref, turned):
    section = lax.axis_index("sec")
    extent_x, extent_y, depth = u_ref.shape
    for a, ref in enumerate((u_ref, e_ref, k_ref)):
        for p in range(2):
            rows = jnp.concatenate([ref[x] for x in range(p, extent_x, 2)], axis=0)
            if a == 1:
                rows = rows * decay
            turned[2 * a + p] = rows.T
    for column in range(len(order)):
        at = slab_of(order, column, section, per_slab)
        start = pl.multiple_of(at * slab, 8)
        for q in range(6):
            out_ref[column, q * slab : (q + 1) * slab, :] = turned[q, pl.ds(start, slab), :]
        out_ref[column, 6 * slab :, :] = jnp.broadcast_to(table_ref[...], (8, LANES))


def steps_kernel(*args):
    sections = args[5]

    @pl.when(lax.axis_index("sec") < sections - 1)
    def _():
        evolve(*args)


def evolve(
    first_step, slab, per_device, last, snaps, sections,
    table, kl, kc, kr, sl, sc, sr, w_in, *rest,
):
    if last:
        send_ref, w_ref, field_a, field_b, gain, own = rest
    else:
        state_ref, w_ref, field_a, field_b, gain, own = rest
    list_start = lax.axis_index("sec") * per_device
    columns = kc.shape[0]
    rows = 3 * slab
    lane = lax.broadcasted_iota(jnp.int32, (8, LANES), 1)
    y_first, y_last = lane % 32 == 0, lane % 32 == 31
    zero = jnp.zeros((8, LANES), jnp.float32)

    for o in range(2 * columns):
        d, p = o // 2, o % 2
        for field, at in ((field_a, p), (field_b, 2 + p)):
            field[o, 0:8, :] = zero
            field[o, 8 + rows : 16 + rows, :] = zero
            for h, ref in enumerate((sl, sc, sr)):
                field[o, 8 + h * slab : 8 + (h + 1) * slab, :] = ref[
                    d, at * slab : (at + 1) * slab, :
                ]
        for h, ref in enumerate((kl, kc, kr)):
            k = ref[d, (4 + p) * slab : (5 + p) * slab, :]
            gain[o, h * slab : (h + 1) * slab, :] = k * (1.0 / decay)
            own[o, h * slab : (h + 1) * slab, :] = ((2.0 - damping) - 6.0 * k) * (1.0 / decay)
    w_ref[...] = w_in[...]

    def step(src, dst, tiles, number):
        for z in tiles:
            at = slice(8 + 8 * z, 16 + 8 * z)
            low = slice(7 + 8 * z, 15 + 8 * z)
            high = slice(9 + 8 * z, 17 + 8 * z)
            here = slice(8 * z, 8 * z + 8)
            values = [src[o, at, :] for o in range(2 * columns)]
            up = [pltpu.roll(values[2 * d + 1], 32, 1) for d in range(columns)]
            down = [pltpu.roll(values[2 * d], LANES - 32, 1) for d in range(columns)]
            for o in range(2 * columns):
                d, p = o // 2, o % 2
                v = values[o]
                if p == 0:
                    side = jnp.where(lane < 32, up[d - 1] if d > 0 else zero, up[d])
                    total = values[o + 1] + side
                else:
                    side = jnp.where(
                        lane >= LANES - 32, down[d + 1] if d + 1 < columns else zero, down[d]
                    )
                    total = values[o - 1] + side
                total = total + (src[o, low, :] + src[o, high, :])
                total = total + jnp.where(y_first, 0.0, pltpu.roll(v, 1, 1))
                total = total + jnp.where(y_last, 0.0, pltpu.roll(v, LANES - 1, 1))
                dst[o, at, :] = own[o, here, :] * v + gain[o, here, :] * total - dst[o, at, :]

        def column_blocks(d, carry):
            for i in range(per_device):
                block = table[d, list_start + i]
                x, y = block >> 5, block & 31
                at_lane = ((x >> 1) << 5) + y
                o = 2 * d + (x & 1)
                j = d * per_device + i
                held = w_ref[j]
                for h in range(slab // 8):
                    target = h * snaps + number
                    value = dst[o, 8 + slab + 8 * h : 16 + slab + 8 * h, :]
                    moved = pltpu.roll(value, (target - at_lane) & (LANES - 1), 1)
                    held = jnp.where(lane == target, moved, held)
                w_ref[j] = held
            return carry

        lax.fori_loop(0, columns, column_blocks, 0, unroll=min(columns, 8))

    for phase in range(slab // 8):
        tiles = range(phase, 3 * slab // 8 - phase)

        def pair(m, carry):
            number = first_step + 8 * phase + 2 * m
            step(field_a, field_b, tiles, number)
            step(field_b, field_a, tiles, number + 1)
            return carry

        lax.fori_loop(0, 4, pair, 0)

    if last:
        send_ref[...] = jnp.zeros(send_ref.shape, jnp.float32)
        width = per_device * (sections - 1)

        def place(d, carry):
            for i in range(per_device):
                mine = table[d, width + list_start + i]

                def earlier(n, c):
                    return c + jnp.where(table[d, width + n] == mine, 1, 0)

                count = lax.fori_loop(0, list_start + i, earlier, 0)
                send_ref[mine, d * CAP + count] = w_ref[d * per_device + i]
            return carry

        lax.fori_loop(0, columns, place, 0)
    else:
        for o in range(2 * columns):
            d, p = o // 2, o % 2
            state_ref[d, p * slab : (p + 1) * slab, :] = field_a[o, 8 + slab : 8 + 2 * slab, :]
            state_ref[d, (2 + p) * slab : (3 + p) * slab, :] = field_b[
                o, 8 + slab : 8 + 2 * slab, :
            ]


def unpack(tile, h, snaps, lane):
    if h:
        tile = pltpu.roll(tile, LANES - h * snaps, 1)
    return jnp.where(lane < snaps, tile, 0.0)


def product_kernel(*args):
    sections = args[4]

    @pl.when(lax.axis_index("sec") < sections - 1)
    def _():
        products(*args)


def products(order, slab, per_slab, snaps, sections, w_ref, s_ref, out_ref, wide, low):
    section = lax.axis_index("sec")
    slots = w_ref.shape[1]
    halves = slab // 8
    lane = lax.broadcasted_iota(jnp.int32, (8, LANES), 1)
    for column in range(0, len(order)):
        if order.index(column) % per_slab:
            continue
        at = slab_of(order, column, section, per_slab)
        for q in range(slots):
            tile = w_ref[column, q]
            for h in range(halves):
                w = unpack(tile, h, snaps, lane)
                w1 = w.astype(jnp.bfloat16).astype(jnp.float32)
                w2 = (w - w1).astype(jnp.bfloat16).astype(jnp.float32)
                w3 = w - w1 - w2
                start = pl.multiple_of(q * LANES + at * slab + 8 * h, 8)
                wide[pl.ds(start, 8), :] = w1 + pltpu.roll(w2, snaps, 1)
                low[pl.ds(start, 8), :] = w3
    both = wide[...].astype(jnp.bfloat16)
    tail = low[...].astype(jnp.bfloat16)
    rows = (((0,), (0,)), ((), ()))
    dot = functools.partial(
        lax.dot_general, dimension_numbers=rows, preferred_element_type=jnp.float32
    )
    sketch = s_ref[...]
    a_first = dot(both, sketch)
    a_tail = dot(tail, sketch)
    cross = a_first[:snaps] + (a_first[snaps:] + a_tail[:snaps])
    c_first = dot(both, both)
    c_tail = dot(tail, both)[:snaps, :]
    c_tail = jnp.where(lax.broadcasted_iota(jnp.int32, c_tail.shape, 1) < snaps, c_tail, 0.0)
    half = c_first[:snaps, :] + c_first[snaps:, :]
    own = half + pltpu.roll(half, snaps, 1)
    square = jnp.concatenate([c_tail, jnp.zeros_like(c_tail)], axis=0).T[:snaps, :]
    inner = jnp.where(
        lax.broadcasted_iota(jnp.int32, own.shape, 1) < snaps, own, 0.0
    ) + (c_tail + square)
    strips = cross.shape[1] // LANES
    share = out_ref.shape[1]
    for r in range(snaps // 8):
        here = slice(8 * r, 8 * r + 8)
        for c in range(strips):
            at = r * (strips + 1) + c
            out_ref[at // share, at % share] = cross[here, c * LANES : (c + 1) * LANES]
        at = r * (strips + 1) + strips
        out_ref[at // share, at % share] = inner[here, :]


def three(x):
    x1 = x.astype(jnp.bfloat16)
    rest = x - x1.astype(jnp.float32)
    x2 = rest.astype(jnp.bfloat16)
    return x1, x2, (rest - x2.astype(jnp.float32)).astype(jnp.bfloat16)


def factor_block(d, e, sub, lane):
    tiles = len(d)

    def wide(x):
        return jnp.broadcast_to(x, (8, LANES))

    def stack(values):
        out = values[0]
        for j in range(1, 8):
            out = jnp.where(sub == j, values[j], out)
        return out

    for p in range(tiles):
        first = 8 * p
        cols = [wide(d[p][:, first + j : first + j + 1]) for j in range(8)]
        s = [[wide(cols[k][j : j + 1, :]) if k >= j else None for k in range(8)] for j in range(8)]
        t = [wide(d[p][j : j + 1, :]) for j in range(8)]
        te = [wide(e[p][j : j + 1, :]) for j in range(8)]
        inv, m = [], [[None] * 8 for _ in range(8)]
        for j in range(8):
            guess = pl.reciprocal(s[j][j], approx=True)
            guess = guess * (2.0 - s[j][j] * guess)
            inv.append(guess * (2.0 - s[j][j] * guess))
            for k in range(j + 1, 8):
                m[j][k] = s[j][k] * inv[j]
            for k in range(j + 1, 8):
                for n in range(k, 8):
                    s[k][n] = s[k][n] - m[j][k] * s[j][n]
                t[k] = t[k] - m[j][k] * t[j]
                te[k] = te[k] - m[j][k] * te[j]
        if p + 1 < tiles:
            z, ze = [None] * 8, [None] * 8
            for j in reversed(range(8)):
                z[j], ze[j] = t[j] * inv[j], te[j] * inv[j]
                for k in range(j + 1, 8):
                    z[j] = z[j] - m[j][k] * z[k]
                    ze[j] = ze[j] - m[j][k] * ze[k]
            i = p + 1
            parts, parts_e = [], []
            for j in range(8):
                col = wide(d[i][:, first + j : first + j + 1])
                parts.append(col * z[j])
                parts_e.append(col * ze[j])
            while len(parts) > 1:
                parts = [x + y for x, y in zip(parts[::2], parts[1::2])]
                parts_e = [x + y for x, y in zip(parts_e[::2], parts_e[1::2])]
            if p + 2 < tiles:
                p1, p2, p3 = three(d[p])
                z1, z2, z3 = three(jnp.concatenate([stack(z), stack(ze)], axis=1))
                change = lax.dot_general(
                    jnp.concatenate([p1, p1, p1, p2, p2, p3], axis=0),
                    jnp.concatenate([z1, z2, z3, z1, z2, z1], axis=0),
                    (((0,), (0,)), ((), ())),
                    preferred_element_type=jnp.float32,
                )
                for n in range(p + 2, tiles):
                    d[n] = d[n] - change[8 * n : 8 * n + 8, :LANES]
                    e[n] = e[n] - change[8 * n : 8 * n + 8, LANES:]
            d[i], e[i] = d[i] - parts[0], e[i] - parts_e[0]
        roots = [lax.rsqrt(s[j][j]) for j in range(8)]
        d[p] = jnp.where(lane >= sub + first, stack([t[j] * roots[j] for j in range(8)]), 0.0)
        e[p] = stack([te[j] * roots[j] for j in range(8)])
    return jnp.concatenate(d, axis=0), jnp.concatenate(e, axis=0)


def factor_kernel(scale, sections, parts_ref, omega_ref, s_ref, factor_ref, inverse_ref, g):
    analysis = lax.axis_index("sec") == sections - 1

    @pl.when(analysis)
    def _():
        factorize(scale, parts_ref, omega_ref, s_ref, factor_ref, inverse_ref, g)

    @pl.when(jnp.logical_not(analysis))
    def _():
        factor_ref[...] = jnp.zeros(factor_ref.shape, jnp.float32)


def factorize(scale, parts_ref, omega_ref, s_ref, factor_ref, inverse_ref, g):
    rank = s_ref.shape[0]
    snaps = omega_ref.shape[0]
    strips = rank // LANES
    rows_first = (((0,), (0,)), ((), ()))

    def band(r, c):
        return parts_ref[r * (strips + 1) + c]

    cross = jnp.concatenate(
        [
            jnp.concatenate([band(r, c) for c in range(strips)], axis=1)
            for r in range(snaps // 8)
        ],
        axis=0,
    )
    inner = jnp.concatenate([band(r, strips) for r in range(snaps // 8)], axis=0)
    omega = omega_ref[...]
    half = cross + 0.5 * jnp.dot(
        inner[:, :snaps], omega, precision=highest, preferred_element_type=jnp.float32
    )
    left = jnp.concatenate([half, omega], axis=0)
    right = jnp.concatenate([omega, half], axis=0)
    g[...] = s_ref[...] + lax.dot_general(
        left, right, rows_first, precision=highest, preferred_element_type=jnp.float32
    )
    inverse_ref[...] = jnp.zeros(inverse_ref.shape, jnp.float32)
    factor_ref[...] = jnp.zeros(factor_ref.shape, jnp.float32)
    sub = lax.broadcasted_iota(jnp.int32, (8, LANES), 0)
    lane = lax.broadcasted_iota(jnp.int32, (8, LANES), 1)
    tiles = LANES // 8

    def block(k, carry):
        start = pl.multiple_of(k * LANES, LANES)
        d = [g[pl.ds(start + 8 * i, 8), pl.ds(start, LANES)] for i in range(tiles)]
        e = [jnp.where(lane == sub + 8 * i, 1.0, 0.0) for i in range(tiles)]
        upper, small = factor_block(d, e, sub, lane)
        factor_ref[pl.ds(start, LANES), pl.ds(start, LANES)] = upper
        inverse_ref[pl.ds(start, LANES), pl.ds(start, LANES)] = small
        for at in range(strips):

            @pl.when(k == at)
            def _(at=at):
                rows = slice(at * LANES, (at + 1) * LANES)
                right, left = slice((at + 1) * LANES, rank), slice(0, at * LANES)
                ahead = rank - (at + 1) * LANES
                pieces = [g[rows, right]] if ahead else []
                pieces += [inverse_ref[rows, left]] if at else []
                panel = jnp.dot(
                    small,
                    jnp.concatenate(pieces, axis=1),
                    precision=highest,
                    preferred_element_type=jnp.float32,
                )
                if at:
                    inverse_ref[rows, left] = panel[:, ahead:]
                if ahead:
                    fresh = panel[:, :ahead]
                    factor_ref[rows, right] = fresh
                    change = lax.dot_general(
                        fresh,
                        jnp.concatenate([panel, small], axis=1),
                        rows_first,
                        precision=highest,
                        preferred_element_type=jnp.float32,
                    )
                    g[right, right] = g[right, right] - change[:, :ahead]
                    done = slice(0, (at + 1) * LANES)
                    inverse_ref[right, done] = inverse_ref[right, done] - change[:, ahead:]

        return carry

    lax.fori_loop(0, strips, block, 0)
    factor_ref[...] = factor_ref[...] * (1.0 / scale)
    inverse_ref[...] = (inverse_ref[...] * scale).T


def basis_kernel(sections, inverse_ref, omega_ref, s_ref, *rest):
    pieces, out_ref = rest[:-1], rest[-1]
    analysis = lax.axis_index("sec") == sections - 1

    @pl.when(analysis)
    def _():
        def split(x):
            high = x.astype(jnp.bfloat16)
            return high, (x - high.astype(jnp.float32)).astype(jnp.bfloat16)

        dot = functools.partial(jnp.dot, preferred_element_type=jnp.float32)
        inverse = inverse_ref[...]
        mixed = jnp.dot(
            omega_ref[...], inverse, precision=highest, preferred_element_type=jnp.float32
        )
        x1, x2 = split(inverse)
        m1, m2 = split(jnp.concatenate([mixed, mixed], axis=0))
        rows = 512

        def strip(i, carry):
            at = pl.ds(pl.multiple_of(i * rows, rows), rows)
            s = s_ref[at, :]
            w = pieces[0][at, :]
            for piece in pieces[1:]:
                w = w + piece[at, :]
            w = w.astype(jnp.bfloat16)
            q = (dot(s, x1) + dot(s, x2)) + (dot(w, m1) + dot(w, m2))
            out_ref[at, :] = q.astype(jnp.bfloat16)
            return carry

        lax.fori_loop(0, s_ref.shape[0] // rows, strip, 0)

    @pl.when(jnp.logical_not(analysis))
    def _():
        out_ref[...] = jnp.zeros(out_ref.shape, jnp.bfloat16)


def shards(potential, previous, wave_coeff, sketch_in, omega, blocks, owners):
    sections = lax.axis_size("sec")
    columns = lax.axis_size("dev")
    devices = sections * columns
    extent_x, extent_y, depth = potential.shape
    list_width = owners.shape[1]
    per_device = list_width // (sections - 1)
    snaps, rank = omega.shape
    slab = max(8, depth // columns)
    per_slab = slab * columns // depth
    slots = columns * CAP
    order = neighbour_path(columns)
    path = []
    for section in range(sections - 1):
        path += [section * columns + d for d in (order if section % 2 == 0 else order[::-1])]
    up = [(path[i], path[i + per_slab]) for i in range(len(path) - per_slab)]
    down = [(b, a) for a, b in up]
    f32 = jnp.float32

    analysis = lax.axis_index("sec") == sections - 1

    def whole_gram():
        own = lax.dot_general(
            sketch_in, sketch_in, (((0,), (0,)), ((), ())), preferred_element_type=f32
        )
        own = own.reshape(columns, rank // columns, rank)
        own = lax.all_to_all(own, "dev", split_axis=0, concat_axis=0, tiled=True)
        own = jnp.broadcast_to(jnp.sum(own, axis=0)[None], own.shape)
        own = lax.all_to_all(own, "dev", split_axis=0, concat_axis=0, tiled=True)
        return own.reshape(rank, rank)

    scaled = omega * jnp.asarray(
        decay ** np.arange(1, snaps + 1, dtype=np.float64), f32
    )[:, None]

    lists = jnp.pad(
        jnp.concatenate([blocks, owners], axis=1).astype(f32), ((0, 0), (0, LANES - 2 * list_width))
    )
    chunk = 6 * slab + 8
    operands = (potential, previous, wave_coeff, lists)
    outgoing = pl.pallas_call(
        functools.partial(split_kernel, order, slab, per_slab),
        out_shape=jax.ShapeDtypeStruct((columns, chunk, LANES), f32),
        in_specs=vmem(*operands),
        out_specs=pl.BlockSpec(memory_space=pltpu.VMEM),
        scratch_shapes=[pltpu.VMEM((6, depth, LANES), f32)],
        compiler_params=big(),
    )(*operands)
    raw = lax.all_to_all(outgoing, "dev", split_axis=0, concat_axis=0, tiled=True)
    gram, scaled, raw = lax.optimization_barrier(
        (lax.cond(analysis, whole_gram, lambda: jnp.zeros((rank, rank), f32)), scaled, raw)
    )
    table = raw[:, 6 * slab, : 2 * list_width].astype(jnp.int32)

    def sides(x):
        return lax.ppermute(x, BOTH, up), x, lax.ppermute(x, BOTH, down)

    fields = sides(raw)
    state = fields
    held = jnp.zeros((columns * per_device, 8, LANES), f32)
    rounds = snaps // slab
    for number in range(rounds):
        last = number == rounds - 1
        operands = (table, *fields, *state, held)
        result = (columns, slots, 8, LANES) if last else (columns, 4 * slab, LANES)
        moved, held = pl.pallas_call(
            functools.partial(
                steps_kernel, number * slab, slab, per_device, last, snaps, sections
            ),
            out_shape=(
                jax.ShapeDtypeStruct(result, f32),
                jax.ShapeDtypeStruct(held.shape, f32),
            ),
            in_specs=[pl.BlockSpec(memory_space=pltpu.SMEM)] + vmem(*operands[1:]),
            out_specs=tuple(vmem(0, 0)),
            scratch_shapes=[pltpu.VMEM((2 * columns, 3 * slab + 16, LANES), f32)] * 2
            + [pltpu.VMEM((2 * columns, 3 * slab, LANES), f32)] * 2,
            compiler_params=big(),
        )(*operands)
        if not last:
            state = sides(moved)
    arrived = lax.all_to_all(moved, "dev", split_axis=0, concat_axis=0, tiled=True)

    operands = (arrived, sketch_in)
    bands = (snaps // 8) * (rank // LANES + 1)
    share = -(-bands // columns)
    parts, wide = pl.pallas_call(
        functools.partial(product_kernel, order, slab, per_slab, snaps, sections),
        out_shape=(
            jax.ShapeDtypeStruct((columns, share, 8, LANES), f32),
            jax.ShapeDtypeStruct((slots * depth, LANES), f32),
        ),
        in_specs=vmem(*operands),
        out_specs=tuple(vmem(0, 0)),
        scratch_shapes=[pltpu.VMEM((slots * depth, LANES), f32)],
        compiler_params=big(60),
    )(*operands)

    def to_analysis(x):
        return [lax.ppermute(x, "sec", [(i, sections - 1)]) for i in range(sections - 1)]

    terms = lax.all_to_all(parts, "dev", split_axis=0, concat_axis=0, tiled=True)
    terms = to_analysis(jnp.sum(terms, axis=0))
    hop = lax.ppermute(wide, "sec", [(i, i + 1) for i in range(0, sections - 1, 2)])
    merged, terms = lax.optimization_barrier((wide + hop, terms))
    pieces = [hop]
    pieces += [lax.ppermute(merged, "sec", [(i, sections - 1)]) for i in range(1, sections - 1, 2)]

    def exchange(terms):
        total = jnp.broadcast_to(sum(terms[1:], terms[0])[None], parts.shape)
        return lax.all_to_all(total, "dev", split_axis=0, concat_axis=0, tiled=True)

    sums = lax.cond(analysis, exchange, lambda terms: jnp.zeros(parts.shape, f32), terms)
    sums = sums.reshape(columns * share, 8, LANES)

    scale = math.sqrt(columns * columns * CAP * depth)
    operands = (sums, scaled, gram)
    factor, inverse = pl.pallas_call(
        functools.partial(factor_kernel, scale, sections),
        out_shape=(jax.ShapeDtypeStruct((rank, rank), f32),) * 2,
        in_specs=vmem(*operands),
        out_specs=tuple(vmem(0, 0)),
        scratch_shapes=[pltpu.VMEM((rank, rank), f32)],
        compiler_params=big(),
    )(*operands)
    operands = (inverse, scaled, sketch_in, *pieces)
    basis = pl.pallas_call(
        functools.partial(basis_kernel, sections),
        out_shape=jax.ShapeDtypeStruct(sketch_in.shape, jnp.bfloat16),
        in_specs=vmem(*operands),
        out_specs=pl.BlockSpec(memory_space=pltpu.VMEM),
        compiler_params=big(60),
    )(*operands)
    return (basis[None], factor[None])


def solution(mesh):
    placed = (
        P("dev", None, "sec"),
        P("dev", None, "sec"),
        P("dev", None, "sec"),
        P("dev", None),
        P(),
        P("dev", None),
        P("dev", None),
    )
    return jax.shard_map(
        shards,
        mesh=mesh,
        in_specs=placed,
        out_specs=(P("sec", "dev", None), P("sec", None, None)),
        check_vma=False,
    )
```

```python
import functools
import math

import jax
import jax.numpy as jnp
import numpy as np
from jax import lax
from jax.experimental import pallas as pl
from jax.experimental.pallas import tpu as pltpu
from jax.sharding import PartitionSpec as P

CAP = 2
damping = 0.05
LANES = 128
highest = lax.Precision.HIGHEST
decay = math.sqrt(1.0 - damping)
BOTH = ("sec", "dev")


def neighbour_path(columns):
    order = []
    for i in range(0, columns, 2):
        pair = [i, i + 1]
        order += pair if (i // 2) % 2 == 0 else pair[::-1]
    return order


def vmem(*arrays):
    return [pl.BlockSpec(memory_space=pltpu.VMEM)] * len(arrays)


def big(limit=48):
    return pltpu.CompilerParams(vmem_limit_bytes=limit << 20)


def slab_of(order, column, section, per_slab):
    place = order.index(column)
    forward, backward = place // per_slab, (len(order) - 1 - place) // per_slab
    return jnp.where(section % 2 == 0, forward, backward)


def split_kernel(order, slab, per_slab, u_ref, e_ref, k_ref, table_ref, out_ref, turned):
    section = lax.axis_index("sec")
    extent_x, extent_y, depth = u_ref.shape
    for a, ref in enumerate((u_ref, e_ref, k_ref)):
        for p in range(2):
            rows = jnp.concatenate([ref[x] for x in range(p, extent_x, 2)], axis=0)
            if a == 1:
                rows = rows * decay
            turned[2 * a + p] = rows.T
    for column in range(len(order)):
        at = slab_of(order, column, section, per_slab)
        start = pl.multiple_of(at * slab, 8)
        for q in range(6):
            out_ref[column, q * slab : (q + 1) * slab, :] = turned[q, pl.ds(start, slab), :]
        out_ref[column, 6 * slab :, :] = jnp.broadcast_to(table_ref[...], (8, LANES))


def steps_kernel(*args):
    sections = args[5]

    @pl.when(lax.axis_index("sec") < sections - 1)
    def _():
        evolve(*args)


def evolve(
    first_step, slab, per_device, last, snaps, sections,
    table, kl, kc, kr, sl, sc, sr, w_in, *rest,
):
    if last:
        send_ref, w_ref, field_a, field_b, gain, own = rest
    else:
        state_ref, w_ref, field_a, field_b, gain, own = rest
    list_start = lax.axis_index("sec") * per_device
    columns = kc.shape[0]
    rows = 3 * slab
    lane = lax.broadcasted_iota(jnp.int32, (8, LANES), 1)
    y_first, y_last = lane % 32 == 0, lane % 32 == 31
    zero = jnp.zeros((8, LANES), jnp.float32)

    for o in range(2 * columns):
        d, p = o // 2, o % 2
        for field, at in ((field_a, p), (field_b, 2 + p)):
            field[o, 0:8, :] = zero
            field[o, 8 + rows : 16 + rows, :] = zero
            for h, ref in enumerate((sl, sc, sr)):
                field[o, 8 + h * slab : 8 + (h + 1) * slab, :] = ref[
                    d, at * slab : (at + 1) * slab, :
                ]
        for h, ref in enumerate((kl, kc, kr)):
            k = ref[d, (4 + p) * slab : (5 + p) * slab, :]
            gain[o, h * slab : (h + 1) * slab, :] = k * (1.0 / decay)
            own[o, h * slab : (h + 1) * slab, :] = ((2.0 - damping) - 6.0 * k) * (1.0 / decay)
    w_ref[...] = w_in[...]

    def step(src, dst, tiles, number):
        for z in tiles:
            at = slice(8 + 8 * z, 16 + 8 * z)
            low = slice(7 + 8 * z, 15 + 8 * z)
            high = slice(9 + 8 * z, 17 + 8 * z)
            here = slice(8 * z, 8 * z + 8)
            values = [src[o, at, :] for o in range(2 * columns)]
            up = [pltpu.roll(values[2 * d + 1], 32, 1) for d in range(columns)]
            down = [pltpu.roll(values[2 * d], LANES - 32, 1) for d in range(columns)]
            for o in range(2 * columns):
                d, p = o // 2, o % 2
                v = values[o]
                if p == 0:
                    side = jnp.where(lane < 32, up[d - 1] if d > 0 else zero, up[d])
                    total = values[o + 1] + side
                else:
                    side = jnp.where(
                        lane >= LANES - 32, down[d + 1] if d + 1 < columns else zero, down[d]
                    )
                    total = values[o - 1] + side
                total = total + (src[o, low, :] + src[o, high, :])
                total = total + jnp.where(y_first, 0.0, pltpu.roll(v, 1, 1))
                total = total + jnp.where(y_last, 0.0, pltpu.roll(v, LANES - 1, 1))
                dst[o, at, :] = own[o, here, :] * v + gain[o, here, :] * total - dst[o, at, :]

        def column_blocks(d, carry):
            for i in range(per_device):
                block = table[d, list_start + i]
                x, y = block >> 5, block & 31
                at_lane = ((x >> 1) << 5) + y
                o = 2 * d + (x & 1)
                j = d * per_device + i
                held = w_ref[j]
                for h in range(slab // 8):
                    target = h * snaps + number
                    value = dst[o, 8 + slab + 8 * h : 16 + slab + 8 * h, :]
                    moved = pltpu.roll(value, (target - at_lane) & (LANES - 1), 1)
                    held = jnp.where(lane == target, moved, held)
                w_ref[j] = held
            return carry

        lax.fori_loop(0, columns, column_blocks, 0, unroll=min(columns, 8))

    for phase in range(slab // 8):
        tiles = range(phase, 3 * slab // 8 - phase)

        def pair(m, carry):
            number = first_step + 8 * phase + 2 * m
            step(field_a, field_b, tiles, number)
            step(field_b, field_a, tiles, number + 1)
            return carry

        lax.fori_loop(0, 4, pair, 0)

    if last:
        send_ref[...] = jnp.zeros(send_ref.shape, jnp.float32)
        width = per_device * (sections - 1)

        def place(d, carry):
            for i in range(per_device):
                mine = table[d, width + list_start + i]

                def earlier(n, c):
                    return c + jnp.where(table[d, width + n] == mine, 1, 0)

                count = lax.fori_loop(0, list_start + i, earlier, 0)
                send_ref[mine, d * CAP + count] = w_ref[d * per_device + i]
            return carry

        lax.fori_loop(0, columns, place, 0)
    else:
        for o in range(2 * columns):
            d, p = o // 2, o % 2
            state_ref[d, p * slab : (p + 1) * slab, :] = field_a[o, 8 + slab : 8 + 2 * slab, :]
            state_ref[d, (2 + p) * slab : (3 + p) * slab, :] = field_b[
                o, 8 + slab : 8 + 2 * slab, :
            ]


def unpack(tile, h, snaps, lane):
    if h:
        tile = pltpu.roll(tile, LANES - h * snaps, 1)
    return jnp.where(lane < snaps, tile, 0.0)


def product_kernel(*args):
    sections = args[4]

    @pl.when(lax.axis_index("sec") < sections - 1)
    def _():
        products(*args)


def products(order, slab, per_slab, snaps, sections, w_ref, s_ref, out_ref, wide, low):
    section = lax.axis_index("sec")
    slots = w_ref.shape[1]
    halves = slab // 8
    lane = lax.broadcasted_iota(jnp.int32, (8, LANES), 1)
    for column in range(0, len(order)):
        if order.index(column) % per_slab:
            continue
        at = slab_of(order, column, section, per_slab)
        for q in range(slots):
            tile = w_ref[column, q]
            for h in range(halves):
                w = unpack(tile, h, snaps, lane)
                w1 = w.astype(jnp.bfloat16).astype(jnp.float32)
                w2 = (w - w1).astype(jnp.bfloat16).astype(jnp.float32)
                w3 = w - w1 - w2
                start = pl.multiple_of(q * LANES + at * slab + 8 * h, 8)
                wide[pl.ds(start, 8), :] = w1 + pltpu.roll(w2, snaps, 1)
                low[pl.ds(start, 8), :] = w3
    both = wide[...].astype(jnp.bfloat16)
    tail = low[...].astype(jnp.bfloat16)
    rows = (((0,), (0,)), ((), ()))
    dot = functools.partial(
        lax.dot_general, dimension_numbers=rows, preferred_element_type=jnp.float32
    )
    sketch = s_ref[...]
    a_first = dot(both, sketch)
    a_tail = dot(tail, sketch)
    cross = a_first[:snaps] + (a_first[snaps:] + a_tail[:snaps])
    c_first = dot(both, both)
    c_tail = dot(tail, both)[:snaps, :]
    c_tail = jnp.where(lax.broadcasted_iota(jnp.int32, c_tail.shape, 1) < snaps, c_tail, 0.0)
    half = c_first[:snaps, :] + c_first[snaps:, :]
    own = half + pltpu.roll(half, snaps, 1)
    square = jnp.concatenate([c_tail, jnp.zeros_like(c_tail)], axis=0).T[:snaps, :]
    inner = jnp.where(
        lax.broadcasted_iota(jnp.int32, own.shape, 1) < snaps, own, 0.0
    ) + (c_tail + square)
    strips = cross.shape[1] // LANES
    share = out_ref.shape[1]
    for r in range(snaps // 8):
        here = slice(8 * r, 8 * r + 8)
        for c in range(strips):
            at = r * (strips + 1) + c
            out_ref[at // share, at % share] = cross[here, c * LANES : (c + 1) * LANES]
        at = r * (strips + 1) + strips
        out_ref[at // share, at % share] = inner[here, :]


def three(x):
    x1 = x.astype(jnp.bfloat16)
    rest = x - x1.astype(jnp.float32)
    x2 = rest.astype(jnp.bfloat16)
    return x1, x2, (rest - x2.astype(jnp.float32)).astype(jnp.bfloat16)


def reciprocal(x):
    guess = pl.reciprocal(x, approx=True)
    return guess * (2.0 - x * guess)


def factor_block(d, e, sub, lane, spread):
    tiles = len(d)

    def wide(x):
        return jnp.broadcast_to(x, (8, LANES))

    def stack(values):
        out = values[0]
        for j in range(1, 8):
            out = jnp.where(sub == j, values[j], out)
        return out

    for p in range(tiles):
        first = 8 * p
        cols = [wide(d[p][:, first + j : first + j + 1]) for j in range(8)]
        base = 80 * (p % 2)
        for k, value in enumerate(cols + [d[p], e[p]]):
            spread[base + 8 * k : base + 8 * k + 8, :] = value

        def row(k, j, base=base):
            return spread[pl.ds(base + 8 * k + j, 8, stride=0), :]

        s = [[row(k, j) if k >= j else None for k in range(8)] for j in range(8)]
        t = [row(8, j) for j in range(8)]
        te = [row(9, j) for j in range(8)]
        inv, m = [], [[None] * 8 for _ in range(8)]
        for j in range(0, 8, 2):
            n = j + 1
            a, b, c = s[j][j], s[j][n], s[n][n]
            det = a * c - b * b
            inv_a, inv_det = reciprocal(a), reciprocal(det)
            inv += [inv_a, a * inv_det]
            m[j][n] = b * inv_a
            s[n][n] = det * inv_a
            t[n] = t[n] - m[j][n] * t[j]
            te[n] = te[n] - m[j][n] * te[j]
            for k in range(j + 2, 8):
                m[j][k] = s[j][k] * inv_a
                m[n][k] = (a * s[n][k] - b * s[j][k]) * inv_det
                s[n][k] = s[n][k] - m[j][n] * s[j][k]
            for k in range(j + 2, 8):
                for i in range(k, 8):
                    s[k][i] = (s[k][i] - m[j][k] * s[j][i]) - m[n][k] * s[n][i]
                t[k] = (t[k] - m[j][k] * t[j]) - m[n][k] * t[n]
                te[k] = (te[k] - m[j][k] * te[j]) - m[n][k] * te[n]
        if p + 1 < tiles:
            z, ze = [None] * 8, [None] * 8
            for j in reversed(range(8)):
                z[j], ze[j] = t[j] * inv[j], te[j] * inv[j]
                for k in range(j + 1, 8):
                    z[j] = z[j] - m[j][k] * z[k]
                    ze[j] = ze[j] - m[j][k] * ze[k]
            i = p + 1
            parts, parts_e = [], []
            for j in range(8):
                col = wide(d[i][:, first + j : first + j + 1])
                parts.append(col * z[j])
                parts_e.append(col * ze[j])
            while len(parts) > 1:
                parts = [x + y for x, y in zip(parts[::2], parts[1::2])]
                parts_e = [x + y for x, y in zip(parts_e[::2], parts_e[1::2])]
            if p + 2 < tiles:
                p1, p2, p3 = three(d[p])
                z1, z2, z3 = three(jnp.concatenate([stack(z), stack(ze)], axis=1))
                change = lax.dot_general(
                    jnp.concatenate([p1, p1, p1, p2, p2, p3], axis=0),
                    jnp.concatenate([z1, z2, z3, z1, z2, z1], axis=0),
                    (((0,), (0,)), ((), ())),
                    preferred_element_type=jnp.float32,
                )
                for n in range(p + 2, tiles):
                    d[n] = d[n] - change[8 * n : 8 * n + 8, :LANES]
                    e[n] = e[n] - change[8 * n : 8 * n + 8, LANES:]
            d[i], e[i] = d[i] - parts[0], e[i] - parts_e[0]
        roots = [lax.rsqrt(s[j][j]) for j in range(8)]
        d[p] = jnp.where(lane >= sub + first, stack([t[j] * roots[j] for j in range(8)]), 0.0)
        e[p] = stack([te[j] * roots[j] for j in range(8)])
    return jnp.concatenate(d, axis=0), jnp.concatenate(e, axis=0)


def factor_kernel(scale, sections, parts_ref, omega_ref, s_ref, factor_ref, inverse_ref, g, spread):
    analysis = lax.axis_index("sec") == sections - 1

    @pl.when(analysis)
    def _():
        factorize(scale, parts_ref, omega_ref, s_ref, factor_ref, inverse_ref, g, spread)

    @pl.when(jnp.logical_not(analysis))
    def _():
        factor_ref[...] = jnp.zeros(factor_ref.shape, jnp.float32)


def factorize(scale, parts_ref, omega_ref, s_ref, factor_ref, inverse_ref, g, spread):
    rank = s_ref.shape[0]
    snaps = omega_ref.shape[0]
    strips = rank // LANES
    rows_first = (((0,), (0,)), ((), ()))

    def band(r, c):
        return parts_ref[r * (strips + 1) + c]

    cross = jnp.concatenate(
        [
            jnp.concatenate([band(r, c) for c in range(strips)], axis=1)
            for r in range(snaps // 8)
        ],
        axis=0,
    )
    inner = jnp.concatenate([band(r, strips) for r in range(snaps // 8)], axis=0)
    omega = omega_ref[...]
    half = cross + 0.5 * jnp.dot(
        inner[:, :snaps], omega, precision=highest, preferred_element_type=jnp.float32
    )
    left = jnp.concatenate([half, omega], axis=0)
    right = jnp.concatenate([omega, half], axis=0)
    g[...] = s_ref[...] + lax.dot_general(
        left, right, rows_first, precision=highest, preferred_element_type=jnp.float32
    )
    inverse_ref[...] = jnp.zeros(inverse_ref.shape, jnp.float32)
    factor_ref[...] = jnp.zeros(factor_ref.shape, jnp.float32)
    sub = lax.broadcasted_iota(jnp.int32, (8, LANES), 0)
    lane = lax.broadcasted_iota(jnp.int32, (8, LANES), 1)
    tiles = LANES // 8

    def block(k, carry):
        start = pl.multiple_of(k * LANES, LANES)
        d = [g[pl.ds(start + 8 * i, 8), pl.ds(start, LANES)] for i in range(tiles)]
        e = [jnp.where(lane == sub + 8 * i, 1.0, 0.0) for i in range(tiles)]
        upper, small = factor_block(d, e, sub, lane, spread)
        factor_ref[pl.ds(start, LANES), pl.ds(start, LANES)] = upper
        inverse_ref[pl.ds(start, LANES), pl.ds(start, LANES)] = small
        for at in range(strips):

            @pl.when(k == at)
            def _(at=at):
                rows = slice(at * LANES, (at + 1) * LANES)
                right, left = slice((at + 1) * LANES, rank), slice(0, at * LANES)
                ahead = rank - (at + 1) * LANES
                pieces = [g[rows, right]] if ahead else []
                pieces += [inverse_ref[rows, left]] if at else []
                panel = jnp.dot(
                    small,
                    jnp.concatenate(pieces, axis=1),
                    precision=highest,
                    preferred_element_type=jnp.float32,
                )
                if at:
                    inverse_ref[rows, left] = panel[:, ahead:]
                if ahead:
                    fresh = panel[:, :ahead]
                    factor_ref[rows, right] = fresh
                    change = lax.dot_general(
                        fresh,
                        jnp.concatenate([panel, small], axis=1),
                        rows_first,
                        precision=highest,
                        preferred_element_type=jnp.float32,
                    )
                    g[right, right] = g[right, right] - change[:, :ahead]
                    done = slice(0, (at + 1) * LANES)
                    inverse_ref[right, done] = inverse_ref[right, done] - change[:, ahead:]

        return carry

    lax.fori_loop(0, strips, block, 0)
    factor_ref[...] = factor_ref[...] * (1.0 / scale)
    inverse_ref[...] = (inverse_ref[...] * scale).T


def basis_kernel(sections, inverse_ref, omega_ref, s_ref, *rest):
    pieces, out_ref = rest[:-1], rest[-1]
    analysis = lax.axis_index("sec") == sections - 1

    @pl.when(analysis)
    def _():
        def split(x):
            high = x.astype(jnp.bfloat16)
            return high, (x - high.astype(jnp.float32)).astype(jnp.bfloat16)

        dot = functools.partial(jnp.dot, preferred_element_type=jnp.float32)
        inverse = inverse_ref[...]
        mixed = jnp.dot(
            omega_ref[...], inverse, precision=highest, preferred_element_type=jnp.float32
        )
        x1, x2 = split(inverse)
        m1, m2 = split(jnp.concatenate([mixed, mixed], axis=0))
        stack = jnp.concatenate([x1, x2, m1, m2], axis=0)
        rows = 1024

        def strip(i, carry):
            at = pl.ds(pl.multiple_of(i * rows, rows), rows)
            s = s_ref[at, :]
            w = pieces[0][at, :]
            for piece in pieces[1:]:
                w = w + piece[at, :]
            w = w.astype(jnp.bfloat16)
            q = dot(jnp.concatenate([s, s, w, w], axis=1), stack)
            out_ref[at, :] = q.astype(jnp.bfloat16)
            return carry

        lax.fori_loop(0, s_ref.shape[0] // rows, strip, 0)

    @pl.when(jnp.logical_not(analysis))
    def _():
        out_ref[...] = jnp.zeros(out_ref.shape, jnp.bfloat16)


def shards(potential, previous, wave_coeff, sketch_in, omega, blocks, owners):
    sections = lax.axis_size("sec")
    columns = lax.axis_size("dev")
    devices = sections * columns
    extent_x, extent_y, depth = potential.shape
    list_width = owners.shape[1]
    per_device = list_width // (sections - 1)
    snaps, rank = omega.shape
    slab = max(8, depth // columns)
    per_slab = slab * columns // depth
    slots = columns * CAP
    order = neighbour_path(columns)
    path = []
    for section in range(sections - 1):
        path += [section * columns + d for d in (order if section % 2 == 0 else order[::-1])]
    up = [(path[i], path[i + per_slab]) for i in range(len(path) - per_slab)]
    down = [(b, a) for a, b in up]
    f32 = jnp.float32

    analysis = lax.axis_index("sec") == sections - 1

    def whole_gram():
        own = lax.dot_general(
            sketch_in, sketch_in, (((0,), (0,)), ((), ())), preferred_element_type=f32
        )
        own = own.reshape(columns, rank // columns, rank)
        own = lax.all_to_all(own, "dev", split_axis=0, concat_axis=0, tiled=True)
        own = jnp.broadcast_to(jnp.sum(own, axis=0)[None], own.shape)
        own = lax.all_to_all(own, "dev", split_axis=0, concat_axis=0, tiled=True)
        return own.reshape(rank, rank)

    scaled = omega * jnp.asarray(
        decay ** np.arange(1, snaps + 1, dtype=np.float64), f32
    )[:, None]

    lists = jnp.pad(
        jnp.concatenate([blocks, owners], axis=1).astype(f32), ((0, 0), (0, LANES - 2 * list_width))
    )
    chunk = 6 * slab + 8
    operands = (potential, previous, wave_coeff, lists)
    outgoing = pl.pallas_call(
        functools.partial(split_kernel, order, slab, per_slab),
        out_shape=jax.ShapeDtypeStruct((columns, chunk, LANES), f32),
        in_specs=vmem(*operands),
        out_specs=pl.BlockSpec(memory_space=pltpu.VMEM),
        scratch_shapes=[pltpu.VMEM((6, depth, LANES), f32)],
        compiler_params=big(),
    )(*operands)
    raw = lax.all_to_all(outgoing, "dev", split_axis=0, concat_axis=0, tiled=True)
    gram, scaled, raw = lax.optimization_barrier(
        (lax.cond(analysis, whole_gram, lambda: jnp.zeros((rank, rank), f32)), scaled, raw)
    )
    table = raw[:, 6 * slab, : 2 * list_width].astype(jnp.int32)

    def sides(x):
        return lax.ppermute(x, BOTH, up), x, lax.ppermute(x, BOTH, down)

    fields = sides(raw)
    state = fields
    held = jnp.zeros((columns * per_device, 8, LANES), f32)
    rounds = snaps // slab
    for number in range(rounds):
        last = number == rounds - 1
        operands = (table, *fields, *state, held)
        result = (columns, slots, 8, LANES) if last else (columns, 4 * slab, LANES)
        moved, held = pl.pallas_call(
            functools.partial(
                steps_kernel, number * slab, slab, per_device, last, snaps, sections
            ),
            out_shape=(
                jax.ShapeDtypeStruct(result, f32),
                jax.ShapeDtypeStruct(held.shape, f32),
            ),
            in_specs=[pl.BlockSpec(memory_space=pltpu.SMEM)] + vmem(*operands[1:]),
            out_specs=tuple(vmem(0, 0)),
            scratch_shapes=[pltpu.VMEM((2 * columns, 3 * slab + 16, LANES), f32)] * 2
            + [pltpu.VMEM((2 * columns, 3 * slab, LANES), f32)] * 2,
            compiler_params=big(),
        )(*operands)
        if not last:
            state = sides(moved)
    arrived = lax.all_to_all(moved, "dev", split_axis=0, concat_axis=0, tiled=True)

    operands = (arrived, sketch_in)
    bands = (snaps // 8) * (rank // LANES + 1)
    share = -(-bands // columns)
    parts, wide = pl.pallas_call(
        functools.partial(product_kernel, order, slab, per_slab, snaps, sections),
        out_shape=(
            jax.ShapeDtypeStruct((columns, share, 8, LANES), f32),
            jax.ShapeDtypeStruct((slots * depth, LANES), f32),
        ),
        in_specs=vmem(*operands),
        out_specs=tuple(vmem(0, 0)),
        scratch_shapes=[pltpu.VMEM((slots * depth, LANES), f32)],
        compiler_params=big(60),
    )(*operands)

    def to_analysis(x):
        return [lax.ppermute(x, "sec", [(i, sections - 1)]) for i in range(sections - 1)]

    terms = lax.all_to_all(parts, "dev", split_axis=0, concat_axis=0, tiled=True)
    total = jnp.sum(terms, axis=0)
    terms = to_analysis(total)
    wide, *terms = lax.optimization_barrier((wide, *terms))
    pieces = to_analysis(wide)

    def exchange(terms):
        total = jnp.broadcast_to(sum(terms[1:], terms[0])[None], parts.shape)
        return lax.all_to_all(total, "dev", split_axis=0, concat_axis=0, tiled=True)

    sums = lax.cond(analysis, exchange, lambda terms: jnp.zeros(parts.shape, f32), terms)
    sums = sums.reshape(columns * share, 8, LANES)

    scale = math.sqrt(columns * columns * CAP * depth)
    operands = (sums, scaled, gram)
    factor, inverse = pl.pallas_call(
        functools.partial(factor_kernel, scale, sections),
        out_shape=(jax.ShapeDtypeStruct((rank, rank), f32),) * 2,
        in_specs=vmem(*operands),
        out_specs=tuple(vmem(0, 0)),
        scratch_shapes=[pltpu.VMEM((rank, rank), f32), pltpu.VMEM((160, LANES), f32)],
        compiler_params=big(),
    )(*operands)
    operands = (inverse, scaled, sketch_in, *pieces)
    basis = pl.pallas_call(
        functools.partial(basis_kernel, sections),
        out_shape=jax.ShapeDtypeStruct(sketch_in.shape, jnp.bfloat16),
        in_specs=vmem(*operands),
        out_specs=pl.BlockSpec(memory_space=pltpu.VMEM),
        compiler_params=big(60),
    )(*operands)
    return (basis[None], factor[None])


def solution(mesh):
    placed = (
        P("dev", None, "sec"),
        P("dev", None, "sec"),
        P("dev", None, "sec"),
        P("dev", None),
        P(),
        P("dev", None),
        P("dev", None),
    )
    return jax.shard_map(
        shards,
        mesh=mesh,
        in_specs=placed,
        out_specs=(P("sec", "dev", None), P("sec", None, None)),
        check_vma=False,
    )
```

```python
import functools
import math

import jax
import jax.numpy as jnp
import numpy as np
from jax import lax
from jax.experimental import pallas as pl
from jax.experimental.pallas import tpu as pltpu
from jax.sharding import PartitionSpec as P

CAP = 2
damping = 0.05
LANES = 128
highest = lax.Precision.HIGHEST
decay = math.sqrt(1.0 - damping)
BOTH = ("sec", "dev")


def neighbour_path(columns):
    order = []
    for i in range(0, columns, 2):
        pair = [i, i + 1]
        order += pair if (i // 2) % 2 == 0 else pair[::-1]
    return order


def vmem(*arrays):
    return [pl.BlockSpec(memory_space=pltpu.VMEM)] * len(arrays)


def big(limit=48):
    return pltpu.CompilerParams(vmem_limit_bytes=limit << 20)


def slab_of(order, column, section, per_slab):
    place = order.index(column)
    forward, backward = place // per_slab, (len(order) - 1 - place) // per_slab
    return jnp.where(section % 2 == 0, forward, backward)


def split_kernel(order, slab, per_slab, u_ref, e_ref, k_ref, blocks_ref, owners_ref, out_ref, turned):
    section = lax.axis_index("sec")
    extent_x, extent_y, depth = u_ref.shape
    for a, ref in enumerate((u_ref, e_ref, k_ref)):
        for p in range(2):
            rows = jnp.concatenate([ref[x] for x in range(p, extent_x, 2)], axis=0)
            if a == 1:
                rows = rows * decay
            turned[2 * a + p] = rows.T
    for column in range(len(order)):
        at = slab_of(order, column, section, per_slab)
        start = pl.multiple_of(at * slab, 8)
        for q in range(6):
            out_ref[column, q * slab : (q + 1) * slab, :] = turned[q, pl.ds(start, slab), :]
        for r, ref in enumerate((blocks_ref, owners_ref)):
            out_ref[column, 6 * slab + r : 6 * slab + r + 1, : ref.shape[1]] = ref[...].astype(
                jnp.float32
            )


def steps_kernel(*args):
    last, sections = args[3], args[5]
    if last:
        flag_ref = args[16]
        flag_ref[0] = 0

    @pl.when(lax.axis_index("sec") < sections - 1)
    def _():
        evolve(*args)


def evolve(
    first_step, slab, per_device, last, snaps, sections,
    table, kl, kc, kr, sl, sc, sr, w_in, *rest,
):
    if last:
        send_ref, over_ref, flag_ref, w_ref, field_a, field_b, gain, own, used = rest
    else:
        state_ref, w_ref, field_a, field_b, gain, own = rest
    list_start = lax.axis_index("sec") * per_device
    columns = kc.shape[0]
    rows = 3 * slab
    lane = lax.broadcasted_iota(jnp.int32, (8, LANES), 1)
    y_first, y_last = lane % 32 == 0, lane % 32 == 31
    zero = jnp.zeros((8, LANES), jnp.float32)

    for o in range(2 * columns):
        d, p = o // 2, o % 2
        for field, at in ((field_a, p), (field_b, 2 + p)):
            field[o, 0:8, :] = zero
            field[o, 8 + rows : 16 + rows, :] = zero
            for h, ref in enumerate((sl, sc, sr)):
                field[o, 8 + h * slab : 8 + (h + 1) * slab, :] = ref[
                    d, at * slab : (at + 1) * slab, :
                ]
        for h, ref in enumerate((kl, kc, kr)):
            k = ref[d, (4 + p) * slab : (5 + p) * slab, :]
            gain[o, h * slab : (h + 1) * slab, :] = k * (1.0 / decay)
            own[o, h * slab : (h + 1) * slab, :] = ((2.0 - damping) - 6.0 * k) * (1.0 / decay)
    w_ref[...] = w_in[...]

    def step(src, dst, tiles, number):
        for z in tiles:
            at = slice(8 + 8 * z, 16 + 8 * z)
            low = slice(7 + 8 * z, 15 + 8 * z)
            high = slice(9 + 8 * z, 17 + 8 * z)
            here = slice(8 * z, 8 * z + 8)
            values = [src[o, at, :] for o in range(2 * columns)]
            up = [pltpu.roll(values[2 * d + 1], 32, 1) for d in range(columns)]
            down = [pltpu.roll(values[2 * d], LANES - 32, 1) for d in range(columns)]
            for o in range(2 * columns):
                d, p = o // 2, o % 2
                v = values[o]
                if p == 0:
                    side = jnp.where(lane < 32, up[d - 1] if d > 0 else zero, up[d])
                    total = values[o + 1] + side
                else:
                    side = jnp.where(
                        lane >= LANES - 32, down[d + 1] if d + 1 < columns else zero, down[d]
                    )
                    total = values[o - 1] + side
                total = total + (src[o, low, :] + src[o, high, :])
                total = total + jnp.where(y_first, 0.0, pltpu.roll(v, 1, 1))
                total = total + jnp.where(y_last, 0.0, pltpu.roll(v, LANES - 1, 1))
                dst[o, at, :] = own[o, here, :] * v + gain[o, here, :] * total - dst[o, at, :]

        def column_blocks(d, carry):
            for i in range(per_device):
                block = table[d, 0, list_start + i]
                x, y = block >> 5, block & 31
                at_lane = ((x >> 1) << 5) + y
                o = 2 * d + (x & 1)
                j = d * per_device + i
                held = w_ref[j]
                for h in range(slab // 8):
                    target = h * snaps + number
                    value = dst[o, 8 + slab + 8 * h : 16 + slab + 8 * h, :]
                    moved = pltpu.roll(value, (target - at_lane) & (LANES - 1), 1)
                    held = jnp.where(lane == target, moved, held)
                w_ref[j] = held
            return carry

        lax.fori_loop(0, columns, column_blocks, 0, unroll=min(columns, 8))

    for phase in range(slab // 8):
        tiles = range(phase, 3 * slab // 8 - phase)

        def pair(m, carry):
            number = first_step + 8 * phase + 2 * m
            step(field_a, field_b, tiles, number)
            step(field_b, field_a, tiles, number + 1)
            return carry

        lax.fori_loop(0, 4, pair, 0)

    if last:
        half = send_ref.shape[1]
        for d in range(columns):
            used[d] = 0

        def place(d, carry):
            for i in range(per_device):
                mine = table[d, 1, list_start + i]
                n = used[mine]
                used[mine] = n + 1

                @pl.when(n < half)
                def _(i=i, mine=mine, n=n):
                    send_ref[mine, n] = w_ref[d * per_device + i]

                @pl.when(n >= half)
                def _(i=i, mine=mine, n=n):
                    over_ref[mine, n - half] = w_ref[d * per_device + i]

            return carry

        lax.fori_loop(0, columns, place, 0)
        for d in range(columns):
            flag_ref[0] = jnp.maximum(flag_ref[0], jnp.where(used[d] > half, 1, 0))
    else:
        for o in range(2 * columns):
            d, p = o // 2, o % 2
            state_ref[d, p * slab : (p + 1) * slab, :] = field_a[o, 8 + slab : 8 + 2 * slab, :]
            state_ref[d, (2 + p) * slab : (3 + p) * slab, :] = field_b[
                o, 8 + slab : 8 + 2 * slab, :
            ]


def unpack(tile, h, snaps, lane):
    if h:
        tile = pltpu.roll(tile, LANES - h * snaps, 1)
    return jnp.where(lane < snaps, tile, 0.0)


def product_kernel(*args):
    sections = args[4]

    @pl.when(lax.axis_index("sec") < sections - 1)
    def _():
        products(*args)


def products(
    order, slab, per_slab, snaps, sections, table, w_ref, over_ref, s_ref, out_ref, wide
):
    section = lax.axis_index("sec")
    me = lax.axis_index("dev")
    columns = len(order)
    per_device = table.shape[2] // (sections - 1)
    list_start = section * per_device
    half = w_ref.shape[1]
    lane = lax.broadcasted_iota(jnp.int32, (8, LANES), 1)
    wide[...] = jnp.zeros(wide.shape, jnp.float32)

    def place(ref, n, slot):
        for column in range(columns):
            if order.index(column) % per_slab:
                continue
            at = slab_of(order, column, section, per_slab)
            tile = ref[column, n]
            for h in range(slab // 8):
                w = unpack(tile, h, snaps, lane)
                w1 = w.astype(jnp.bfloat16).astype(jnp.float32)
                w2 = (w - w1).astype(jnp.bfloat16).astype(jnp.float32)
                start = pl.multiple_of(slot * LANES + at * slab + 8 * h, 8)
                wide[pl.ds(start, 8), :] = w1 + pltpu.roll(w2, snaps, 1)

    def row(d, n):
        def earlier(m, c):
            return c + jnp.where(table[d, 1, m] == me, 1, 0)

        count = lax.fori_loop(0, list_start, earlier, 0)
        for i in range(per_device):
            mine = table[d, 1, list_start + i] == me
            slot = d * CAP + count

            @pl.when(jnp.logical_and(mine, n < half))
            def _(n=n, slot=slot):
                place(w_ref, n, slot)

            @pl.when(jnp.logical_and(mine, n >= half))
            def _(n=n, slot=slot):
                place(over_ref, n - half, slot)

            step = jnp.where(mine, 1, 0)
            n, count = n + step, count + step
        return n

    lax.fori_loop(0, columns, row, 0)
    both = wide[...].astype(jnp.bfloat16)
    dot = functools.partial(
        lax.dot_general,
        dimension_numbers=(((0,), (0,)), ((), ())),
        preferred_element_type=jnp.float32,
    )
    cross = dot(both, s_ref[...])
    cross = cross[:snaps] + cross[snaps:]
    inner = dot(both, both)
    inner = inner[:snaps, :] + inner[snaps:, :]
    inner = inner + pltpu.roll(inner, snaps, 1)
    strips = cross.shape[1] // LANES
    share = out_ref.shape[1]
    for r in range(snaps // 8):
        here = slice(8 * r, 8 * r + 8)
        for c in range(strips):
            at = r * (strips + 1) + c
            out_ref[at // share, at % share] = cross[here, c * LANES : (c + 1) * LANES]
        at = r * (strips + 1) + strips
        out_ref[at // share, at % share] = inner[here, :]


def three(x):
    x1 = x.astype(jnp.bfloat16)
    rest = x - x1.astype(jnp.float32)
    x2 = rest.astype(jnp.bfloat16)
    return x1, x2, (rest - x2.astype(jnp.float32)).astype(jnp.bfloat16)


def reciprocal(x):
    guess = pl.reciprocal(x, approx=True)
    return guess * (2.0 - x * guess)


def factor_block(d, e, sub, lane, spread):
    tiles = len(d)

    def wide(x):
        return jnp.broadcast_to(x, (8, LANES))

    def stack(values):
        out = values[0]
        for j in range(1, 8):
            out = jnp.where(sub == j, values[j], out)
        return out

    for p in range(tiles):
        first = 8 * p
        cols = [wide(d[p][:, first + j : first + j + 1]) for j in range(8)]
        base = 80 * (p % 2)
        for k, value in enumerate(cols + [d[p], e[p]]):
            spread[base + 8 * k : base + 8 * k + 8, :] = value

        def row(k, j, base=base):
            return spread[pl.ds(base + 8 * k + j, 8, stride=0), :]

        s = [[row(k, j) if k >= j else None for k in range(8)] for j in range(8)]
        t = [row(8, j) for j in range(8)]
        te = [row(9, j) for j in range(8)]
        inv, m = [], [[None] * 8 for _ in range(8)]
        for j in range(0, 8, 2):
            n = j + 1
            a, b, c = s[j][j], s[j][n], s[n][n]
            det = a * c - b * b
            inv_a, inv_det = reciprocal(a), reciprocal(det)
            inv += [inv_a, a * inv_det]
            m[j][n] = b * inv_a
            s[n][n] = det * inv_a
            t[n] = t[n] - m[j][n] * t[j]
            te[n] = te[n] - m[j][n] * te[j]
            for k in range(j + 2, 8):
                m[j][k] = s[j][k] * inv_a
                m[n][k] = (a * s[n][k] - b * s[j][k]) * inv_det
                s[n][k] = s[n][k] - m[j][n] * s[j][k]
            for k in range(j + 2, 8):
                for i in range(k, 8):
                    s[k][i] = (s[k][i] - m[j][k] * s[j][i]) - m[n][k] * s[n][i]
                t[k] = (t[k] - m[j][k] * t[j]) - m[n][k] * t[n]
                te[k] = (te[k] - m[j][k] * te[j]) - m[n][k] * te[n]
        if p + 1 < tiles:
            z, ze = [None] * 8, [None] * 8
            for j in reversed(range(8)):
                z[j], ze[j] = t[j] * inv[j], te[j] * inv[j]
                for k in range(j + 1, 8):
                    z[j] = z[j] - m[j][k] * z[k]
                    ze[j] = ze[j] - m[j][k] * ze[k]
            i = p + 1
            parts, parts_e = [], []
            for j in range(8):
                col = wide(d[i][:, first + j : first + j + 1])
                parts.append(col * z[j])
                parts_e.append(col * ze[j])
            while len(parts) > 1:
                parts = [x + y for x, y in zip(parts[::2], parts[1::2])]
                parts_e = [x + y for x, y in zip(parts_e[::2], parts_e[1::2])]
            if p + 2 < tiles:
                p1, p2, p3 = three(d[p])
                z1, z2, z3 = three(jnp.concatenate([stack(z), stack(ze)], axis=1))
                change = lax.dot_general(
                    jnp.concatenate([p1, p1, p1, p2, p2, p3], axis=0),
                    jnp.concatenate([z1, z2, z3, z1, z2, z1], axis=0),
                    (((0,), (0,)), ((), ())),
                    preferred_element_type=jnp.float32,
                )
                for n in range(p + 2, tiles):
                    d[n] = d[n] - change[8 * n : 8 * n + 8, :LANES]
                    e[n] = e[n] - change[8 * n : 8 * n + 8, LANES:]
            d[i], e[i] = d[i] - parts[0], e[i] - parts_e[0]
        roots = [lax.rsqrt(s[j][j]) for j in range(8)]
        d[p] = jnp.where(lane >= sub + first, stack([t[j] * roots[j] for j in range(8)]), 0.0)
        e[p] = stack([te[j] * roots[j] for j in range(8)])
    return jnp.concatenate(d, axis=0), jnp.concatenate(e, axis=0)


def factor_kernel(scale, sections, *refs):
    factor_ref = refs[3]
    analysis = lax.axis_index("sec") == sections - 1

    @pl.when(analysis)
    def _():
        factorize(scale, *refs)

    @pl.when(jnp.logical_not(analysis))
    def _():
        factor_ref[...] = jnp.zeros(factor_ref.shape, jnp.float32)


def factorize(
    scale, parts_ref, omega_ref, s_ref, factor_ref, inverse_ref, g, inner_ref, spread
):
    rank = s_ref.shape[0]
    snaps = omega_ref.shape[0]
    strips = rank // LANES
    rows_first = (((0,), (0,)), ((), ()))

    def band(r, c):
        return parts_ref[r * (strips + 1) + c]

    cross = jnp.concatenate(
        [
            jnp.concatenate([band(r, c) for c in range(strips)], axis=1)
            for r in range(snaps // 8)
        ],
        axis=0,
    )
    inner = jnp.concatenate([band(r, strips) for r in range(snaps // 8)], axis=0)
    omega = omega_ref[...]
    half = cross + 0.5 * jnp.dot(
        inner[:, :snaps], omega, precision=highest, preferred_element_type=jnp.float32
    )
    left = jnp.concatenate([half, omega], axis=0)
    right = jnp.concatenate([omega, half], axis=0)
    g[...] = s_ref[...] + lax.dot_general(
        left, right, rows_first, precision=highest, preferred_element_type=jnp.float32
    )
    inverse_ref[...] = jnp.zeros(inverse_ref.shape, jnp.float32)
    inner_ref[...] = jnp.zeros(inner_ref.shape, jnp.float32)
    factor_ref[...] = jnp.zeros(factor_ref.shape, jnp.float32)
    sub = lax.broadcasted_iota(jnp.int32, (8, LANES), 0)
    lane = lax.broadcasted_iota(jnp.int32, (8, LANES), 1)
    tiles = LANES // 8

    def rows_of(k):
        return slice(k * LANES, (k + 1) * LANES)

    for k in range(strips):
        here = rows_of(k)
        d = [g[k * LANES + 8 * i : k * LANES + 8 * i + 8, here] for i in range(tiles)]
        e = [jnp.where(lane == sub + 8 * i, 1.0, 0.0) for i in range(tiles)]
        upper, small = factor_block(d, e, sub, lane, spread.at[k % 2])
        factor_ref[here, here] = upper * (1.0 / scale)
        small_rows = [small]
        if k + 1 < strips:
            right = slice((k + 1) * LANES, rank)
            fresh = jnp.dot(
                small, g[here, right], precision=highest, preferred_element_type=jnp.float32
            )
            factor_ref[here, right] = fresh * (1.0 / scale)
            change = functools.partial(
                lax.dot_general,
                dimension_numbers=rows_first,
                precision=highest,
                preferred_element_type=jnp.float32,
            )
            following = rows_of(k + 1)
            g[following, right] = g[following, right] - change(fresh[:, :LANES], fresh)
            if k + 2 < strips:
                later = slice((k + 2) * LANES, rank)
                g[later, later] = g[later, later] - change(fresh[:, LANES:], fresh[:, LANES:])
        if k:
            left = slice(0, k * LANES)
            small_rows = [
                jnp.dot(
                    small, inner_ref[here, left], precision=highest,
                    preferred_element_type=jnp.float32,
                ),
                small,
            ]
        done = jnp.concatenate(small_rows, axis=1)
        if k + 1 < strips:
            upto = slice(0, (k + 1) * LANES)
            inner_ref[right, upto] = inner_ref[right, upto] - change(fresh, done)
        inverse_ref[0 : (k + 1) * LANES, here] = (done * scale).T


def basis_kernel(sections, inverse_ref, omega_ref, s_ref, *rest):
    pieces, out_ref = rest[:-1], rest[-1]
    analysis = lax.axis_index("sec") == sections - 1

    @pl.when(analysis)
    def _():
        def split(x):
            high = x.astype(jnp.bfloat16)
            return high, (x - high.astype(jnp.float32)).astype(jnp.bfloat16)

        dot = functools.partial(jnp.dot, preferred_element_type=jnp.float32)
        inverse = inverse_ref[...]
        mixed = jnp.dot(
            omega_ref[...], inverse, precision=highest, preferred_element_type=jnp.float32
        )
        x1, x2 = split(inverse)
        m1, m2 = split(jnp.concatenate([mixed, mixed], axis=0))
        stack = jnp.concatenate([x1, x2, m1, m2], axis=0)
        rows = 1024

        def strip(i, carry):
            at = pl.ds(pl.multiple_of(i * rows, rows), rows)
            s = s_ref[at, :]
            w = pieces[0][at, :]
            for piece in pieces[1:]:
                w = w + piece[at, :]
            w = w.astype(jnp.bfloat16)
            q = dot(jnp.concatenate([s, s, w, w], axis=1), stack)
            out_ref[at, :] = q.astype(jnp.bfloat16)
            return carry

        lax.fori_loop(0, s_ref.shape[0] // rows, strip, 0)

    @pl.when(jnp.logical_not(analysis))
    def _():
        out_ref[...] = jnp.zeros(out_ref.shape, jnp.bfloat16)


def shards(potential, previous, wave_coeff, sketch_in, omega, blocks, owners):
    sections = lax.axis_size("sec")
    columns = lax.axis_size("dev")
    devices = sections * columns
    extent_x, extent_y, depth = potential.shape
    list_width = owners.shape[1]
    per_device = list_width // (sections - 1)
    snaps, rank = omega.shape
    slab = max(8, depth // columns)
    per_slab = slab * columns // depth
    slots = columns * CAP
    order = neighbour_path(columns)
    path = []
    for section in range(sections - 1):
        path += [section * columns + d for d in (order if section % 2 == 0 else order[::-1])]
    up = [(path[i], path[i + per_slab]) for i in range(len(path) - per_slab)]
    down = [(b, a) for a, b in up]
    f32 = jnp.float32

    analysis = lax.axis_index("sec") == sections - 1

    def whole_gram():
        own = lax.dot_general(
            sketch_in, sketch_in, (((0,), (0,)), ((), ())), preferred_element_type=f32
        )
        own = own.reshape(columns, rank // columns, rank)
        own = lax.all_to_all(own, "dev", split_axis=0, concat_axis=0, tiled=True)
        own = jnp.broadcast_to(jnp.sum(own, axis=0)[None], own.shape)
        own = lax.all_to_all(own, "dev", split_axis=0, concat_axis=0, tiled=True)
        return own.reshape(rank, rank)

    scaled = omega * jnp.asarray(
        decay ** np.arange(1, snaps + 1, dtype=np.float64), f32
    )[:, None]

    chunk = 6 * slab + 8
    operands = (potential, previous, wave_coeff, blocks, owners)
    outgoing = pl.pallas_call(
        functools.partial(split_kernel, order, slab, per_slab),
        out_shape=jax.ShapeDtypeStruct((columns, chunk, LANES), f32),
        in_specs=vmem(*operands),
        out_specs=pl.BlockSpec(memory_space=pltpu.VMEM),
        scratch_shapes=[pltpu.VMEM((6, depth, LANES), f32)],
        compiler_params=big(),
    )(*operands)
    raw = lax.all_to_all(outgoing, "dev", split_axis=0, concat_axis=0, tiled=True)
    gram, scaled, raw = lax.optimization_barrier(
        (lax.cond(analysis, whole_gram, lambda: jnp.zeros((rank, rank), f32)), scaled, raw)
    )
    table = raw[:, 6 * slab : 6 * slab + 2, :list_width].astype(jnp.int32)

    def sides(x):
        return lax.ppermute(x, BOTH, up), x, lax.ppermute(x, BOTH, down)

    fields = sides(raw)
    state = fields
    held = jnp.zeros((columns * per_device, 8, LANES), f32)
    rounds = snaps // slab
    for number in range(rounds):
        last = number == rounds - 1
        operands = (table, *fields, *state, held)
        sent = jax.ShapeDtypeStruct((columns, slots // 2, 8, LANES), f32)
        flag = jax.ShapeDtypeStruct((1,), jnp.int32)
        result = [sent, sent, flag] if last else [jax.ShapeDtypeStruct((columns, 4 * slab, LANES), f32)]
        *moved, held = pl.pallas_call(
            functools.partial(
                steps_kernel, number * slab, slab, per_device, last, snaps, sections
            ),
            out_shape=(*result, jax.ShapeDtypeStruct(held.shape, f32)),
            in_specs=[pl.BlockSpec(memory_space=pltpu.SMEM)] + vmem(*operands[1:]),
            out_specs=tuple(
                pl.BlockSpec(memory_space=pltpu.SMEM if x.dtype == jnp.int32 else pltpu.VMEM)
                for x in (*result, held)
            ),
            scratch_shapes=[pltpu.VMEM((2 * columns, 3 * slab + 16, LANES), f32)] * 2
            + [pltpu.VMEM((2 * columns, 3 * slab, LANES), f32)] * 2
            + [pltpu.SMEM((columns,), jnp.int32)] * last,
            compiler_params=big(),
        )(*operands)
        if not last:
            state = sides(moved[0])

    def trade(x):
        return lax.all_to_all(x, "dev", split_axis=0, concat_axis=0, tiled=True)

    arrived = trade(moved[0])
    over = lax.cond(moved[2][0] > 0, trade, lambda x: x, moved[1])
    operands = (table, arrived, over, sketch_in)
    bands = (snaps // 8) * (rank // LANES + 1)
    share = -(-bands // columns)
    parts, wide = pl.pallas_call(
        functools.partial(product_kernel, order, slab, per_slab, snaps, sections),
        out_shape=(
            jax.ShapeDtypeStruct((columns, share, 8, LANES), f32),
            jax.ShapeDtypeStruct((slots * depth, LANES), f32),
        ),
        in_specs=[pl.BlockSpec(memory_space=pltpu.SMEM)] + vmem(*operands[1:]),
        out_specs=tuple(vmem(0, 0)),
        compiler_params=big(60),
    )(*operands)

    def to_analysis(x):
        return [lax.ppermute(x, "sec", [(i, sections - 1)]) for i in range(sections - 1)]

    terms = lax.all_to_all(parts, "dev", split_axis=0, concat_axis=0, tiled=True)
    total = jnp.sum(terms, axis=0)
    terms = to_analysis(total)
    wide, *terms = lax.optimization_barrier((wide, *terms))
    pieces = to_analysis(wide)

    def exchange(terms):
        total = jnp.broadcast_to(sum(terms[1:], terms[0])[None], parts.shape)
        return lax.all_to_all(total, "dev", split_axis=0, concat_axis=0, tiled=True)

    sums = lax.cond(analysis, exchange, lambda terms: jnp.zeros(parts.shape, f32), terms)
    sums = sums.reshape(columns * share, 8, LANES)

    scale = math.sqrt(columns * columns * CAP * depth)
    operands = (sums, scaled, gram)
    factor, inverse = pl.pallas_call(
        functools.partial(factor_kernel, scale, sections),
        out_shape=(jax.ShapeDtypeStruct((rank, rank), f32),) * 2,
        in_specs=vmem(*operands),
        out_specs=tuple(vmem(0, 0)),
        scratch_shapes=[pltpu.VMEM((rank, rank), f32)] * 2 + [pltpu.VMEM((2, 160, LANES), f32)],
        compiler_params=big(),
    )(*operands)
    operands = (inverse, scaled, sketch_in, *pieces)
    basis = pl.pallas_call(
        functools.partial(basis_kernel, sections),
        out_shape=jax.ShapeDtypeStruct(sketch_in.shape, jnp.bfloat16),
        in_specs=vmem(*operands),
        out_specs=pl.BlockSpec(memory_space=pltpu.VMEM),
        compiler_params=big(60),
    )(*operands)
    return (basis[None], factor[None])


def solution(mesh):
    placed = (
        P("dev", None, "sec"),
        P("dev", None, "sec"),
        P("dev", None, "sec"),
        P("dev", None),
        P(),
        P("dev", None),
        P("dev", None),
    )
    return jax.shard_map(
        shards,
        mesh=mesh,
        in_specs=placed,
        out_specs=(P("sec", "dev", None), P("sec", None, None)),
        check_vma=False,
    )
```

```python
import functools
import math

import jax
import jax.numpy as jnp
import numpy as np
from jax import lax
from jax.experimental import pallas as pl
from jax.experimental.pallas import tpu as pltpu
from jax.sharding import PartitionSpec as P

CAP = 2
damping = 0.05
LANES = 128
highest = lax.Precision.HIGHEST
decay = math.sqrt(1.0 - damping)
BOTH = ("sec", "dev")


def neighbour_path(columns):
    order = []
    for i in range(0, columns, 2):
        pair = [i, i + 1]
        order += pair if (i // 2) % 2 == 0 else pair[::-1]
    return order


def vmem(*arrays):
    return [pl.BlockSpec(memory_space=pltpu.VMEM)] * len(arrays)


def big(limit=48):
    return pltpu.CompilerParams(vmem_limit_bytes=limit << 20)


def slab_of(order, column, section, per_slab):
    place = order.index(column)
    forward, backward = place // per_slab, (len(order) - 1 - place) // per_slab
    return jnp.where(section % 2 == 0, forward, backward)


def split_kernel(order, slab, per_slab, u_ref, e_ref, k_ref, blocks_ref, owners_ref, out_ref, turned):
    section = lax.axis_index("sec")
    extent_x, extent_y, depth = u_ref.shape
    for a, ref in enumerate((u_ref, e_ref, k_ref)):
        for p in range(2):
            rows = jnp.concatenate([ref[x] for x in range(p, extent_x, 2)], axis=0)
            if a == 1:
                rows = rows * decay
            turned[2 * a + p] = rows.T
    for column in range(len(order)):
        at = slab_of(order, column, section, per_slab)
        start = pl.multiple_of(at * slab, 8)
        for q in range(6):
            out_ref[column, q * slab : (q + 1) * slab, :] = turned[q, pl.ds(start, slab), :]
        for r, ref in enumerate((blocks_ref, owners_ref)):
            out_ref[column, 6 * slab + r : 6 * slab + r + 1, : ref.shape[1]] = ref[...].astype(
                jnp.float32
            )


def steps_kernel(*args):
    last, sections = args[3], args[5]
    if last:
        flag_ref = args[16]
        flag_ref[0] = 0

    @pl.when(lax.axis_index("sec") < sections - 1)
    def _():
        evolve(*args)


def evolve(
    first_step, slab, per_device, last, snaps, sections,
    table, kl, kc, kr, sl, sc, sr, w_in, *rest,
):
    if last:
        send_ref, over_ref, flag_ref, w_ref, field_a, field_b, gain, own, used = rest
    else:
        state_ref, w_ref, field_a, field_b, gain, own = rest
    list_start = lax.axis_index("sec") * per_device
    columns = kc.shape[0]
    rows = 3 * slab
    lane = lax.broadcasted_iota(jnp.int32, (8, LANES), 1)
    y_first, y_last = lane % 32 == 0, lane % 32 == 31
    zero = jnp.zeros((8, LANES), jnp.float32)

    for o in range(2 * columns):
        d, p = o // 2, o % 2
        for field, at in ((field_a, p), (field_b, 2 + p)):
            field[o, 0:8, :] = zero
            field[o, 8 + rows : 16 + rows, :] = zero
            for h, ref in enumerate((sl, sc, sr)):
                field[o, 8 + h * slab : 8 + (h + 1) * slab, :] = ref[
                    d, at * slab : (at + 1) * slab, :
                ]
        for h, ref in enumerate((kl, kc, kr)):
            k = ref[d, (4 + p) * slab : (5 + p) * slab, :]
            gain[o, h * slab : (h + 1) * slab, :] = k * (1.0 / decay)
            own[o, h * slab : (h + 1) * slab, :] = ((2.0 - damping) - 6.0 * k) * (1.0 / decay)
    w_ref[...] = w_in[...]

    def step(src, dst, tiles, number):
        for z in tiles:
            at = slice(8 + 8 * z, 16 + 8 * z)
            low = slice(7 + 8 * z, 15 + 8 * z)
            high = slice(9 + 8 * z, 17 + 8 * z)
            here = slice(8 * z, 8 * z + 8)
            values = [src[o, at, :] for o in range(2 * columns)]
            up = [pltpu.roll(values[2 * d + 1], 32, 1) for d in range(columns)]
            down = [pltpu.roll(values[2 * d], LANES - 32, 1) for d in range(columns)]
            for o in range(2 * columns):
                d, p = o // 2, o % 2
                v = values[o]
                if p == 0:
                    side = jnp.where(lane < 32, up[d - 1] if d > 0 else zero, up[d])
                    total = values[o + 1] + side
                else:
                    side = jnp.where(
                        lane >= LANES - 32, down[d + 1] if d + 1 < columns else zero, down[d]
                    )
                    total = values[o - 1] + side
                total = total + (src[o, low, :] + src[o, high, :])
                total = total + jnp.where(y_first, 0.0, pltpu.roll(v, 1, 1))
                total = total + jnp.where(y_last, 0.0, pltpu.roll(v, LANES - 1, 1))
                dst[o, at, :] = own[o, here, :] * v + gain[o, here, :] * total - dst[o, at, :]

        def column_blocks(d, carry):
            for i in range(per_device):
                block = table[d, 0, list_start + i]
                x, y = block >> 5, block & 31
                at_lane = ((x >> 1) << 5) + y
                o = 2 * d + (x & 1)
                j = d * per_device + i
                held = w_ref[j]
                for h in range(slab // 8):
                    target = h * snaps + number
                    value = dst[o, 8 + slab + 8 * h : 16 + slab + 8 * h, :]
                    moved = pltpu.roll(value, (target - at_lane) & (LANES - 1), 1)
                    held = jnp.where(lane == target, moved, held)
                w_ref[j] = held
            return carry

        lax.fori_loop(0, columns, column_blocks, 0, unroll=min(columns, 8))

    for phase in range(slab // 8):
        tiles = range(phase, 3 * slab // 8 - phase)

        def pair(m, carry):
            number = first_step + 8 * phase + 2 * m
            step(field_a, field_b, tiles, number)
            step(field_b, field_a, tiles, number + 1)
            return carry

        lax.fori_loop(0, 4, pair, 0)

    if last:
        half = send_ref.shape[1]
        for d in range(columns):
            used[d] = 0

        def place(d, carry):
            for i in range(per_device):
                mine = table[d, 1, list_start + i]
                n = used[mine]
                used[mine] = n + 1

                @pl.when(n < half)
                def _(i=i, mine=mine, n=n):
                    send_ref[mine, n] = w_ref[d * per_device + i]

                @pl.when(n >= half)
                def _(i=i, mine=mine, n=n):
                    over_ref[mine, n - half] = w_ref[d * per_device + i]

            return carry

        lax.fori_loop(0, columns, place, 0)
        for d in range(columns):
            flag_ref[0] = jnp.maximum(flag_ref[0], jnp.where(used[d] > half, 1, 0))
    else:
        for o in range(2 * columns):
            d, p = o // 2, o % 2
            state_ref[d, p * slab : (p + 1) * slab, :] = field_a[o, 8 + slab : 8 + 2 * slab, :]
            state_ref[d, (2 + p) * slab : (3 + p) * slab, :] = field_b[
                o, 8 + slab : 8 + 2 * slab, :
            ]


def unpack(tile, h, snaps, lane):
    if h:
        tile = pltpu.roll(tile, LANES - h * snaps, 1)
    return jnp.where(lane < snaps, tile, 0.0)


def product_kernel(*args):
    sections = args[4]

    @pl.when(lax.axis_index("sec") < sections - 1)
    def _():
        products(*args)


def products(
    order, slab, per_slab, snaps, sections, table, w_ref, over_ref, s_ref, out_ref, wide
):
    section = lax.axis_index("sec")
    me = lax.axis_index("dev")
    columns = len(order)
    per_device = table.shape[2] // (sections - 1)
    list_start = section * per_device
    half = w_ref.shape[1]
    lane = lax.broadcasted_iota(jnp.int32, (8, LANES), 1)
    wide[...] = jnp.zeros(wide.shape, jnp.float32)

    def place(ref, n, slot):
        for column in range(columns):
            if order.index(column) % per_slab:
                continue
            at = slab_of(order, column, section, per_slab)
            tile = ref[column, n]
            for h in range(slab // 8):
                w = unpack(tile, h, snaps, lane)
                w1 = w.astype(jnp.bfloat16).astype(jnp.float32)
                w2 = (w - w1).astype(jnp.bfloat16).astype(jnp.float32)
                start = pl.multiple_of(slot * LANES + at * slab + 8 * h, 8)
                wide[pl.ds(start, 8), :] = w1 + pltpu.roll(w2, snaps, 1)

    def row(d, n):
        def earlier(m, c):
            return c + jnp.where(table[d, 1, m] == me, 1, 0)

        count = lax.fori_loop(0, list_start, earlier, 0)
        for i in range(per_device):
            mine = table[d, 1, list_start + i] == me
            slot = d * CAP + count

            @pl.when(jnp.logical_and(mine, n < half))
            def _(n=n, slot=slot):
                place(w_ref, n, slot)

            @pl.when(jnp.logical_and(mine, n >= half))
            def _(n=n, slot=slot):
                place(over_ref, n - half, slot)

            step = jnp.where(mine, 1, 0)
            n, count = n + step, count + step
        return n

    lax.fori_loop(0, columns, row, 0)
    both = wide[...].astype(jnp.bfloat16)
    dot = functools.partial(
        lax.dot_general,
        dimension_numbers=(((0,), (0,)), ((), ())),
        preferred_element_type=jnp.float32,
    )
    cross = dot(both, s_ref[...])
    cross = cross[:snaps] + cross[snaps:]
    inner = dot(both, both)
    inner = inner[:snaps, :] + inner[snaps:, :]
    inner = inner + pltpu.roll(inner, snaps, 1)
    strips = cross.shape[1] // LANES
    share = out_ref.shape[1]
    for r in range(snaps // 8):
        here = slice(8 * r, 8 * r + 8)
        for c in range(strips):
            at = r * (strips + 1) + c
            out_ref[at // share, at % share] = cross[here, c * LANES : (c + 1) * LANES]
        at = r * (strips + 1) + strips
        out_ref[at // share, at % share] = inner[here, :]


def three(x):
    x1 = x.astype(jnp.bfloat16)
    rest = x - x1.astype(jnp.float32)
    x2 = rest.astype(jnp.bfloat16)
    return x1, x2, (rest - x2.astype(jnp.float32)).astype(jnp.bfloat16)


def reciprocal(x):
    guess = pl.reciprocal(x, approx=True)
    return guess * (2.0 - x * guess)


def factor_block(d, e, sub, lane, spread):
    tiles = len(d)

    def wide(x):
        return jnp.broadcast_to(x, (8, LANES))

    def stack(values):
        out = values[0]
        for j in range(1, 8):
            out = jnp.where(sub == j, values[j], out)
        return out

    for p in range(tiles):
        first = 8 * p
        cols = [wide(d[p][:, first + j : first + j + 1]) for j in range(8)]
        base = 80 * (p % 2)
        for k, value in enumerate(cols + [d[p], e[p]]):
            spread[base + 8 * k : base + 8 * k + 8, :] = value

        def row(k, j, base=base):
            return spread[pl.ds(base + 8 * k + j, 8, stride=0), :]

        s = [[row(k, j) if k >= j else None for k in range(8)] for j in range(8)]
        t = [row(8, j) for j in range(8)]
        te = [row(9, j) for j in range(8)]
        inv, m = [], [[None] * 8 for _ in range(8)]
        for j in range(0, 8, 2):
            n = j + 1
            a, b, c = s[j][j], s[j][n], s[n][n]
            det = a * c - b * b
            inv_a, inv_det = reciprocal(a), reciprocal(det)
            inv += [inv_a, a * inv_det]
            m[j][n] = b * inv_a
            s[n][n] = det * inv_a
            t[n] = t[n] - m[j][n] * t[j]
            te[n] = te[n] - m[j][n] * te[j]
            for k in range(j + 2, 8):
                m[j][k] = s[j][k] * inv_a
                m[n][k] = (a * s[n][k] - b * s[j][k]) * inv_det
                s[n][k] = s[n][k] - m[j][n] * s[j][k]
            for k in range(j + 2, 8):
                for i in range(k, 8):
                    s[k][i] = (s[k][i] - m[j][k] * s[j][i]) - m[n][k] * s[n][i]
                t[k] = (t[k] - m[j][k] * t[j]) - m[n][k] * t[n]
                te[k] = (te[k] - m[j][k] * te[j]) - m[n][k] * te[n]
        if p + 1 < tiles:
            z, ze = [None] * 8, [None] * 8
            for j in reversed(range(8)):
                z[j], ze[j] = t[j] * inv[j], te[j] * inv[j]
                for k in range(j + 1, 8):
                    z[j] = z[j] - m[j][k] * z[k]
                    ze[j] = ze[j] - m[j][k] * ze[k]
            i = p + 1
            parts, parts_e = [], []
            for j in range(8):
                col = wide(d[i][:, first + j : first + j + 1])
                parts.append(col * z[j])
                parts_e.append(col * ze[j])
            while len(parts) > 1:
                parts = [x + y for x, y in zip(parts[::2], parts[1::2])]
                parts_e = [x + y for x, y in zip(parts_e[::2], parts_e[1::2])]
            if p + 2 < tiles:
                p1, p2, p3 = three(d[p])
                z1, z2, z3 = three(jnp.concatenate([stack(z), stack(ze)], axis=1))
                change = lax.dot_general(
                    jnp.concatenate([p1, p1, p1, p2, p2, p3], axis=0),
                    jnp.concatenate([z1, z2, z3, z1, z2, z1], axis=0),
                    (((0,), (0,)), ((), ())),
                    preferred_element_type=jnp.float32,
                )
                for n in range(p + 2, tiles):
                    d[n] = d[n] - change[8 * n : 8 * n + 8, :LANES]
                    e[n] = e[n] - change[8 * n : 8 * n + 8, LANES:]
            d[i], e[i] = d[i] - parts[0], e[i] - parts_e[0]
        roots = [lax.rsqrt(s[j][j]) for j in range(8)]
        d[p] = jnp.where(lane >= sub + first, stack([t[j] * roots[j] for j in range(8)]), 0.0)
        e[p] = stack([te[j] * roots[j] for j in range(8)])
    return jnp.concatenate(d, axis=0), jnp.concatenate(e, axis=0)


def factor_kernel(scale, sections, *refs):
    factor_ref = refs[3]
    analysis = lax.axis_index("sec") == sections - 1

    @pl.when(analysis)
    def _():
        factorize(scale, *refs)

    @pl.when(jnp.logical_not(analysis))
    def _():
        factor_ref[...] = jnp.zeros(factor_ref.shape, jnp.float32)


def factorize(
    scale, parts_ref, omega_ref, s_ref, factor_ref, inverse_ref, g, inner_ref, spread
):
    rank = s_ref.shape[0]
    snaps = omega_ref.shape[0]
    strips = rank // LANES
    rows_first = (((0,), (0,)), ((), ()))

    def band(r, c):
        return parts_ref[r * (strips + 1) + c]

    cross = jnp.concatenate(
        [
            jnp.concatenate([band(r, c) for c in range(strips)], axis=1)
            for r in range(snaps // 8)
        ],
        axis=0,
    )
    inner = jnp.concatenate([band(r, strips) for r in range(snaps // 8)], axis=0)
    omega = omega_ref[...]
    half = cross + 0.5 * jnp.dot(
        inner[:, :snaps], omega, precision=highest, preferred_element_type=jnp.float32
    )
    left = jnp.concatenate([half, omega], axis=0)
    right = jnp.concatenate([omega, half], axis=0)
    g[...] = s_ref[...] + lax.dot_general(
        left, right, rows_first, precision=highest, preferred_element_type=jnp.float32
    )
    inverse_ref[...] = jnp.zeros(inverse_ref.shape, jnp.float32)
    inner_ref[...] = jnp.zeros(inner_ref.shape, jnp.float32)
    factor_ref[...] = jnp.zeros(factor_ref.shape, jnp.float32)
    sub = lax.broadcasted_iota(jnp.int32, (8, LANES), 0)
    lane = lax.broadcasted_iota(jnp.int32, (8, LANES), 1)
    tiles = LANES // 8

    def rows_of(k):
        return slice(k * LANES, (k + 1) * LANES)

    for k in range(strips):
        here = rows_of(k)
        d = [g[k * LANES + 8 * i : k * LANES + 8 * i + 8, here] for i in range(tiles)]
        e = [jnp.where(lane == sub + 8 * i, 1.0, 0.0) for i in range(tiles)]
        upper, small = factor_block(d, e, sub, lane, spread.at[k % 2])
        factor_ref[here, here] = upper * (1.0 / scale)
        small_rows = [small]
        if k + 1 < strips:
            right = slice((k + 1) * LANES, rank)
            fresh = jnp.dot(
                small, g[here, right], precision=highest, preferred_element_type=jnp.float32
            )
            factor_ref[here, right] = fresh * (1.0 / scale)
            change = functools.partial(
                lax.dot_general,
                dimension_numbers=rows_first,
                precision=highest,
                preferred_element_type=jnp.float32,
            )
            following = rows_of(k + 1)
            g[following, right] = g[following, right] - change(fresh[:, :LANES], fresh)
            if k + 2 < strips:
                later = slice((k + 2) * LANES, rank)
                g[later, later] = g[later, later] - change(fresh[:, LANES:], fresh[:, LANES:])
        if k:
            left = slice(0, k * LANES)
            small_rows = [
                jnp.dot(
                    small, inner_ref[here, left], precision=highest,
                    preferred_element_type=jnp.float32,
                ),
                small,
            ]
        done = jnp.concatenate(small_rows, axis=1)
        if k + 1 < strips:
            upto = slice(0, (k + 1) * LANES)
            inner_ref[right, upto] = inner_ref[right, upto] - change(fresh, done)
        inverse_ref[0 : (k + 1) * LANES, here] = (done * scale).T


def basis_kernel(sections, inverse_ref, omega_ref, s_ref, *rest):
    pieces, out_ref, stack = rest[:-2], rest[-2], rest[-1]
    analysis = lax.axis_index("sec") == sections - 1
    rank = inverse_ref.shape[0]
    dot = functools.partial(jnp.dot, preferred_element_type=jnp.float32)

    @pl.when(jnp.logical_and(analysis, pl.program_id(0) == 0))
    def _():
        def split(x):
            high = x.astype(jnp.bfloat16)
            return high, (x - high.astype(jnp.float32)).astype(jnp.bfloat16)

        inverse = inverse_ref[...]
        mixed = dot(omega_ref[...], inverse, precision=highest)
        x1, x2 = split(inverse)
        m1, m2 = split(jnp.concatenate([mixed, mixed], axis=0))
        stack[...] = jnp.concatenate([x1, x2, m1, m2], axis=0)

    @pl.when(analysis)
    def _():
        s = s_ref[...]
        w = pieces[0][...]
        for piece in pieces[1:]:
            w = w + piece[...]
        w = w.astype(jnp.bfloat16)
        q = dot(jnp.concatenate([s, s, w, w], axis=1), stack[...])
        out_ref[...] = q.astype(jnp.bfloat16)

    @pl.when(jnp.logical_not(analysis))
    def _():
        out_ref[...] = jnp.zeros(out_ref.shape, jnp.bfloat16)


def shards(potential, previous, wave_coeff, sketch_in, omega, blocks, owners):
    sections = lax.axis_size("sec")
    columns = lax.axis_size("dev")
    devices = sections * columns
    extent_x, extent_y, depth = potential.shape
    list_width = owners.shape[1]
    per_device = list_width // (sections - 1)
    snaps, rank = omega.shape
    slab = max(8, depth // columns)
    per_slab = slab * columns // depth
    slots = columns * CAP
    order = neighbour_path(columns)
    path = []
    for section in range(sections - 1):
        path += [section * columns + d for d in (order if section % 2 == 0 else order[::-1])]
    up = [(path[i], path[i + per_slab]) for i in range(len(path) - per_slab)]
    down = [(b, a) for a, b in up]
    f32 = jnp.float32

    analysis = lax.axis_index("sec") == sections - 1

    def whole_gram():
        own = lax.dot_general(
            sketch_in, sketch_in, (((0,), (0,)), ((), ())), preferred_element_type=f32
        )
        own = own.reshape(columns, rank // columns, rank)
        own = lax.all_to_all(own, "dev", split_axis=0, concat_axis=0, tiled=True)
        own = jnp.broadcast_to(jnp.sum(own, axis=0)[None], own.shape)
        own = lax.all_to_all(own, "dev", split_axis=0, concat_axis=0, tiled=True)
        return own.reshape(rank, rank)

    scaled = omega * jnp.asarray(
        decay ** np.arange(1, snaps + 1, dtype=np.float64), f32
    )[:, None]

    chunk = 6 * slab + 8
    operands = (potential, previous, wave_coeff, blocks, owners)
    outgoing = pl.pallas_call(
        functools.partial(split_kernel, order, slab, per_slab),
        out_shape=jax.ShapeDtypeStruct((columns, chunk, LANES), f32),
        in_specs=vmem(*operands),
        out_specs=pl.BlockSpec(memory_space=pltpu.VMEM),
        scratch_shapes=[pltpu.VMEM((6, depth, LANES), f32)],
        compiler_params=big(),
    )(*operands)
    raw = lax.all_to_all(outgoing, "dev", split_axis=0, concat_axis=0, tiled=True)
    gram, scaled, raw = lax.optimization_barrier(
        (lax.cond(analysis, whole_gram, lambda: jnp.zeros((rank, rank), f32)), scaled, raw)
    )
    table = raw[:, 6 * slab : 6 * slab + 2, :list_width].astype(jnp.int32)

    def sides(x):
        return lax.ppermute(x, BOTH, up), x, lax.ppermute(x, BOTH, down)

    fields = sides(raw)
    state = fields
    held = jnp.zeros((columns * per_device, 8, LANES), f32)
    rounds = snaps // slab
    for number in range(rounds):
        last = number == rounds - 1
        operands = (table, *fields, *state, held)
        sent = jax.ShapeDtypeStruct((columns, slots // 2, 8, LANES), f32)
        flag = jax.ShapeDtypeStruct((1,), jnp.int32)
        result = [sent, sent, flag] if last else [jax.ShapeDtypeStruct((columns, 4 * slab, LANES), f32)]
        *moved, held = pl.pallas_call(
            functools.partial(
                steps_kernel, number * slab, slab, per_device, last, snaps, sections
            ),
            out_shape=(*result, jax.ShapeDtypeStruct(held.shape, f32)),
            in_specs=[pl.BlockSpec(memory_space=pltpu.SMEM)] + vmem(*operands[1:]),
            out_specs=tuple(
                pl.BlockSpec(memory_space=pltpu.SMEM if x.dtype == jnp.int32 else pltpu.VMEM)
                for x in (*result, held)
            ),
            scratch_shapes=[pltpu.VMEM((2 * columns, 3 * slab + 16, LANES), f32)] * 2
            + [pltpu.VMEM((2 * columns, 3 * slab, LANES), f32)] * 2
            + [pltpu.SMEM((columns,), jnp.int32)] * last,
            compiler_params=big(),
        )(*operands)
        if not last:
            state = sides(moved[0])

    def trade(x):
        return lax.all_to_all(x, "dev", split_axis=0, concat_axis=0, tiled=True)

    arrived = trade(moved[0])
    over = lax.cond(moved[2][0] > 0, trade, lambda x: x, moved[1])
    operands = (table, arrived, over, sketch_in)
    bands = (snaps // 8) * (rank // LANES + 1)
    share = -(-bands // columns)
    parts, wide = pl.pallas_call(
        functools.partial(product_kernel, order, slab, per_slab, snaps, sections),
        out_shape=(
            jax.ShapeDtypeStruct((columns, share, 8, LANES), f32),
            jax.ShapeDtypeStruct((slots * depth, LANES), f32),
        ),
        in_specs=[pl.BlockSpec(memory_space=pltpu.SMEM)] + vmem(*operands[1:]),
        out_specs=tuple(vmem(0, 0)),
        compiler_params=big(60),
    )(*operands)

    def to_analysis(x):
        return [lax.ppermute(x, "sec", [(i, sections - 1)]) for i in range(sections - 1)]

    terms = lax.all_to_all(parts, "dev", split_axis=0, concat_axis=0, tiled=True)
    total = jnp.sum(terms, axis=0)
    terms = to_analysis(total)
    wide, *terms = lax.optimization_barrier((wide, *terms))
    pieces = to_analysis(wide)

    def exchange(terms):
        total = jnp.broadcast_to(sum(terms[1:], terms[0])[None], parts.shape)
        return lax.all_to_all(total, "dev", split_axis=0, concat_axis=0, tiled=True)

    sums = lax.cond(analysis, exchange, lambda terms: jnp.zeros(parts.shape, f32), terms)
    sums = sums.reshape(columns * share, 8, LANES)

    scale = math.sqrt(columns * columns * CAP * depth)
    operands = (sums, scaled, gram)
    factor, inverse = pl.pallas_call(
        functools.partial(factor_kernel, scale, sections),
        out_shape=(jax.ShapeDtypeStruct((rank, rank), f32),) * 2,
        in_specs=vmem(*operands),
        out_specs=tuple(vmem(0, 0)),
        scratch_shapes=[pltpu.VMEM((rank, rank), f32)] * 2 + [pltpu.VMEM((2, 160, LANES), f32)],
        compiler_params=big(),
    )(*operands)
    operands = (inverse, scaled, sketch_in, *pieces)
    rows = 512

    def whole(x):
        return pl.BlockSpec(x.shape, lambda i: (0, 0))

    def strip(x):
        return pl.BlockSpec((rows, x.shape[1]), lambda i: (i, 0))

    basis = pl.pallas_call(
        functools.partial(basis_kernel, sections),
        out_shape=jax.ShapeDtypeStruct(sketch_in.shape, jnp.bfloat16),
        grid=(sketch_in.shape[0] // rows,),
        in_specs=[whole(inverse), whole(scaled), strip(sketch_in)] + [strip(x) for x in pieces],
        out_specs=strip(sketch_in),
        scratch_shapes=[pltpu.VMEM((2 * rank + 4 * snaps, rank), jnp.bfloat16)],
        compiler_params=big(60),
    )(*operands)
    return (basis[None], factor[None])


def solution(mesh):
    placed = (
        P("dev", None, "sec"),
        P("dev", None, "sec"),
        P("dev", None, "sec"),
        P("dev", None),
        P(),
        P("dev", None),
        P("dev", None),
    )
    return jax.shard_map(
        shards,
        mesh=mesh,
        in_specs=placed,
        out_specs=(P("sec", "dev", None), P("sec", None, None)),
        check_vma=False,
    )
```

```python
import functools
import math

import jax
import jax.numpy as jnp
import numpy as np
from jax import lax
from jax.experimental import pallas as pl
from jax.experimental.pallas import tpu as pltpu
from jax.sharding import PartitionSpec as P

CAP = 2
damping = 0.05
LANES = 128
highest = lax.Precision.HIGHEST
decay = math.sqrt(1.0 - damping)
BOTH = ("sec", "dev")


def neighbour_path(columns):
    order = []
    for i in range(0, columns, 2):
        pair = [i, i + 1]
        order += pair if (i // 2) % 2 == 0 else pair[::-1]
    return order


def vmem(*arrays):
    return [pl.BlockSpec(memory_space=pltpu.VMEM)] * len(arrays)


def big(limit=48):
    return pltpu.CompilerParams(vmem_limit_bytes=limit << 20)


def slab_of(order, column, section, per_slab):
    place = order.index(column)
    forward, backward = place // per_slab, (len(order) - 1 - place) // per_slab
    return jnp.where(section % 2 == 0, forward, backward)


def split_kernel(order, slab, per_slab, u_ref, e_ref, k_ref, blocks_ref, owners_ref, out_ref, turned):
    section = lax.axis_index("sec")
    extent_x, extent_y, depth = u_ref.shape
    for a, ref in enumerate((u_ref, e_ref, k_ref)):
        for p in range(2):
            rows = jnp.concatenate([ref[x] for x in range(p, extent_x, 2)], axis=0)
            if a == 1:
                rows = rows * decay
            turned[2 * a + p] = rows.T
    for column in range(len(order)):
        at = slab_of(order, column, section, per_slab)
        start = pl.multiple_of(at * slab, 8)
        for q in range(6):
            out_ref[column, q * slab : (q + 1) * slab, :] = turned[q, pl.ds(start, slab), :]
        for r, ref in enumerate((blocks_ref, owners_ref)):
            out_ref[column, 6 * slab + r : 6 * slab + r + 1, : ref.shape[1]] = ref[...].astype(
                jnp.float32
            )


def steps_kernel(*args):
    last, sections = args[3], args[5]
    if last:
        flag_ref = args[16]
        flag_ref[0] = 0

    @pl.when(lax.axis_index("sec") < sections - 1)
    def _():
        evolve(*args)


def evolve(
    first_step, slab, per_device, last, snaps, sections,
    table, kl, kc, kr, sl, sc, sr, w_in, *rest,
):
    if last:
        send_ref, over_ref, flag_ref, w_ref, field_a, field_b, gain, own, used = rest
    else:
        state_ref, w_ref, field_a, field_b, gain, own = rest
    list_start = lax.axis_index("sec") * per_device
    columns = kc.shape[0]
    rows = 3 * slab
    lane = lax.broadcasted_iota(jnp.int32, (8, LANES), 1)
    y_first, y_last = lane % 32 == 0, lane % 32 == 31
    zero = jnp.zeros((8, LANES), jnp.float32)

    for o in range(2 * columns):
        d, p = o // 2, o % 2
        for field, at in ((field_a, p), (field_b, 2 + p)):
            field[o, 0:8, :] = zero
            field[o, 8 + rows : 16 + rows, :] = zero
            for h, ref in enumerate((sl, sc, sr)):
                field[o, 8 + h * slab : 8 + (h + 1) * slab, :] = ref[
                    d, at * slab : (at + 1) * slab, :
                ]
        for h, ref in enumerate((kl, kc, kr)):
            k = ref[d, (4 + p) * slab : (5 + p) * slab, :]
            gain[o, h * slab : (h + 1) * slab, :] = k * (1.0 / decay)
            own[o, h * slab : (h + 1) * slab, :] = ((2.0 - damping) - 6.0 * k) * (1.0 / decay)
    w_ref[...] = w_in[...]

    def step(src, dst, tiles, number):
        for z in tiles:
            at = slice(8 + 8 * z, 16 + 8 * z)
            low = slice(7 + 8 * z, 15 + 8 * z)
            high = slice(9 + 8 * z, 17 + 8 * z)
            here = slice(8 * z, 8 * z + 8)
            values = [src[o, at, :] for o in range(2 * columns)]
            up = [pltpu.roll(values[2 * d + 1], 32, 1) for d in range(columns)]
            down = [pltpu.roll(values[2 * d], LANES - 32, 1) for d in range(columns)]
            for o in range(2 * columns):
                d, p = o // 2, o % 2
                v = values[o]
                if p == 0:
                    side = jnp.where(lane < 32, up[d - 1] if d > 0 else zero, up[d])
                    total = values[o + 1] + side
                else:
                    side = jnp.where(
                        lane >= LANES - 32, down[d + 1] if d + 1 < columns else zero, down[d]
                    )
                    total = values[o - 1] + side
                total = total + (src[o, low, :] + src[o, high, :])
                total = total + jnp.where(y_first, 0.0, pltpu.roll(v, 1, 1))
                total = total + jnp.where(y_last, 0.0, pltpu.roll(v, LANES - 1, 1))
                dst[o, at, :] = own[o, here, :] * v + gain[o, here, :] * total - dst[o, at, :]

        def column_blocks(d, carry):
            for i in range(per_device):
                block = table[d, 0, list_start + i]
                x, y = block >> 5, block & 31
                at_lane = ((x >> 1) << 5) + y
                o = 2 * d + (x & 1)
                j = d * per_device + i
                held = w_ref[j]
                for h in range(slab // 8):
                    target = h * snaps + number
                    value = dst[o, 8 + slab + 8 * h : 16 + slab + 8 * h, :]
                    moved = pltpu.roll(value, (target - at_lane) & (LANES - 1), 1)
                    held = jnp.where(lane == target, moved, held)
                w_ref[j] = held
            return carry

        lax.fori_loop(0, columns, column_blocks, 0, unroll=min(columns, 8))

    for phase in range(slab // 8):
        tiles = range(phase, 3 * slab // 8 - phase)

        def pair(m, carry):
            number = first_step + 8 * phase + 2 * m
            step(field_a, field_b, tiles, number)
            step(field_b, field_a, tiles, number + 1)
            return carry

        lax.fori_loop(0, 4, pair, 0)

    if last:
        half = send_ref.shape[1]
        for d in range(columns):
            used[d] = 0

        def place(d, carry):
            for i in range(per_device):
                mine = table[d, 1, list_start + i]
                n = used[mine]
                used[mine] = n + 1

                @pl.when(n < half)
                def _(i=i, mine=mine, n=n):
                    send_ref[mine, n] = w_ref[d * per_device + i]

                @pl.when(n >= half)
                def _(i=i, mine=mine, n=n):
                    over_ref[mine, n - half] = w_ref[d * per_device + i]

            return carry

        lax.fori_loop(0, columns, place, 0)
        for d in range(columns):
            flag_ref[0] = jnp.maximum(flag_ref[0], jnp.where(used[d] > half, 1, 0))
    else:
        for o in range(2 * columns):
            d, p = o // 2, o % 2
            state_ref[d, p * slab : (p + 1) * slab, :] = field_a[o, 8 + slab : 8 + 2 * slab, :]
            state_ref[d, (2 + p) * slab : (3 + p) * slab, :] = field_b[
                o, 8 + slab : 8 + 2 * slab, :
            ]


def unpack(tile, h, snaps, lane):
    if h:
        tile = pltpu.roll(tile, LANES - h * snaps, 1)
    return jnp.where(lane < snaps, tile, 0.0)


def product_kernel(*args):
    sections = args[4]

    @pl.when(lax.axis_index("sec") < sections - 1)
    def _():
        products(*args)


def products(
    order, slab, per_slab, snaps, sections, table, w_ref, over_ref, s_ref, out_ref, wide
):
    section = lax.axis_index("sec")
    me = lax.axis_index("dev")
    columns = len(order)
    per_device = table.shape[2] // (sections - 1)
    list_start = section * per_device
    half = w_ref.shape[1]
    lane = lax.broadcasted_iota(jnp.int32, (8, LANES), 1)
    wide[...] = jnp.zeros(wide.shape, jnp.float32)

    def place(ref, n, slot):
        for column in range(columns):
            if order.index(column) % per_slab:
                continue
            at = slab_of(order, column, section, per_slab)
            tile = ref[column, n]
            for h in range(slab // 8):
                w = unpack(tile, h, snaps, lane)
                w1 = w.astype(jnp.bfloat16).astype(jnp.float32)
                w2 = (w - w1).astype(jnp.bfloat16).astype(jnp.float32)
                start = pl.multiple_of(slot * LANES + at * slab + 8 * h, 8)
                wide[pl.ds(start, 8), :] = w1 + pltpu.roll(w2, snaps, 1)

    def row(d, n):
        def earlier(m, c):
            return c + jnp.where(table[d, 1, m] == me, 1, 0)

        count = lax.fori_loop(0, list_start, earlier, 0)
        for i in range(per_device):
            mine = table[d, 1, list_start + i] == me
            slot = d * CAP + count

            @pl.when(jnp.logical_and(mine, n < half))
            def _(n=n, slot=slot):
                place(w_ref, n, slot)

            @pl.when(jnp.logical_and(mine, n >= half))
            def _(n=n, slot=slot):
                place(over_ref, n - half, slot)

            step = jnp.where(mine, 1, 0)
            n, count = n + step, count + step
        return n

    lax.fori_loop(0, columns, row, 0)
    both = wide[...].astype(jnp.bfloat16)
    dot = functools.partial(
        lax.dot_general,
        dimension_numbers=(((0,), (0,)), ((), ())),
        preferred_element_type=jnp.float32,
    )
    cross = dot(both, s_ref[...])
    cross = cross[:snaps] + cross[snaps:]
    inner = dot(both, both)
    inner = inner[:snaps, :] + inner[snaps:, :]
    inner = inner + pltpu.roll(inner, snaps, 1)
    strips = cross.shape[1] // LANES
    share = out_ref.shape[1]
    for r in range(snaps // 8):
        here = slice(8 * r, 8 * r + 8)
        for c in range(strips):
            at = r * (strips + 1) + c
            out_ref[at // share, at % share] = cross[here, c * LANES : (c + 1) * LANES]
        at = r * (strips + 1) + strips
        out_ref[at // share, at % share] = inner[here, :]


def three(x):
    x1 = x.astype(jnp.bfloat16)
    rest = x - x1.astype(jnp.float32)
    x2 = rest.astype(jnp.bfloat16)
    return x1, x2, (rest - x2.astype(jnp.float32)).astype(jnp.bfloat16)


def reciprocal(x):
    guess = pl.reciprocal(x, approx=True)
    return guess * (2.0 - x * guess)


def factor_block(d, e, sub, lane, spread):
    tiles = len(d)

    def wide(x):
        return jnp.broadcast_to(x, (8, LANES))

    def stack(values):
        out = values[0]
        for j in range(1, 8):
            out = jnp.where(sub == j, values[j], out)
        return out

    for p in range(tiles):
        first = 8 * p
        cols = [wide(d[p][:, first + j : first + j + 1]) for j in range(8)]
        base = 80 * (p % 2)
        for k, value in enumerate(cols + [d[p], e[p]]):
            spread[base + 8 * k : base + 8 * k + 8, :] = value

        def row(k, j, base=base):
            return spread[pl.ds(base + 8 * k + j, 8, stride=0), :]

        s = [[row(k, j) if k >= j else None for k in range(8)] for j in range(8)]
        t = [row(8, j) for j in range(8)]
        te = [row(9, j) for j in range(8)]
        inv, m = [], [[None] * 8 for _ in range(8)]
        for j in range(0, 8, 2):
            n = j + 1
            a, b, c = s[j][j], s[j][n], s[n][n]
            det = a * c - b * b
            inv_a, inv_det = reciprocal(a), reciprocal(det)
            inv += [inv_a, a * inv_det]
            m[j][n] = b * inv_a
            s[n][n] = det * inv_a
            t[n] = t[n] - m[j][n] * t[j]
            te[n] = te[n] - m[j][n] * te[j]
            for k in range(j + 2, 8):
                m[j][k] = s[j][k] * inv_a
                m[n][k] = (a * s[n][k] - b * s[j][k]) * inv_det
                s[n][k] = s[n][k] - m[j][n] * s[j][k]
            for k in range(j + 2, 8):
                for i in range(k, 8):
                    s[k][i] = (s[k][i] - m[j][k] * s[j][i]) - m[n][k] * s[n][i]
                t[k] = (t[k] - m[j][k] * t[j]) - m[n][k] * t[n]
                te[k] = (te[k] - m[j][k] * te[j]) - m[n][k] * te[n]
        if p + 1 < tiles:
            z, ze = [None] * 8, [None] * 8
            for j in reversed(range(8)):
                z[j], ze[j] = t[j] * inv[j], te[j] * inv[j]
                for k in range(j + 1, 8):
                    z[j] = z[j] - m[j][k] * z[k]
                    ze[j] = ze[j] - m[j][k] * ze[k]
            i = p + 1
            parts, parts_e = [], []
            for j in range(8):
                col = wide(d[i][:, first + j : first + j + 1])
                parts.append(col * z[j])
                parts_e.append(col * ze[j])
            while len(parts) > 1:
                parts = [x + y for x, y in zip(parts[::2], parts[1::2])]
                parts_e = [x + y for x, y in zip(parts_e[::2], parts_e[1::2])]
            if p + 2 < tiles:
                p1, p2, p3 = three(d[p])
                z1, z2, z3 = three(jnp.concatenate([stack(z), stack(ze)], axis=1))
                change = lax.dot_general(
                    jnp.concatenate([p1, p1, p1, p2, p2, p3], axis=0),
                    jnp.concatenate([z1, z2, z3, z1, z2, z1], axis=0),
                    (((0,), (0,)), ((), ())),
                    preferred_element_type=jnp.float32,
                )
                for n in range(p + 2, tiles):
                    d[n] = d[n] - change[8 * n : 8 * n + 8, :LANES]
                    e[n] = e[n] - change[8 * n : 8 * n + 8, LANES:]
            d[i], e[i] = d[i] - parts[0], e[i] - parts_e[0]
        roots = [lax.rsqrt(s[j][j]) for j in range(8)]
        d[p] = jnp.where(lane >= sub + first, stack([t[j] * roots[j] for j in range(8)]), 0.0)
        e[p] = stack([te[j] * roots[j] for j in range(8)])
    return jnp.concatenate(d, axis=0), jnp.concatenate(e, axis=0)


def factor_kernel(scale, sections, *refs):
    factor_ref = refs[3]
    analysis = lax.axis_index("sec") == sections - 1

    @pl.when(analysis)
    def _():
        factorize(scale, *refs)

    @pl.when(jnp.logical_not(analysis))
    def _():
        factor_ref[...] = jnp.zeros(factor_ref.shape, jnp.float32)


def factorize(
    scale, parts_ref, omega_ref, s_ref, factor_ref, inverse_ref, g, inner_ref, spread
):
    rank = s_ref.shape[0]
    snaps = omega_ref.shape[0]
    strips = rank // LANES
    rows_first = (((0,), (0,)), ((), ()))

    def band(r, c):
        return parts_ref[r * (strips + 1) + c]

    cross = jnp.concatenate(
        [
            jnp.concatenate([band(r, c) for c in range(strips)], axis=1)
            for r in range(snaps // 8)
        ],
        axis=0,
    )
    inner = jnp.concatenate([band(r, strips) for r in range(snaps // 8)], axis=0)
    omega = omega_ref[...]
    half = cross + 0.5 * jnp.dot(
        inner[:, :snaps], omega, precision=highest, preferred_element_type=jnp.float32
    )
    left = jnp.concatenate([half, omega], axis=0)
    right = jnp.concatenate([omega, half], axis=0)
    g[...] = s_ref[...] + lax.dot_general(
        left, right, rows_first, precision=highest, preferred_element_type=jnp.float32
    )
    inverse_ref[...] = jnp.zeros(inverse_ref.shape, jnp.float32)
    inner_ref[...] = jnp.zeros(inner_ref.shape, jnp.float32)
    factor_ref[...] = jnp.zeros(factor_ref.shape, jnp.float32)
    sub = lax.broadcasted_iota(jnp.int32, (8, LANES), 0)
    lane = lax.broadcasted_iota(jnp.int32, (8, LANES), 1)
    tiles = LANES // 8

    def rows_of(k):
        return slice(k * LANES, (k + 1) * LANES)

    for k in range(strips):
        here = rows_of(k)
        d = [g[k * LANES + 8 * i : k * LANES + 8 * i + 8, here] for i in range(tiles)]
        e = [jnp.where(lane == sub + 8 * i, 1.0, 0.0) for i in range(tiles)]
        upper, small = factor_block(d, e, sub, lane, spread.at[k % 2])
        factor_ref[here, here] = upper * (1.0 / scale)
        small_rows = [small]
        if k + 1 < strips:
            right = slice((k + 1) * LANES, rank)
            fresh = jnp.dot(
                small, g[here, right], precision=highest, preferred_element_type=jnp.float32
            )
            factor_ref[here, right] = fresh * (1.0 / scale)
            change = functools.partial(
                lax.dot_general,
                dimension_numbers=rows_first,
                precision=highest,
                preferred_element_type=jnp.float32,
            )
            following = rows_of(k + 1)
            g[following, right] = g[following, right] - change(fresh[:, :LANES], fresh)
            if k + 2 < strips:
                later = slice((k + 2) * LANES, rank)
                g[later, later] = g[later, later] - change(fresh[:, LANES:], fresh[:, LANES:])
        if k:
            left = slice(0, k * LANES)
            small_rows = [
                jnp.dot(
                    small, inner_ref[here, left], precision=highest,
                    preferred_element_type=jnp.float32,
                ),
                small,
            ]
        done = jnp.concatenate(small_rows, axis=1)
        if k + 1 < strips:
            upto = slice(0, (k + 1) * LANES)
            inner_ref[right, upto] = inner_ref[right, upto] - change(fresh, done)
        inverse_ref[0 : (k + 1) * LANES, here] = (done * scale).T


def basis_kernel(sections, inverse_ref, omega_ref, s_ref, *rest):
    pieces, out_ref, stack = rest[:-2], rest[-2], rest[-1]
    analysis = lax.axis_index("sec") == sections - 1
    rank, snaps = inverse_ref.shape[0], omega_ref.shape[0]
    band = 2 * LANES
    dot = functools.partial(jnp.dot, preferred_element_type=jnp.float32)

    @pl.when(jnp.logical_and(analysis, pl.program_id(0) == 0))
    def _():
        def split(x):
            high = x.astype(jnp.bfloat16)
            return high, (x - high.astype(jnp.float32)).astype(jnp.bfloat16)

        inverse = inverse_ref[...]
        mixed = dot(omega_ref[...], inverse, precision=highest)
        x1, x2 = split(inverse)
        m1, m2 = split(jnp.concatenate([mixed, mixed], axis=0))
        for to in range(band, rank + 1, band):
            cols = slice(to - band, to)
            stack[: 2 * to + 4 * snaps, cols] = jnp.concatenate(
                [x1[:to, cols], x2[:to, cols], m1[:, cols], m2[:, cols]], axis=0
            )

    @pl.when(analysis)
    def _():
        s = s_ref[...]
        w = pieces[0][...]
        for piece in pieces[1:]:
            w = w + piece[...]
        w = w.astype(jnp.bfloat16)
        for to in range(band, rank + 1, band):
            left = jnp.concatenate([s[:, :to], s[:, :to], w, w], axis=1)
            q = dot(left, stack[: 2 * to + 4 * snaps, to - band : to])
            out_ref[:, to - band : to] = q.astype(jnp.bfloat16)

    @pl.when(jnp.logical_not(analysis))
    def _():
        out_ref[...] = jnp.zeros(out_ref.shape, jnp.bfloat16)


def shards(potential, previous, wave_coeff, sketch_in, omega, blocks, owners):
    sections = lax.axis_size("sec")
    columns = lax.axis_size("dev")
    devices = sections * columns
    extent_x, extent_y, depth = potential.shape
    list_width = owners.shape[1]
    per_device = list_width // (sections - 1)
    snaps, rank = omega.shape
    slab = max(8, depth // columns)
    per_slab = slab * columns // depth
    slots = columns * CAP
    order = neighbour_path(columns)
    path = []
    for section in range(sections - 1):
        path += [section * columns + d for d in (order if section % 2 == 0 else order[::-1])]
    up = [(path[i], path[i + per_slab]) for i in range(len(path) - per_slab)]
    down = [(b, a) for a, b in up]
    f32 = jnp.float32

    analysis = lax.axis_index("sec") == sections - 1

    def whole_gram():
        own = lax.dot_general(
            sketch_in, sketch_in, (((0,), (0,)), ((), ())), preferred_element_type=f32
        )
        own = own.reshape(columns, rank // columns, rank)
        own = lax.all_to_all(own, "dev", split_axis=0, concat_axis=0, tiled=True)
        own = jnp.broadcast_to(jnp.sum(own, axis=0)[None], own.shape)
        own = lax.all_to_all(own, "dev", split_axis=0, concat_axis=0, tiled=True)
        return own.reshape(rank, rank)

    scaled = omega * jnp.asarray(
        decay ** np.arange(1, snaps + 1, dtype=np.float64), f32
    )[:, None]

    chunk = 6 * slab + 8
    operands = (potential, previous, wave_coeff, blocks, owners)
    outgoing = pl.pallas_call(
        functools.partial(split_kernel, order, slab, per_slab),
        out_shape=jax.ShapeDtypeStruct((columns, chunk, LANES), f32),
        in_specs=vmem(*operands),
        out_specs=pl.BlockSpec(memory_space=pltpu.VMEM),
        scratch_shapes=[pltpu.VMEM((6, depth, LANES), f32)],
        compiler_params=big(),
    )(*operands)
    raw = lax.all_to_all(outgoing, "dev", split_axis=0, concat_axis=0, tiled=True)
    gram, scaled, raw = lax.optimization_barrier(
        (lax.cond(analysis, whole_gram, lambda: jnp.zeros((rank, rank), f32)), scaled, raw)
    )
    table = raw[:, 6 * slab : 6 * slab + 2, :list_width].astype(jnp.int32)

    def sides(x):
        return lax.ppermute(x, BOTH, up), x, lax.ppermute(x, BOTH, down)

    fields = sides(raw)
    state = fields
    held = jnp.zeros((columns * per_device, 8, LANES), f32)
    rounds = snaps // slab
    for number in range(rounds):
        last = number == rounds - 1
        operands = (table, *fields, *state, held)
        sent = jax.ShapeDtypeStruct((columns, slots // 2, 8, LANES), f32)
        flag = jax.ShapeDtypeStruct((1,), jnp.int32)
        result = [sent, sent, flag] if last else [jax.ShapeDtypeStruct((columns, 4 * slab, LANES), f32)]
        *moved, held = pl.pallas_call(
            functools.partial(
                steps_kernel, number * slab, slab, per_device, last, snaps, sections
            ),
            out_shape=(*result, jax.ShapeDtypeStruct(held.shape, f32)),
            in_specs=[pl.BlockSpec(memory_space=pltpu.SMEM)] + vmem(*operands[1:]),
            out_specs=tuple(
                pl.BlockSpec(memory_space=pltpu.SMEM if x.dtype == jnp.int32 else pltpu.VMEM)
                for x in (*result, held)
            ),
            scratch_shapes=[pltpu.VMEM((2 * columns, 3 * slab + 16, LANES), f32)] * 2
            + [pltpu.VMEM((2 * columns, 3 * slab, LANES), f32)] * 2
            + [pltpu.SMEM((columns,), jnp.int32)] * last,
            compiler_params=big(),
        )(*operands)
        if not last:
            state = sides(moved[0])

    def trade(x):
        return lax.all_to_all(x, "dev", split_axis=0, concat_axis=0, tiled=True)

    arrived = trade(moved[0])
    over = lax.cond(moved[2][0] > 0, trade, lambda x: x, moved[1])
    operands = (table, arrived, over, sketch_in)
    bands = (snaps // 8) * (rank // LANES + 1)
    share = -(-bands // columns)
    parts, wide = pl.pallas_call(
        functools.partial(product_kernel, order, slab, per_slab, snaps, sections),
        out_shape=(
            jax.ShapeDtypeStruct((columns, share, 8, LANES), f32),
            jax.ShapeDtypeStruct((slots * depth, LANES), f32),
        ),
        in_specs=[pl.BlockSpec(memory_space=pltpu.SMEM)] + vmem(*operands[1:]),
        out_specs=tuple(vmem(0, 0)),
        compiler_params=big(60),
    )(*operands)

    def to_analysis(x):
        return [lax.ppermute(x, "sec", [(i, sections - 1)]) for i in range(sections - 1)]

    terms = lax.all_to_all(parts, "dev", split_axis=0, concat_axis=0, tiled=True)
    total = jnp.sum(terms, axis=0)
    terms = to_analysis(total)
    wide, *terms = lax.optimization_barrier((wide, *terms))
    pieces = to_analysis(wide)

    def exchange(terms):
        total = jnp.broadcast_to(sum(terms[1:], terms[0])[None], parts.shape)
        return lax.all_to_all(total, "dev", split_axis=0, concat_axis=0, tiled=True)

    sums = lax.cond(analysis, exchange, lambda terms: jnp.zeros(parts.shape, f32), terms)
    sums = sums.reshape(columns * share, 8, LANES)

    scale = math.sqrt(columns * columns * CAP * depth)
    operands = (sums, scaled, gram)
    factor, inverse = pl.pallas_call(
        functools.partial(factor_kernel, scale, sections),
        out_shape=(jax.ShapeDtypeStruct((rank, rank), f32),) * 2,
        in_specs=vmem(*operands),
        out_specs=tuple(vmem(0, 0)),
        scratch_shapes=[pltpu.VMEM((rank, rank), f32)] * 2 + [pltpu.VMEM((2, 160, LANES), f32)],
        compiler_params=big(),
    )(*operands)
    operands = (inverse, scaled, sketch_in, *pieces)
    rows = 512

    def whole(x):
        return pl.BlockSpec(x.shape, lambda i: (0, 0))

    def strip(x):
        return pl.BlockSpec((rows, x.shape[1]), lambda i: (i, 0))

    basis = pl.pallas_call(
        functools.partial(basis_kernel, sections),
        out_shape=jax.ShapeDtypeStruct(sketch_in.shape, jnp.bfloat16),
        grid=(sketch_in.shape[0] // rows,),
        in_specs=[whole(inverse), whole(scaled), strip(sketch_in)] + [strip(x) for x in pieces],
        out_specs=strip(sketch_in),
        scratch_shapes=[pltpu.VMEM((2 * rank + 4 * snaps, rank), jnp.bfloat16)],
        compiler_params=big(60),
    )(*operands)
    return (basis[None], factor[None])


def solution(mesh):
    placed = (
        P("dev", None, "sec"),
        P("dev", None, "sec"),
        P("dev", None, "sec"),
        P("dev", None),
        P(),
        P("dev", None),
        P("dev", None),
    )
    return jax.shard_map(
        shards,
        mesh=mesh,
        in_specs=placed,
        out_specs=(P("sec", "dev", None), P("sec", None, None)),
        check_vma=False,
    )
```

```python
import functools
import math

import jax
import jax.numpy as jnp
import numpy as np
from jax import lax
from jax.experimental import pallas as pl
from jax.experimental.pallas import tpu as pltpu
from jax.sharding import PartitionSpec as P

CAP = 2
damping = 0.05
LANES = 128
highest = lax.Precision.HIGHEST
decay = math.sqrt(1.0 - damping)
BOTH = ("sec", "dev")


def neighbour_path(columns):
    order = []
    for i in range(0, columns, 2):
        pair = [i, i + 1]
        order += pair if (i // 2) % 2 == 0 else pair[::-1]
    return order


def vmem(*arrays):
    return [pl.BlockSpec(memory_space=pltpu.VMEM)] * len(arrays)


def big(limit=48):
    return pltpu.CompilerParams(vmem_limit_bytes=limit << 20)


def slab_of(order, column, section, per_slab):
    place = order.index(column)
    forward, backward = place // per_slab, (len(order) - 1 - place) // per_slab
    return jnp.where(section % 2 == 0, forward, backward)


def split_kernel(order, slab, per_slab, u_ref, e_ref, k_ref, blocks_ref, owners_ref, out_ref, turned):
    section = lax.axis_index("sec")
    extent_x, extent_y, depth = u_ref.shape
    for a, ref in enumerate((u_ref, e_ref, k_ref)):
        for p in range(2):
            rows = jnp.concatenate([ref[x] for x in range(p, extent_x, 2)], axis=0)
            if a == 1:
                rows = rows * decay
            turned[2 * a + p] = rows.T
    for column in range(len(order)):
        at = slab_of(order, column, section, per_slab)
        start = pl.multiple_of(at * slab, 8)
        for q in range(6):
            out_ref[column, q * slab : (q + 1) * slab, :] = turned[q, pl.ds(start, slab), :]
        for r, ref in enumerate((blocks_ref, owners_ref)):
            out_ref[column, 6 * slab + r : 6 * slab + r + 1, : ref.shape[1]] = ref[...].astype(
                jnp.float32
            )


def steps_kernel(*args):
    last, sections = args[3], args[5]
    if last:
        flag_ref = args[16]
        flag_ref[0] = 0

    @pl.when(lax.axis_index("sec") < sections - 1)
    def _():
        evolve(*args)


def evolve(
    first_step, slab, per_device, last, snaps, sections,
    table, kl, kc, kr, sl, sc, sr, w_in, *rest,
):
    if last:
        send_ref, over_ref, flag_ref, w_ref, field_a, field_b, gain, own, used = rest
    else:
        state_ref, w_ref, field_a, field_b, gain, own = rest
    list_start = lax.axis_index("sec") * per_device
    columns = kc.shape[0]
    rows = 3 * slab
    lane = lax.broadcasted_iota(jnp.int32, (8, LANES), 1)
    y_first, y_last = lane % 32 == 0, lane % 32 == 31
    zero = jnp.zeros((8, LANES), jnp.float32)

    for o in range(2 * columns):
        d, p = o // 2, o % 2
        for field, at in ((field_a, p), (field_b, 2 + p)):
            field[o, 0:8, :] = zero
            field[o, 8 + rows : 16 + rows, :] = zero
            for h, ref in enumerate((sl, sc, sr)):
                field[o, 8 + h * slab : 8 + (h + 1) * slab, :] = ref[
                    d, at * slab : (at + 1) * slab, :
                ]
        for h, ref in enumerate((kl, kc, kr)):
            k = ref[d, (4 + p) * slab : (5 + p) * slab, :]
            gain[o, h * slab : (h + 1) * slab, :] = k * (1.0 / decay)
            own[o, h * slab : (h + 1) * slab, :] = ((2.0 - damping) - 6.0 * k) * (1.0 / decay)
    w_ref[...] = w_in[...]

    def step(src, dst, tiles, number):
        for z in tiles:
            at = slice(8 + 8 * z, 16 + 8 * z)
            low = slice(7 + 8 * z, 15 + 8 * z)
            high = slice(9 + 8 * z, 17 + 8 * z)
            here = slice(8 * z, 8 * z + 8)
            values = [src[o, at, :] for o in range(2 * columns)]
            up = [pltpu.roll(values[2 * d + 1], 32, 1) for d in range(columns)]
            down = [pltpu.roll(values[2 * d], LANES - 32, 1) for d in range(columns)]
            for o in range(2 * columns):
                d, p = o // 2, o % 2
                v = values[o]
                if p == 0:
                    side = jnp.where(lane < 32, up[d - 1] if d > 0 else zero, up[d])
                    total = values[o + 1] + side
                else:
                    side = jnp.where(
                        lane >= LANES - 32, down[d + 1] if d + 1 < columns else zero, down[d]
                    )
                    total = values[o - 1] + side
                total = total + (src[o, low, :] + src[o, high, :])
                total = total + jnp.where(y_first, 0.0, pltpu.roll(v, 1, 1))
                total = total + jnp.where(y_last, 0.0, pltpu.roll(v, LANES - 1, 1))
                dst[o, at, :] = own[o, here, :] * v + gain[o, here, :] * total - dst[o, at, :]

        def column_blocks(d, carry):
            for i in range(per_device):
                block = table[d, 0, list_start + i]
                x, y = block >> 5, block & 31
                at_lane = ((x >> 1) << 5) + y
                o = 2 * d + (x & 1)
                j = d * per_device + i
                held = w_ref[j]
                for h in range(slab // 8):
                    target = h * snaps + number
                    value = dst[o, 8 + slab + 8 * h : 16 + slab + 8 * h, :]
                    moved = pltpu.roll(value, (target - at_lane) & (LANES - 1), 1)
                    held = jnp.where(lane == target, moved, held)
                w_ref[j] = held
            return carry

        lax.fori_loop(0, columns, column_blocks, 0, unroll=min(columns, 8))

    for phase in range(slab // 8):
        tiles = range(phase, 3 * slab // 8 - phase)

        def pair(m, carry):
            number = first_step + 8 * phase + 2 * m
            step(field_a, field_b, tiles, number)
            step(field_b, field_a, tiles, number + 1)
            return carry

        lax.fori_loop(0, 4, pair, 0)

    if last:
        half = send_ref.shape[1]
        for d in range(columns):
            used[d] = 0

        def place(d, carry):
            for i in range(per_device):
                mine = table[d, 1, list_start + i]
                n = used[mine]
                used[mine] = n + 1

                @pl.when(n < half)
                def _(i=i, mine=mine, n=n):
                    send_ref[mine, n] = w_ref[d * per_device + i]

                @pl.when(n >= half)
                def _(i=i, mine=mine, n=n):
                    over_ref[mine, n - half] = w_ref[d * per_device + i]

            return carry

        lax.fori_loop(0, columns, place, 0)
        for d in range(columns):
            flag_ref[0] = jnp.maximum(flag_ref[0], jnp.where(used[d] > half, 1, 0))
    else:
        for o in range(2 * columns):
            d, p = o // 2, o % 2
            state_ref[d, p * slab : (p + 1) * slab, :] = field_a[o, 8 + slab : 8 + 2 * slab, :]
            state_ref[d, (2 + p) * slab : (3 + p) * slab, :] = field_b[
                o, 8 + slab : 8 + 2 * slab, :
            ]


def unpack(tile, h, snaps, lane):
    if h:
        tile = pltpu.roll(tile, LANES - h * snaps, 1)
    return jnp.where(lane < snaps, tile, 0.0)


def product_kernel(*args):
    sections = args[4]

    @pl.when(lax.axis_index("sec") < sections - 1)
    def _():
        products(*args)


def products(
    order, slab, per_slab, snaps, sections, table, w_ref, over_ref, s_ref, out_ref, wide
):
    section = lax.axis_index("sec")
    me = lax.axis_index("dev")
    columns = len(order)
    per_device = table.shape[2] // (sections - 1)
    list_start = section * per_device
    half = w_ref.shape[1]
    lane = lax.broadcasted_iota(jnp.int32, (8, LANES), 1)
    wide[...] = jnp.zeros(wide.shape, jnp.float32)

    def place(ref, n, slot):
        for column in range(columns):
            if order.index(column) % per_slab:
                continue
            at = slab_of(order, column, section, per_slab)
            tile = ref[column, n]
            for h in range(slab // 8):
                w = unpack(tile, h, snaps, lane)
                w1 = w.astype(jnp.bfloat16).astype(jnp.float32)
                w2 = (w - w1).astype(jnp.bfloat16).astype(jnp.float32)
                start = pl.multiple_of(slot * LANES + at * slab + 8 * h, 8)
                wide[pl.ds(start, 8), :] = w1 + pltpu.roll(w2, snaps, 1)

    def row(d, n):
        def earlier(m, c):
            return c + jnp.where(table[d, 1, m] == me, 1, 0)

        count = lax.fori_loop(0, list_start, earlier, 0)
        for i in range(per_device):
            mine = table[d, 1, list_start + i] == me
            slot = d * CAP + count

            @pl.when(jnp.logical_and(mine, n < half))
            def _(n=n, slot=slot):
                place(w_ref, n, slot)

            @pl.when(jnp.logical_and(mine, n >= half))
            def _(n=n, slot=slot):
                place(over_ref, n - half, slot)

            step = jnp.where(mine, 1, 0)
            n, count = n + step, count + step
        return n

    lax.fori_loop(0, columns, row, 0)
    both = wide[...].astype(jnp.bfloat16)
    dot = functools.partial(
        lax.dot_general,
        dimension_numbers=(((0,), (0,)), ((), ())),
        preferred_element_type=jnp.float32,
    )
    cross = dot(both, s_ref[...])
    cross = cross[:snaps] + cross[snaps:]
    inner = dot(both, both)
    inner = inner[:snaps, :] + inner[snaps:, :]
    inner = inner + pltpu.roll(inner, snaps, 1)
    strips = cross.shape[1] // LANES
    share = out_ref.shape[1]
    for r in range(snaps // 8):
        here = slice(8 * r, 8 * r + 8)
        for c in range(strips):
            at = r * (strips + 1) + c
            out_ref[at // share, at % share] = cross[here, c * LANES : (c + 1) * LANES]
        at = r * (strips + 1) + strips
        out_ref[at // share, at % share] = inner[here, :]


def three(x):
    x1 = x.astype(jnp.bfloat16)
    rest = x - x1.astype(jnp.float32)
    x2 = rest.astype(jnp.bfloat16)
    return x1, x2, (rest - x2.astype(jnp.float32)).astype(jnp.bfloat16)


def reciprocal(x):
    guess = pl.reciprocal(x, approx=True)
    return guess * (2.0 - x * guess)


def factor_block(d, e, sub, lane, spread):
    tiles = len(d)

    def wide(x):
        return jnp.broadcast_to(x, (8, LANES))

    def stack(values):
        out = values[0]
        for j in range(1, 8):
            out = jnp.where(sub == j, values[j], out)
        return out

    for p in range(tiles):
        first = 8 * p
        cols = [wide(d[p][:, first + j : first + j + 1]) for j in range(8)]
        base = 80 * (p % 2)
        for k, value in enumerate(cols + [d[p], e[p]]):
            spread[base + 8 * k : base + 8 * k + 8, :] = value

        def row(k, j, base=base):
            return spread[pl.ds(base + 8 * k + j, 8, stride=0), :]

        s = [[row(k, j) if k >= j else None for k in range(8)] for j in range(8)]
        t = [row(8, j) for j in range(8)]
        te = [row(9, j) for j in range(8)]
        inv, m = [], [[None] * 8 for _ in range(8)]
        for j in range(0, 8, 2):
            n = j + 1
            a, b, c = s[j][j], s[j][n], s[n][n]
            det = a * c - b * b
            inv_a, inv_det = reciprocal(a), reciprocal(det)
            inv += [inv_a, a * inv_det]
            m[j][n] = b * inv_a
            s[n][n] = det * inv_a
            t[n] = t[n] - m[j][n] * t[j]
            te[n] = te[n] - m[j][n] * te[j]
            for k in range(j + 2, 8):
                m[j][k] = s[j][k] * inv_a
                m[n][k] = (a * s[n][k] - b * s[j][k]) * inv_det
                s[n][k] = s[n][k] - m[j][n] * s[j][k]
            for k in range(j + 2, 8):
                for i in range(k, 8):
                    s[k][i] = (s[k][i] - m[j][k] * s[j][i]) - m[n][k] * s[n][i]
                t[k] = (t[k] - m[j][k] * t[j]) - m[n][k] * t[n]
                te[k] = (te[k] - m[j][k] * te[j]) - m[n][k] * te[n]
        if p + 1 < tiles:
            z, ze = [None] * 8, [None] * 8
            for j in reversed(range(8)):
                z[j], ze[j] = t[j] * inv[j], te[j] * inv[j]
                for k in range(j + 1, 8):
                    z[j] = z[j] - m[j][k] * z[k]
                    ze[j] = ze[j] - m[j][k] * ze[k]
            i = p + 1
            parts, parts_e = [], []
            for j in range(8):
                col = wide(d[i][:, first + j : first + j + 1])
                parts.append(col * z[j])
                parts_e.append(col * ze[j])
            while len(parts) > 1:
                parts = [x + y for x, y in zip(parts[::2], parts[1::2])]
                parts_e = [x + y for x, y in zip(parts_e[::2], parts_e[1::2])]
            if p + 2 < tiles:
                p1, p2, p3 = three(d[p])
                z1, z2, z3 = three(jnp.concatenate([stack(z), stack(ze)], axis=1))
                change = lax.dot_general(
                    jnp.concatenate([p1, p1, p1, p2, p2, p3], axis=0),
                    jnp.concatenate([z1, z2, z3, z1, z2, z1], axis=0),
                    (((0,), (0,)), ((), ())),
                    preferred_element_type=jnp.float32,
                )
                for n in range(p + 2, tiles):
                    d[n] = d[n] - change[8 * n : 8 * n + 8, :LANES]
                    e[n] = e[n] - change[8 * n : 8 * n + 8, LANES:]
            d[i], e[i] = d[i] - parts[0], e[i] - parts_e[0]
        roots = [lax.rsqrt(s[j][j]) for j in range(8)]
        d[p] = jnp.where(lane >= sub + first, stack([t[j] * roots[j] for j in range(8)]), 0.0)
        e[p] = stack([te[j] * roots[j] for j in range(8)])
    return jnp.concatenate(d, axis=0), jnp.concatenate(e, axis=0)


def factor_kernel(scale, sections, *refs):
    factor_ref = refs[3]
    analysis = lax.axis_index("sec") == sections - 1

    @pl.when(analysis)
    def _():
        factorize(scale, *refs)

    @pl.when(jnp.logical_not(analysis))
    def _():
        factor_ref[...] = jnp.zeros(factor_ref.shape, jnp.float32)


def factorize(
    scale, parts_ref, omega_ref, s_ref, factor_ref, inverse_ref, g, inner_ref, spread
):
    rank = s_ref.shape[0]
    snaps = omega_ref.shape[0]
    strips = rank // LANES
    rows_first = (((0,), (0,)), ((), ()))

    def band(r, c):
        return parts_ref[r * (strips + 1) + c]

    cross = jnp.concatenate(
        [
            jnp.concatenate([band(r, c) for c in range(strips)], axis=1)
            for r in range(snaps // 8)
        ],
        axis=0,
    )
    inner = jnp.concatenate([band(r, strips) for r in range(snaps // 8)], axis=0)
    omega = omega_ref[...]
    half = cross + 0.5 * jnp.dot(
        inner[:, :snaps], omega, precision=highest, preferred_element_type=jnp.float32
    )
    left = jnp.concatenate([half, omega], axis=0)
    right = jnp.concatenate([omega, half], axis=0)
    g[...] = s_ref[...] + lax.dot_general(
        left, right, rows_first, precision=highest, preferred_element_type=jnp.float32
    )
    inverse_ref[...] = jnp.zeros(inverse_ref.shape, jnp.float32)
    inner_ref[...] = jnp.zeros(inner_ref.shape, jnp.float32)
    factor_ref[...] = jnp.zeros(factor_ref.shape, jnp.float32)
    sub = lax.broadcasted_iota(jnp.int32, (8, LANES), 0)
    lane = lax.broadcasted_iota(jnp.int32, (8, LANES), 1)
    tiles = LANES // 8

    def rows_of(k):
        return slice(k * LANES, (k + 1) * LANES)

    for k in range(strips):
        here = rows_of(k)
        d = [g[k * LANES + 8 * i : k * LANES + 8 * i + 8, here] for i in range(tiles)]
        e = [jnp.where(lane == sub + 8 * i, 1.0, 0.0) for i in range(tiles)]
        upper, small = factor_block(d, e, sub, lane, spread.at[k % 2])
        factor_ref[here, here] = upper * (1.0 / scale)
        small_rows = [small]
        if k + 1 < strips:
            right = slice((k + 1) * LANES, rank)
            fresh = jnp.dot(
                small, g[here, right], precision=highest, preferred_element_type=jnp.float32
            )
            factor_ref[here, right] = fresh * (1.0 / scale)
            change = functools.partial(
                lax.dot_general,
                dimension_numbers=rows_first,
                precision=highest,
                preferred_element_type=jnp.float32,
            )
            following = rows_of(k + 1)
            g[following, right] = g[following, right] - change(fresh[:, :LANES], fresh)
            if k + 2 < strips:
                later = slice((k + 2) * LANES, rank)
                g[later, later] = g[later, later] - change(fresh[:, LANES:], fresh[:, LANES:])
        if k:
            left = slice(0, k * LANES)
            small_rows = [
                jnp.dot(
                    small, inner_ref[here, left], precision=highest,
                    preferred_element_type=jnp.float32,
                ),
                small,
            ]
        done = jnp.concatenate(small_rows, axis=1)
        if k + 1 < strips:
            upto = slice(0, (k + 1) * LANES)
            inner_ref[right, upto] = inner_ref[right, upto] - change(fresh, done)
        inverse_ref[0 : (k + 1) * LANES, here] = (done * scale).T


def basis_kernel(sections, inverse_ref, omega_ref, s_ref, *rest):
    pieces, out_ref, stack = rest[:-2], rest[-2], rest[-1]
    analysis = lax.axis_index("sec") == sections - 1
    rank, snaps = inverse_ref.shape[0], omega_ref.shape[0]
    band = 2 * LANES
    dot = functools.partial(jnp.dot, preferred_element_type=jnp.float32)

    @pl.when(jnp.logical_and(analysis, pl.program_id(0) == 0))
    def _():
        def split(x):
            high = x.astype(jnp.bfloat16)
            return high, (x - high.astype(jnp.float32)).astype(jnp.bfloat16)

        inverse = inverse_ref[...]
        mixed = dot(omega_ref[...], inverse, precision=highest)
        x1, x2 = split(inverse)
        m1, m2 = split(jnp.concatenate([mixed, mixed], axis=0))
        for to in range(band, rank + 1, band):
            cols = slice(to - band, to)
            stack[: 2 * to + 4 * snaps, cols] = jnp.concatenate(
                [x1[:to, cols], x2[:to, cols], m1[:, cols], m2[:, cols]], axis=0
            )

    @pl.when(analysis)
    def _():
        s = s_ref[...]
        w = pieces[0][...]
        for piece in pieces[1:]:
            w = w + piece[...]
        w = w.astype(jnp.bfloat16)
        for to in range(band, rank + 1, band):
            left = jnp.concatenate([s[:, :to], s[:, :to], w, w], axis=1)
            q = dot(left, stack[: 2 * to + 4 * snaps, to - band : to])
            out_ref[:, to - band : to] = q.astype(jnp.bfloat16)

    @pl.when(jnp.logical_not(analysis))
    def _():
        out_ref[...] = jnp.zeros(out_ref.shape, jnp.bfloat16)


def shards(potential, previous, wave_coeff, sketch_in, omega, blocks, owners):
    sections = lax.axis_size("sec")
    columns = lax.axis_size("dev")
    devices = sections * columns
    extent_x, extent_y, depth = potential.shape
    list_width = owners.shape[1]
    per_device = list_width // (sections - 1)
    snaps, rank = omega.shape
    slab = max(8, depth // columns)
    per_slab = slab * columns // depth
    slots = columns * CAP
    order = neighbour_path(columns)
    path = []
    for section in range(sections - 1):
        path += [section * columns + d for d in (order if section % 2 == 0 else order[::-1])]
    up = [(path[i], path[i + per_slab]) for i in range(len(path) - per_slab)]
    down = [(b, a) for a, b in up]
    f32 = jnp.float32

    analysis = lax.axis_index("sec") == sections - 1

    def whole_gram():
        own = lax.dot_general(
            sketch_in, sketch_in, (((0,), (0,)), ((), ())), preferred_element_type=f32
        )
        own = own.reshape(columns, rank // columns, rank)
        own = lax.all_to_all(own, "dev", split_axis=0, concat_axis=0, tiled=True)
        own = jnp.broadcast_to(jnp.sum(own, axis=0)[None], own.shape)
        own = lax.all_to_all(own, "dev", split_axis=0, concat_axis=0, tiled=True)
        return own.reshape(rank, rank)

    scaled = omega * jnp.asarray(
        decay ** np.arange(1, snaps + 1, dtype=np.float64), f32
    )[:, None]

    chunk = 6 * slab + 8
    operands = (potential, previous, wave_coeff, blocks, owners)
    outgoing = pl.pallas_call(
        functools.partial(split_kernel, order, slab, per_slab),
        out_shape=jax.ShapeDtypeStruct((columns, chunk, LANES), f32),
        in_specs=vmem(*operands),
        out_specs=pl.BlockSpec(memory_space=pltpu.VMEM),
        scratch_shapes=[pltpu.VMEM((6, depth, LANES), f32)],
        compiler_params=big(),
    )(*operands)
    raw = lax.all_to_all(outgoing, "dev", split_axis=0, concat_axis=0, tiled=True)
    gram, scaled, raw = lax.optimization_barrier(
        (lax.cond(analysis, whole_gram, lambda: jnp.zeros((rank, rank), f32)), scaled, raw)
    )
    table = raw[:, 6 * slab : 6 * slab + 2, :list_width].astype(jnp.int32)

    def sides(x):
        return lax.ppermute(x, BOTH, up), x, lax.ppermute(x, BOTH, down)

    fields = sides(raw)
    state = fields
    held = jnp.zeros((columns * per_device, 8, LANES), f32)
    rounds = snaps // slab
    for number in range(rounds):
        last = number == rounds - 1
        operands = (table, *fields, *state, held)
        sent = jax.ShapeDtypeStruct((columns, slots // 2, 8, LANES), f32)
        flag = jax.ShapeDtypeStruct((1,), jnp.int32)
        result = [sent, sent, flag] if last else [jax.ShapeDtypeStruct((columns, 4 * slab, LANES), f32)]
        *moved, held = pl.pallas_call(
            functools.partial(
                steps_kernel, number * slab, slab, per_device, last, snaps, sections
            ),
            out_shape=(*result, jax.ShapeDtypeStruct(held.shape, f32)),
            in_specs=[pl.BlockSpec(memory_space=pltpu.SMEM)] + vmem(*operands[1:]),
            out_specs=tuple(
                pl.BlockSpec(memory_space=pltpu.SMEM if x.dtype == jnp.int32 else pltpu.VMEM)
                for x in (*result, held)
            ),
            scratch_shapes=[pltpu.VMEM((2 * columns, 3 * slab + 16, LANES), f32)] * 2
            + [pltpu.VMEM((2 * columns, 3 * slab, LANES), f32)] * 2
            + [pltpu.SMEM((columns,), jnp.int32)] * last,
            compiler_params=big(),
        )(*operands)
        if not last:
            state = sides(moved[0])

    def trade(x):
        return lax.all_to_all(x, "dev", split_axis=0, concat_axis=0, tiled=True)

    arrived = trade(moved[0])
    over = lax.cond(moved[2][0] > 0, trade, lambda x: x, moved[1])
    operands = (table, arrived, over, sketch_in)
    bands = (snaps // 8) * (rank // LANES + 1)
    share = -(-bands // columns)
    parts, wide = pl.pallas_call(
        functools.partial(product_kernel, order, slab, per_slab, snaps, sections),
        out_shape=(
            jax.ShapeDtypeStruct((columns, share, 8, LANES), f32),
            jax.ShapeDtypeStruct((slots * depth, LANES), f32),
        ),
        in_specs=[pl.BlockSpec(memory_space=pltpu.SMEM)] + vmem(*operands[1:]),
        out_specs=tuple(vmem(0, 0)),
        compiler_params=big(60),
    )(*operands)

    def to_analysis(x):
        return [lax.ppermute(x, "sec", [(i, sections - 1)]) for i in range(sections - 1)]

    terms = lax.all_to_all(parts, "dev", split_axis=0, concat_axis=0, tiled=True)
    total = jnp.sum(terms, axis=0)
    terms = to_analysis(total)
    wide, *terms = lax.optimization_barrier((wide, *terms))
    pieces = to_analysis(wide)

    def exchange(terms):
        total = jnp.broadcast_to(sum(terms[1:], terms[0])[None], parts.shape)
        return lax.all_to_all(total, "dev", split_axis=0, concat_axis=0, tiled=True)

    sums = lax.cond(analysis, exchange, lambda terms: jnp.zeros(parts.shape, f32), terms)
    sums = sums.reshape(columns * share, 8, LANES)

    scale = math.sqrt(columns * columns * CAP * depth)
    operands = (sums, scaled, gram)
    factor, inverse = pl.pallas_call(
        functools.partial(factor_kernel, scale, sections),
        out_shape=(jax.ShapeDtypeStruct((rank, rank), f32),) * 2,
        in_specs=vmem(*operands),
        out_specs=tuple(vmem(0, 0)),
        scratch_shapes=[pltpu.VMEM((rank, rank), f32)] * 2 + [pltpu.VMEM((2, 160, LANES), f32)],
        compiler_params=big(),
    )(*operands)
    operands = (inverse, scaled, sketch_in, *pieces)
    rows = 1024

    def whole(x):
        return pl.BlockSpec(x.shape, lambda i: (0, 0))

    def strip(x):
        return pl.BlockSpec((rows, x.shape[1]), lambda i: (i, 0))

    basis = pl.pallas_call(
        functools.partial(basis_kernel, sections),
        out_shape=jax.ShapeDtypeStruct(sketch_in.shape, jnp.bfloat16),
        grid=(sketch_in.shape[0] // rows,),
        in_specs=[whole(inverse), whole(scaled), strip(sketch_in)] + [strip(x) for x in pieces],
        out_specs=strip(sketch_in),
        scratch_shapes=[pltpu.VMEM((2 * rank + 4 * snaps, rank), jnp.bfloat16)],
        compiler_params=big(60),
    )(*operands)
    return (basis[None], factor[None])


def solution(mesh):
    placed = (
        P("dev", None, "sec"),
        P("dev", None, "sec"),
        P("dev", None, "sec"),
        P("dev", None),
        P(),
        P("dev", None),
        P("dev", None),
    )
    return jax.shard_map(
        shards,
        mesh=mesh,
        in_specs=placed,
        out_specs=(P("sec", "dev", None), P("sec", None, None)),
        check_vma=False,
    )
```
